32 devices in a mesh: rows: 8 (over z, x), feat: 4 (over y, core).
Axes of the slice: x: 2, y: 2, z: 4, core: 2. Of those that a mesh axis runs over, the one named last changes fastest.
Arguments:
- pixels: bfloat16 [12288, 1024], P(('rows', 'feat')), may hold values from -6 to 6
- qkv_weight: bfloat16 [3, 1024, 1024], P(None, None, 'feat'), may hold values from -0.1875 to 0.1875
- out_weight: bfloat16 [1024, 1024], P('feat'), may hold values from -1.5 to 1.5
- up_weight: bfloat16 [1024, 4096], P(None, 'feat'), as said below
- down_weight: bfloat16 [4096, 1024], P('feat'), may hold values from -0.09375 to 0.09375
- norm1_gain: float32 [1024], replicated, may hold values from 0.5 to 1.5
- norm1_bias: float32 [1024], replicated, may hold values from -3 to 3
- norm2_gain: float32 [1024], replicated, may hold values from 0.5 to 1.5
- norm2_bias: float32 [1024], replicated, may hold values from -3 to 3
- crop_lengths: int32 [32], replicated, may hold values from 0 to 3072, as said below
- crop_offsets: int32 [32], replicated, may hold values from 0 to 12288, as said below
- pixel_mask: int32 [12288], P('rows'), may hold values 0 or 1
- out_grad: bfloat16 [12288, 1024], P(('rows', 'feat')), may hold values from -6 to 6
Outputs:
- output: bfloat16 [12288, 1024], P(('rows', 'feat'))
- pixels_grad: bfloat16 [12288, 1024], P(('rows', 'feat'))
- qkv_weight_grad: float32 [3, 1024, 1024], P(None, None, 'feat')
- out_weight_grad: float32 [1024, 1024], P('feat')
- up_weight_grad: float32 [1024, 4096], P(None, 'feat')
- down_weight_grad: float32 [4096, 1024], P('feat')
- norm1_gain_grad: float32 [1024], replicated
- norm1_bias_grad: float32 [1024], replicated
- norm2_gain_grad: float32 [1024], replicated
- norm2_bias_grad: float32 [1024], replicated
- crop_rms: float32 [3, 32], replicated
The draws below stay inside these ranges and needn't reach their ends.
Inputs may be any that keep to these rules, and one draw needn't show every extreme that they name: Crops lie in order and do not intersection: crop c covers pixels crop_offsets[c] to crop_offsets[c] + crop_lengths[c] - 1. Crop 0 starts at pixel 0 and has exactly 3072 pixels. Crops that would pass the end are cut short; those starting at or past the end have length 0. `crop_offsets`: Non-decreasing; a crop of length 0 at the end has offset 12288. `up_weight`: entries of order 1024 ** -0.5.
All inputs are finite; a program needn't handle non-finite values. No bound on the sum of `pixel_mask` on one device may be relied on, other than what follows from the above.
Results may differ from the reference program's by a relative error of at most 0.02.
Values may be sent and summed in bfloat16 or wider, within the bound.
No kernel may reach another device: no remote copies, remote signals or barrier semaphores. Data moves between devices by JAX's collectives and lax.ppermute only.
A program may use at most 192 MiB of HBM per device.

```python
import jax
import jax.numpy as jnp
from jax import lax

D = 1024
HEADS = 16
HEAD = 64
FF = 4096
BLOCK = 512
CROP_MAX = 3072
TOKENS = 12288
CROPS = 32


def crop_table(key):
    unit = CROP_MAX // 96
    base_key = jax.random.fold_in(key, 7)
    level_key, size_key, gap_key = jax.random.split(base_key, 3)
    levels = jax.random.randint(level_key, (CROPS,), 0, 6, dtype=jnp.int32)
    lowest = unit * jnp.left_shift(jnp.ones((CROPS,), jnp.int32), levels)
    extra = jax.random.randint(size_key, (CROPS,), 0, 1 << 30, dtype=jnp.int32) % (2 * lowest)
    lengths = lowest + extra
    lengths = jnp.where(jnp.arange(CROPS, dtype=jnp.int32) == 0, CROP_MAX, lengths).astype(jnp.int32)
    gaps = jax.random.randint(gap_key, (CROPS,), 0, 1 + unit // 2, dtype=jnp.int32)
    spans = lengths + gaps
    offsets = (jnp.cumsum(spans) - spans).astype(jnp.int32)
    offsets = jnp.minimum(offsets, TOKENS).astype(jnp.int32)
    lengths = jnp.minimum(lengths, TOKENS - offsets).astype(jnp.int32)
    return (lengths, offsets)


def draw_crop_lengths(key, part):
    return crop_table(key)[0]


def draw_crop_offsets(key, part):
    return crop_table(key)[1]


def draw_up_weight(key, part):
    base_key = jax.random.fold_in(key, 11)
    entry_key, column_key = jax.random.split(base_key, 2)
    scale = float(D) ** (-0.5)
    entries = jnp.clip(jax.random.normal(entry_key, (D, FF), jnp.float32), -6.0, 6.0)
    columns = jnp.clip(jax.random.normal(column_key, (FF,), jnp.float32), -6.0, 6.0)
    total = scale * entries + 0.5 * scale * columns[None, :]
    total = jnp.clip(total, -4.0 * scale, 4.0 * scale)
    return total.astype(jnp.bfloat16)


def set_ends(drawn, rng, low, top_value):
    longest = drawn.shape.index(max(drawn.shape))
    spots = []
    for shift in (0, 1):
        where = [jax.random.randint(jax.random.fold_in(rng, axis), (), 0, length) for axis, length in enumerate(drawn.shape)]
        where[longest] = (where[longest] + shift) % drawn.shape[longest]
        spots.append(tuple(where))
    return drawn.at[spots[0]].set(low).at[spots[1]].set(top_value)


def level_of(key, shape, pieces, low, largest):
    level, own = 1.0, jax.random.fold_in(key, 6)
    for dim, shards_of in pieces:
        heights = jnp.exp(jax.random.uniform(jax.random.fold_in(own, dim), (shards_of,), jnp.float32, low / len(pieces), largest / len(pieces)))
        level = level * jnp.repeat(heights, shape[dim] // shards_of).reshape([-1 if axis == dim else 1 for axis in range(len(shape))])
    return level


def normal_values(rng, dims, width, reach, cuts=(), kind=jnp.bfloat16):
    values = width * jax.random.normal(rng, dims, jnp.float32)
    if cuts:
        values = values * level_of(rng, dims, cuts, -0.22, 0.18)
    return jnp.clip(values, -reach, reach).astype(kind)


def setup_inputs(seed: int = 0) -> dict:
    arg_keys = jax.random.split(jax.random.key(seed), 14)
    pixels = normal_values(arg_keys[0], (TOKENS, D), 1.0, 6.0, ((0, 32),))
    qkv_weight = normal_values(arg_keys[1], (3, D, D), D ** -0.5, 0.1875, ((2, 4),))
    out_weight = normal_values(arg_keys[2], (D, D), (D // 64) ** -0.5, 1.5, ((0, 4),))
    up_weight = draw_up_weight(jax.random.fold_in(arg_keys[13], 71), 0)
    down_weight = normal_values(arg_keys[4], (FF, D), FF ** -0.5, 0.09375, ((0, 4),))
    norm1_gain = jnp.clip(1.0 + 0.1 * jax.random.normal(arg_keys[5], (D,), jnp.float32), 0.5, 1.5)
    norm1_bias = normal_values(arg_keys[6], (D,), 0.5, 3.0, (), jnp.float32)
    norm2_gain = jnp.clip(1.0 + 0.1 * jax.random.normal(arg_keys[7], (D,), jnp.float32), 0.5, 1.5)
    norm2_bias = normal_values(arg_keys[8], (D,), 0.5, 3.0, (), jnp.float32)
    crop_lengths = draw_crop_lengths(jax.random.fold_in(arg_keys[13], 71), 0)
    crop_offsets = draw_crop_offsets(jax.random.fold_in(arg_keys[13], 71), 0)
    pixel_mask = set_ends((jax.random.randint(arg_keys[11], (TOKENS,), 0, 16) < 15).astype(jnp.int32), jax.random.fold_in(arg_keys[11], 1), 0, 1)
    out_grad = normal_values(arg_keys[12], (TOKENS, D), 1.0, 6.0, ((0, 32),))
    return {"pixels": pixels, "qkv_weight": qkv_weight, "out_weight": out_weight, "up_weight": up_weight, "down_weight": down_weight, "norm1_gain": norm1_gain, "norm1_bias": norm1_bias, "norm2_gain": norm2_gain, "norm2_bias": norm2_bias, "crop_lengths": crop_lengths, "crop_offsets": crop_offsets, "pixel_mask": pixel_mask, "out_grad": out_grad}


@jax.custom_vjp
def low(v):
    return lax.optimization_barrier(v.astype(jnp.bfloat16)).astype(jnp.float32)

@jax.custom_vjp
def low_back(v):
    return v

def low_keep(v):
    return (low(v), None)

def low_pass(kept, grad):
    return (grad,)

def back_keep(v):
    return (v, None)

def back_low(kept, grad):
    return (low(grad),)
low.defvjp(low_keep, low_pass)
low_back.defvjp(back_keep, back_low)
precise = lax.Precision.HIGHEST

def layer_norm(values, norm_gain, norm_bias):
    centre = lax.optimization_barrier(jnp.mean(values, axis=-1, keepdims=True))
    shifted = values - centre
    spread = lax.optimization_barrier(jnp.mean(shifted * shifted, axis=-1, keepdims=True))
    return shifted * lax.rsqrt(spread + 1e-05) * norm_gain + norm_bias

def feature(values):
    return jax.nn.elu(values) + 1.0

def crop_layout(crop_lengths, crop_offsets, pixel_mask):
    places = jnp.arange(TOKENS, dtype=jnp.int32)
    started = crop_offsets[None, :] <= places[:, None]
    before_end = places[:, None] < (crop_offsets + crop_lengths)[None, :]
    segment = lax.optimization_barrier(jnp.sum(started.astype(jnp.int32), axis=1)).astype(jnp.int32) - 1
    inside = lax.optimization_barrier(jnp.sum((started & before_end).astype(jnp.int32), axis=1)).astype(jnp.int32)
    pixel_valid = (pixel_mask * inside).astype(jnp.float32)
    return (segment, pixel_valid)

def linear_attention(queries, key_rows, value_rows, segment):
    block_count = TOKENS // BLOCK
    block_shape = (block_count, BLOCK, HEADS, HEAD)
    causal = jnp.arange(BLOCK)[:, None] >= jnp.arange(BLOCK)[None, :]

    def advance(running, inputs):
        carry_state, carry_sum, last_crop = running
        block_q, block_k, block_v, block_seg = inputs
        same_crop = causal & (block_seg[:, None] == block_seg[None, :])
        scores = jnp.einsum('ihd,jhd->hij', block_q, block_k, precision=precise)
        scores = low(low_back(scores * same_crop.astype(jnp.float32)[None]))
        carried = (block_seg == last_crop).astype(jnp.float32)
        numerator = jnp.einsum('hij,jhe->ihe', scores, block_v, precision=precise)
        numerator = numerator + carried[:, None, None] * jnp.einsum('ihd,hde->ihe', block_q, carry_state, precision=precise)
        denominator = lax.optimization_barrier(jnp.sum(scores, axis=2)).T + carried[:, None] * jnp.einsum('ihd,hd->ih', block_q, carry_sum, precision=precise)
        tail_crop = block_seg[-1]
        tail_rows = (block_seg == tail_crop).astype(jnp.float32)
        continues = (tail_crop == last_crop).astype(jnp.float32)
        carry_state = continues * carry_state + jnp.einsum('jhd,jhe->hde', block_k * tail_rows[:, None, None], block_v, precision=precise)
        carry_sum = continues * carry_sum + jnp.einsum('jhd,j->hd', block_k, tail_rows, precision=precise)
        return ((carry_state, carry_sum, tail_crop), (numerator, denominator))
    opening = (jnp.zeros((HEADS, HEAD, HEAD), jnp.float32), jnp.zeros((HEADS, HEAD), jnp.float32), jnp.array(-1, jnp.int32))
    inputs = (queries.reshape(block_shape), key_rows.reshape(block_shape), value_rows.reshape(block_shape), segment.reshape(block_count, BLOCK))
    _, (numerator, denominator) = lax.scan(jax.checkpoint(advance), opening, inputs)
    return (numerator.reshape(TOKENS, HEADS, HEAD), denominator.reshape(TOKENS, HEADS))

def forward(pixels, qkv_weight, out_weight, up_weight, down_weight, gain_one, bias_one, gain_two, bias_two, segment, pixel_valid):
    normed = low(layer_norm(pixels, gain_one, bias_one))
    mixed = low_back(jnp.einsum('td,cde->cte', normed, qkv_weight, precision=precise))
    queries = low(feature(mixed[0])).reshape(TOKENS, HEADS, HEAD)
    key_rows = (pixel_valid[:, None] * low(feature(mixed[1]))).reshape(TOKENS, HEADS, HEAD)
    value_rows = low(mixed[2]).reshape(TOKENS, HEADS, HEAD)
    numerator, denominator = linear_attention(queries, key_rows, value_rows, segment)
    numerator = low_back(numerator)
    spread = denominator + 1e-06 + 1.0 - pixel_valid[:, None]
    heads_out = low((pixel_valid[:, None, None] * numerator / spread[:, :, None]).reshape(TOKENS, D))
    attended = low_back(jnp.dot(heads_out, out_weight, precision=precise))
    middle = pixels + attended
    normed_two = low(layer_norm(middle, gain_two, bias_two))
    hidden = low_back(jnp.dot(normed_two, up_weight, precision=precise))
    activated = low(jax.nn.gelu(hidden, approximate=True))
    branch = low_back(jnp.dot(activated, down_weight, precision=precise))
    return (middle + branch, (attended, branch))

def reference(pixels, qkv_weight, out_weight, up_weight, down_weight, norm1_gain, norm1_bias, norm2_gain, norm2_bias, crop_lengths, crop_offsets, pixel_mask, out_grad):
    segment, pixel_valid = crop_layout(crop_lengths, crop_offsets, pixel_mask)

    def wrapped(pix, w_qkv, w_out, w_up, w_down, gain_one, bias_one, gain_two, bias_two):
        return forward(pix, w_qkv, w_out, w_up, w_down, gain_one, bias_one, gain_two, bias_two, segment, pixel_valid)
    floats = (pixels.astype(jnp.float32), qkv_weight.astype(jnp.float32), out_weight.astype(jnp.float32), up_weight.astype(jnp.float32), down_weight.astype(jnp.float32), norm1_gain, norm1_bias, norm2_gain, norm2_bias)
    result, pullback, (attended, branch) = jax.vjp(wrapped, *floats, has_aux=True)
    grads = pullback(out_grad.astype(jnp.float32))
    crop_onehot = (segment[:, None] == jnp.arange(CROPS, dtype=jnp.int32)[None, :]).astype(jnp.float32)
    squares = jnp.stack([lax.optimization_barrier(jnp.sum(result * result, axis=1)), lax.optimization_barrier(jnp.sum(attended * attended, axis=1)), lax.optimization_barrier(jnp.sum(branch * branch, axis=1))]) * pixel_valid[None, :]
    crop_sums = jnp.dot(squares, crop_onehot, precision=precise)
    crop_counts = jnp.dot(pixel_valid, crop_onehot, precision=precise)
    crop_rms = jnp.sqrt(crop_sums / (D * jnp.maximum(crop_counts, 1.0))[None, :])
    return (result.astype(jnp.bfloat16), grads[0].astype(jnp.bfloat16), grads[1], grads[2], grads[3], grads[4], grads[5], grads[6], grads[7], grads[8], crop_rms)
```

```python
import functools

import jax
import jax.numpy as jnp
from jax import lax
from jax.experimental import pallas as pl
from jax.experimental.pallas import tpu as pltpu
from jax.sharding import PartitionSpec as P

D = 1024
HEAD = 64
CHUNK = 256
CROP_MAX = 3072
PACK = HEAD + 16

BF = jnp.bfloat16
F32 = jnp.float32
precise = lax.Precision.HIGHEST


def nn(a, b):
    return lax.dot_general(a, b, (((1,), (0,)), ((), ())), preferred_element_type=F32)


def nt(a, b):
    return lax.dot_general(a, b, (((1,), (1,)), ((), ())), preferred_element_type=F32)


def tn(a, b):
    return lax.dot_general(a, b, (((0,), (0,)), ((), ())), preferred_element_type=F32)


def same_head(width):
    row = lax.broadcasted_iota(jnp.int32, (width, width), 0) // HEAD
    col = lax.broadcasted_iota(jnp.int32, (width, width), 1) // HEAD
    return row == col


def lane_head(rows, width):
    return lax.broadcasted_iota(jnp.int32, (rows, width), 1) // HEAD


def causal(rows):
    row = lax.broadcasted_iota(jnp.int32, (rows, rows), 0)
    col = lax.broadcasted_iota(jnp.int32, (rows, rows), 1)
    return row >= col


def fold_heads(full, width):
    out = full[0:HEAD]
    for h in range(1, width // HEAD):
        out = out + full[h * HEAD : (h + 1) * HEAD]
    return out


def spread_heads(part, width, block):
    tall = jnp.concatenate([part] * (width // HEAD), axis=0)
    return jnp.where(block, tall, jnp.zeros_like(tall))


def pick(mask, value):
    return jnp.where(mask, value, jnp.zeros_like(value))


def forward_body(last_ref, q_ref, k_ref, v_ref, segc_ref, segr_ref, num_ref, den_ref, st_ref, ks_ref):
    rows, width = q_ref.shape
    size = CHUNK
    block = same_head(width)
    ones_block = block.astype(BF)
    lanes = lane_head(size, width)
    lower = causal(size)
    st_ref[...] = jnp.zeros_like(st_ref)
    ks_ref[...] = jnp.zeros_like(ks_ref)

    def step(c, carry):
        at = pl.ds(pl.multiple_of(c * size, size), size)
        q, k, v = q_ref[at, :], k_ref[at, :], v_ref[at, :]
        seg = segc_ref[at, :]
        keep = lower & (seg == segr_ref[c])
        before, after = last_ref[c], last_ref[c + 1]
        carried = (seg == before).astype(F32)
        num = carried * nn(q, st_ref[...].astype(BF))
        den = carried * nn((q.astype(F32) * ks_ref[0:1, :]).astype(BF), ones_block)
        for h in range(width // HEAD):
            mine = lanes == h
            score = pick(keep, nt(pick(mine, q), k)).astype(BF)
            num = num + nn(score, pick(mine, v))
            den = den + nn(score, mine.astype(BF))
        num_ref[at, :] = num
        den_ref[at, :] = den
        kept = pick(seg == after, k)
        cont = (before == after).astype(F32)
        st_ref[...] = cont * st_ref[...] + pick(block, tn(kept, v))
        ks_ref[...] = cont * ks_ref[...] + jnp.sum(kept.astype(F32), axis=0, keepdims=True)
        return carry

    lax.fori_loop(0, rows // size, step, 0)


def full_spec():
    return pl.BlockSpec(memory_space=pltpu.VMEM)


def smem_spec():
    return pl.BlockSpec(memory_space=pltpu.SMEM)


def attend(last, q, k, v, segc, segr):
    rows, width = q.shape
    return pl.pallas_call(
        forward_body,
        out_shape=(jax.ShapeDtypeStruct((rows, width), F32),) * 2,
        in_specs=[smem_spec()] + [full_spec()] * 5,
        out_specs=(full_spec(),) * 2,
        scratch_shapes=[pltpu.VMEM((width, width), F32), pltpu.VMEM((8, width), F32)],
        name="attend",
    )(last, q, k, v, segc, segr)


def tail_body(last_ref, k_ref, v_ref, segc_ref, out_ref):
    rows, width = k_ref.shape
    tail = last_ref[rows // CHUNK]
    kept = pick(segc_ref[...] == tail, k_ref[...])
    state = fold_heads(pick(same_head(width), tn(kept, v_ref[...])), width)
    sums = jnp.sum(kept.astype(F32), axis=0, keepdims=True)
    out_ref[0:HEAD, :] = state.astype(BF)
    out_ref[HEAD:PACK, :] = jnp.broadcast_to(sums, (PACK - HEAD, width)).astype(BF)


def tail_pack(last, k, v, segc):
    return pl.pallas_call(
        tail_body,
        out_shape=jax.ShapeDtypeStruct((PACK, k.shape[1]), BF),
        in_specs=[smem_spec()] + [full_spec()] * 3,
        out_specs=full_spec(),
        name="tail_pack",
    )(last, k, v, segc)


def project_body(
    first_ref, num_ref, den_ref, q_ref, pack_ref, segc_ref, valid_ref, w_ref,
    heads_ref, wide_ref, rinv_ref, out_ref
):
    rows, width = q_ref.shape
    block = same_head(width)
    state = spread_heads(pack_ref[0:HEAD, :], width, block).astype(BF)
    sums = pack_ref[HEAD : HEAD + 1, :]
    q = q_ref[...]
    opening = (segc_ref[...] == first_ref[0]).astype(F32)
    valid = valid_ref[...]
    num = num_ref[...] + opening * nn(q, state)
    den = den_ref[...] + opening * nn((q.astype(F32) * sums).astype(BF), block.astype(BF))
    rinv = valid / (den + 1e-06 + 1.0 - valid)
    wide = num * rinv
    heads = wide.astype(BF)
    heads_ref[...] = heads
    wide_ref[...] = wide
    rinv_ref[...] = rinv
    out_ref[...] = nn(heads, w_ref[...]).astype(BF)


def project(last, num, den, q, pack, segc, valid, w):
    rows, width = q.shape
    tile = 512
    by_row = lambda cols: pl.BlockSpec((tile, cols), lambda i: (i, 0))
    whole = lambda a: pl.BlockSpec(a.shape, lambda i: (0, 0))
    return pl.pallas_call(
        project_body,
        grid=(rows // tile,),
        out_shape=(
            jax.ShapeDtypeStruct((rows, width), BF),
            jax.ShapeDtypeStruct((rows, width), F32),
            jax.ShapeDtypeStruct((rows, width), F32),
            jax.ShapeDtypeStruct((rows, D), BF),
        ),
        in_specs=[
            smem_spec(), by_row(width), by_row(width), by_row(width), whole(pack),
            by_row(1), by_row(1), whole(w),
        ],
        out_specs=(by_row(width), by_row(width), by_row(width), by_row(D)),
        name="project",
    )(last, num, den, q, pack, segc, valid, w)


def heads_back_body(
    first_ref, grad_ref, w_ref, wide_ref, rinv_ref, q_ref, segc_ref,
    ng_ref, dg_ref, pack_ref, st_ref, ks_ref
):
    width = q_ref.shape[1]
    block = same_head(width)
    ones_block = block.astype(BF)
    hg = nt(grad_ref[...], w_ref[...])
    rinv = rinv_ref[...]
    ng = (hg * rinv).astype(BF)
    prod = hg * wide_ref[...]
    high = prod.astype(BF)
    low = (prod - high.astype(F32)).astype(BF)
    dg = -(nn(high, ones_block) + nn(low, ones_block)) * rinv
    ng_ref[...] = ng
    dg_ref[...] = dg
    opened = pick(segc_ref[...] == first_ref[0], q_ref[...])

    @pl.when(pl.program_id(0) == 0)
    def _():
        st_ref[...] = jnp.zeros_like(st_ref)
        ks_ref[...] = jnp.zeros_like(ks_ref)

    st_ref[...] += tn(opened, ng)
    ks_ref[...] += jnp.sum(opened.astype(F32) * dg, axis=0, keepdims=True)

    @pl.when(pl.program_id(0) == pl.num_programs(0) - 1)
    def _():
        pack_ref[0:HEAD, :] = fold_heads(pick(block, st_ref[...]), width).astype(BF)
        pack_ref[HEAD:PACK, :] = jnp.broadcast_to(ks_ref[0:1, :], (PACK - HEAD, width)).astype(BF)


def heads_back(last, grad, w, wide, rinv, q, segc):
    rows, width = q.shape
    tile = 512
    by_row = lambda cols: pl.BlockSpec((tile, cols), lambda i: (i, 0))
    whole = lambda shape: pl.BlockSpec(shape, lambda i: (0, 0))
    return pl.pallas_call(
        heads_back_body,
        grid=(rows // tile,),
        out_shape=(
            jax.ShapeDtypeStruct((rows, width), BF),
            jax.ShapeDtypeStruct((rows, width), F32),
            jax.ShapeDtypeStruct((PACK, width), BF),
        ),
        in_specs=[
            smem_spec(), by_row(D), whole(w.shape), by_row(width), by_row(width), by_row(width),
            by_row(1),
        ],
        out_specs=(by_row(width), by_row(width), whole((PACK, width))),
        scratch_shapes=[pltpu.VMEM((width, width), F32), pltpu.VMEM((8, width), F32)],
        name="heads_back",
    )(last, grad, w, wide, rinv, q, segc)


def backward_body(
    last_ref, q_ref, k_ref, v_ref, ng_ref, dg_ref, segc_ref, segr_ref, pack_ref,
    dq_ref, dk_ref, dv_ref, all_ref, sums_ref, st_ref, ks_ref
):
    rows, width = q_ref.shape
    size = CHUNK
    count = rows // size
    block = same_head(width)
    lanes = lane_head(size, width)
    lower = causal(size)
    st_ref[...] = spread_heads(pack_ref[0:HEAD, :], width, block)
    ks_ref[...] = jnp.broadcast_to(pack_ref[HEAD : HEAD + 1, :], ks_ref.shape)

    def collect(c, carry):
        at = pl.ds(pl.multiple_of(c * size, size), size)
        all_ref[c] = st_ref[...].astype(BF)
        sums_ref[c] = ks_ref[...]
        before, after = last_ref[c], last_ref[c + 1]
        kept = pick(segc_ref[at, :] == after, k_ref[at, :])
        cont = (before == after).astype(F32)
        st_ref[...] = cont * st_ref[...] + pick(block, tn(kept, v_ref[at, :]))
        ks_ref[...] = cont * ks_ref[...] + jnp.sum(kept.astype(F32), axis=0, keepdims=True)
        return carry

    lax.fori_loop(0, count, collect, 0)
    st_ref[...] = jnp.zeros_like(st_ref)
    ks_ref[...] = jnp.zeros_like(ks_ref)

    def step(i, carry):
        c = count - 1 - i
        at = pl.ds(pl.multiple_of(c * size, size), size)
        q, k, v, ng, dg = q_ref[at, :], k_ref[at, :], v_ref[at, :], ng_ref[at, :], dg_ref[at, :]
        seg = segc_ref[at, :]
        keep = lower & (seg == segr_ref[c])
        before, after = last_ref[c], last_ref[c + 1]
        opened = seg == before
        carried = opened.astype(F32)
        tail = (seg == after).astype(F32)
        grad_state = st_ref[...].astype(BF)
        dq = carried * (nt(ng, all_ref[c]) + dg * sums_ref[c][0:1, :])
        dk = tail * (nt(v, grad_state) + ks_ref[0:1, :])
        dv = tail * nn(k, grad_state)
        for h in range(width // HEAD):
            mine = lanes == h
            qh, kh, nh = pick(mine, q), pick(mine, k), pick(mine, ng)
            score = pick(keep, nt(qh, k)).astype(BF)
            lead = dg[:, h * HEAD : h * HEAD + 1]
            back = pick(keep, nt(nh, v) + lead).astype(BF)
            dq = dq + nn(back, kh)
            dk = dk + tn(back, qh)
            dv = dv + tn(score, nh)
        dq_ref[at, :] = (dq * jnp.minimum(q.astype(F32), 1.0)).astype(BF)
        dk_ref[at, :] = dk
        dv_ref[at, :] = dv
        cont = (before == after).astype(F32)
        st_ref[...] = cont * st_ref[...] + pick(block, tn(pick(opened, q), ng))
        ks_ref[...] = cont * ks_ref[...] + jnp.sum(carried * q.astype(F32) * dg, axis=0, keepdims=True)
        return carry

    lax.fori_loop(0, count, step, 0)


def attend_back(last, q, k, v, ng, dg, segc, segr, pack):
    rows, width = q.shape
    count = rows // CHUNK
    return pl.pallas_call(
        backward_body,
        out_shape=(
            jax.ShapeDtypeStruct((rows, width), BF),
            jax.ShapeDtypeStruct((rows, width), F32),
            jax.ShapeDtypeStruct((rows, width), F32),
        ),
        in_specs=[smem_spec()] + [full_spec()] * 8,
        out_specs=(full_spec(),) * 3,
        scratch_shapes=[
            pltpu.VMEM((count, width, width), BF),
            pltpu.VMEM((count, 8, width), F32),
            pltpu.VMEM((width, width), F32),
            pltpu.VMEM((8, width), F32),
        ],
        name="attend_back",
    )(last, q, k, v, ng, dg, segc, segr, pack)


def mix_body(tail_ref, dq_ref, dk_ref, dv_ref, k_ref, v_ref, segc_ref, valid_ref, pack_ref, out_ref):
    rows, width = k_ref.shape
    block = same_head(width)
    state = spread_heads(pack_ref[0:HEAD, :], width, block).astype(BF)
    sums = pack_ref[HEAD : HEAD + 1, :]
    tail = (segc_ref[...] == tail_ref[0]).astype(F32)
    k = k_ref[...]
    dk = dk_ref[...] + tail * (nt(v_ref[...], state) + sums)
    dv = dv_ref[...] + tail * nn(k, state)
    out_ref[:, 0:width] = dq_ref[...]
    out_ref[:, width : 2 * width] = (valid_ref[...] * dk * jnp.minimum(k.astype(F32), 1.0)).astype(BF)
    out_ref[:, 2 * width : 3 * width] = dv.astype(BF)


def mix(tail, dq, dk, dv, k, v, segc, valid, pack):
    rows, width = k.shape
    tile = 512
    by_row = lambda cols: pl.BlockSpec((tile, cols), lambda i: (i, 0))
    return pl.pallas_call(
        mix_body,
        grid=(rows // tile,),
        out_shape=jax.ShapeDtypeStruct((rows, 3 * width), BF),
        in_specs=[smem_spec()] + [by_row(width)] * 5 + [by_row(1)] * 2
        + [pl.BlockSpec(pack.shape, lambda i: (0, 0))],
        out_specs=by_row(3 * width),
        name="mix",
    )(tail, dq, dk, dv, k, v, segc, valid, pack)


def layer_norm(values, norm_gain, norm_bias):
    centre = jnp.mean(values, axis=-1, keepdims=True)
    shifted = values - centre
    spread = jnp.mean(shifted * shifted, axis=-1, keepdims=True)
    return shifted * lax.rsqrt(spread + 1e-05) * norm_gain + norm_bias


def feature(values):
    return jnp.where(values > 0, values + 1.0, jnp.exp(jnp.minimum(values, 0.0)))


def gelu_tanh(values):
    return jax.nn.gelu(values, approximate=True)


def shifted(pack, hop, groups, reverse):
    if reverse:
        pairs = [(i, i - hop) for i in range(hop, groups)]
    else:
        pairs = [(i, i + hop) for i in range(groups - hop)]
    return lax.ppermute(pack, "rows", pairs)


def gather_carry(pack, crops_at, here, groups, reach, reverse):
    total = jnp.zeros(pack.shape, F32)
    mine = crops_at[here + 1] if reverse else crops_at[here]
    for hop in range(1, reach + 1):
        got = shifted(pack, hop, groups, reverse).astype(F32)
        other = here + hop if reverse else here - hop
        inside = (other < groups) if reverse else (other >= 0)
        at = jnp.clip(other, 0, groups - 1)
        theirs = crops_at[at] if reverse else crops_at[at + 1]
        total = total + jnp.where(inside & (theirs == mine), got, 0.0)
    return total


def on_device(
    pixels,
    qkv_weight,
    out_weight,
    up_weight,
    down_weight,
    norm1_gain,
    norm1_bias,
    norm2_gain,
    norm2_bias,
    crop_lengths,
    crop_offsets,
    pixel_mask,
    out_grad,
):
    local_rows = pixels.shape[0]
    group_rows = pixel_mask.shape[0]
    width_local = qkv_weight.shape[2]
    crop_count = crop_offsets.shape[0]
    groups = lax.axis_size("rows")
    here = lax.axis_index("rows")
    reach = min(groups - 1, -(-(CROP_MAX - 1) // group_rows))
    group_start = here * group_rows
    local_start = lax.axis_index("feat") * local_rows
    places = group_start + jnp.arange(group_rows, dtype=jnp.int32)
    started = crop_offsets[None, :] <= places[:, None]
    crop_ends = crop_offsets + crop_lengths
    segment = jnp.sum(started.astype(jnp.int32), axis=1) - 1
    inside = jnp.sum((started & (places[:, None] < crop_ends[None, :])).astype(jnp.int32), axis=1)
    pixel_valid = (pixel_mask * inside).astype(F32)
    edges = jnp.arange(groups + 1, dtype=jnp.int32) * group_rows - 1
    crops_at = jnp.sum((crop_offsets[None, :] <= edges[:, None]).astype(jnp.int32), axis=1) - 1
    chunk_edges = group_start - 1 + jnp.arange(group_rows // CHUNK + 1, dtype=jnp.int32) * CHUNK
    last = jnp.sum((crop_offsets[None, :] <= chunk_edges[:, None]).astype(jnp.int32), axis=1) - 1
    segc = segment[:, None]
    segr = segment.reshape(group_rows // CHUNK, 1, CHUNK)
    validc = pixel_valid[:, None]
    local_valid = lax.dynamic_slice_in_dim(pixel_valid, local_start, local_rows)
    local_segment = lax.dynamic_slice_in_dim(segment, local_start, local_rows)

    inputs = pixels.astype(F32)
    normed, norm1_back = jax.vjp(layer_norm, inputs, norm1_gain, norm1_bias)
    normed_all = lax.all_gather(normed.astype(BF), "feat", axis=0, tiled=True)
    grad_all = lax.all_gather(out_grad, "feat", axis=0, tiled=True)
    k = (feature(nn(normed_all, qkv_weight[1])) * validc).astype(BF)
    v = nn(normed_all, qkv_weight[2]).astype(BF)
    pack = tail_pack(last, k, v, segc)
    carry = gather_carry(pack, crops_at, here, groups, reach, False)
    q = feature(nn(normed_all, qkv_weight[0])).astype(BF)
    num, den = attend(last, q, k, v, segc, segr)
    heads_out, heads_wide, rinv, part = project(last, num, den, q, carry, segc, validc, out_weight)
    attended = lax.psum_scatter(part, "feat", scatter_dimension=0, tiled=True).astype(F32)
    middle = inputs + attended
    normed_two, norm2_back = jax.vjp(layer_norm, middle, norm2_gain, norm2_bias)
    normed_two_all = lax.all_gather(normed_two.astype(BF), "feat", axis=0, tiled=True)
    hidden = nn(normed_two_all, up_weight)
    activated, gelu_back = jax.vjp(gelu_tanh, hidden)
    activated_low = activated.astype(BF)
    active_grad = nt(grad_all, down_weight)
    hidden_grad = gelu_back(active_grad)[0].astype(BF)
    normed_two_grad = lax.psum_scatter(
        nt(hidden_grad, up_weight).astype(BF), "feat", scatter_dimension=0, tiled=True
    ).astype(F32)
    branch = lax.psum_scatter(
        nn(activated_low, down_weight).astype(BF), "feat", scatter_dimension=0, tiled=True
    ).astype(F32)
    up_grad = tn(normed_two_all, hidden_grad)
    down_grad = tn(activated_low, grad_all)
    result = middle + branch
    middle_part, gain2_grad, bias2_grad = norm2_back(normed_two_grad)
    middle_grad = out_grad.astype(F32) + middle_part
    middle_all = lax.all_gather(middle_grad.astype(BF), "feat", axis=0, tiled=True)
    ng, dg, grad_pack = heads_back(last, middle_all, out_weight, heads_wide, rinv, q, segc)
    grad_carry = gather_carry(grad_pack, crops_at, here, groups, reach, True)
    out_weight_grad = tn(heads_out, middle_all)
    dq, dk, dv = attend_back(last, q, k, v, ng, dg, segc, segr, carry)
    mixed_grad = mix(last[-1:], dq, dk, dv, k, v, segc, validc, grad_carry)
    qkv_flat = jnp.concatenate([qkv_weight[0], qkv_weight[1], qkv_weight[2]], axis=1)
    normed_grad = lax.psum_scatter(
        nt(mixed_grad, qkv_flat).astype(BF), "feat", scatter_dimension=0, tiled=True
    ).astype(F32)
    qkv_grad = jnp.stack(
        [
            tn(normed_all, mixed_grad[:, c * width_local : (c + 1) * width_local])
            for c in range(3)
        ]
    )
    input_part, gain1_grad, bias1_grad = norm1_back(normed_grad)
    pixels_grad = (middle_grad + input_part).astype(BF)
    crop_onehot = (
        local_segment[:, None] == jnp.arange(crop_count, dtype=jnp.int32)[None, :]
    ).astype(F32)
    squares = (
        jnp.stack(
            [
                jnp.sum(result * result, axis=1),
                jnp.sum(attended * attended, axis=1),
                jnp.sum(branch * branch, axis=1),
            ]
        )
        * local_valid[None, :]
    )
    crop_sums = jnp.dot(squares, crop_onehot, precision=precise)
    crop_counts = jnp.dot(local_valid, crop_onehot, precision=precise)
    crop_sums, crop_counts, gain1_grad, bias1_grad, gain2_grad, bias2_grad = lax.psum(
        (crop_sums, crop_counts, gain1_grad, bias1_grad, gain2_grad, bias2_grad), ("rows", "feat")
    )
    qkv_grad, out_weight_grad, up_grad, down_grad = (
        lax.psum(qkv_grad.astype(BF), "rows").astype(F32),
        lax.psum(out_weight_grad.astype(BF), "rows").astype(F32),
        lax.psum(up_grad.astype(BF), "rows").astype(F32),
        lax.psum(down_grad.astype(BF), "rows").astype(F32),
    )
    crop_rms = jnp.sqrt(crop_sums / (D * jnp.maximum(crop_counts, 1.0))[None, :])
    return (
        result.astype(BF),
        pixels_grad,
        qkv_grad,
        out_weight_grad,
        up_grad,
        down_grad,
        gain1_grad,
        bias1_grad,
        gain2_grad,
        bias2_grad,
        crop_rms,
    )


def solution(mesh):
    split = P(("rows", "feat"), None)
    qkv, rows_feat, cols_feat = P(None, None, "feat"), P("feat", None), P(None, "feat")
    in_specs = (
        (split, qkv, rows_feat, cols_feat, rows_feat) + (P(),) * 6 + (P("rows"), split)
    )
    out_specs = (split, split, qkv, rows_feat, cols_feat, rows_feat) + (P(),) * 5
    return jax.shard_map(
        on_device, mesh=mesh, in_specs=in_specs, out_specs=out_specs, check_vma=False
    )
```

```python
import functools

import jax
import jax.numpy as jnp
from jax import lax
from jax.experimental import pallas as pl
from jax.experimental.pallas import tpu as pltpu
from jax.sharding import PartitionSpec as P

D = 1024
HEAD = 64
CHUNK = 128
CROP_MAX = 3072
UNROLL = 3
PACK = HEAD + 16

BF = jnp.bfloat16
F32 = jnp.float32
precise = lax.Precision.HIGHEST


def nn(a, b):
    return lax.dot_general(a, b, (((1,), (0,)), ((), ())), preferred_element_type=F32)


def nt(a, b):
    return lax.dot_general(a, b, (((1,), (1,)), ((), ())), preferred_element_type=F32)


def tn(a, b):
    return lax.dot_general(a, b, (((0,), (0,)), ((), ())), preferred_element_type=F32)


def same_head(width):
    row = lax.broadcasted_iota(jnp.int32, (width, width), 0) // HEAD
    col = lax.broadcasted_iota(jnp.int32, (width, width), 1) // HEAD
    return row == col


def lane_head(rows, width):
    return lax.broadcasted_iota(jnp.int32, (rows, width), 1) // HEAD


def causal(rows):
    row = lax.broadcasted_iota(jnp.int32, (rows, rows), 0)
    col = lax.broadcasted_iota(jnp.int32, (rows, rows), 1)
    return row >= col


def fold_heads(full, width):
    out = full[0:HEAD]
    for h in range(1, width // HEAD):
        out = out + full[h * HEAD : (h + 1) * HEAD]
    return out


def spread_heads(part, width, block):
    tall = jnp.concatenate([part] * (width // HEAD), axis=0)
    return jnp.where(block, tall, jnp.zeros_like(tall))


def pick(mask, value):
    return jnp.where(mask, value, jnp.zeros_like(value))


def vmem():
    return pl.BlockSpec(memory_space=pltpu.VMEM)


def smem():
    return pl.BlockSpec(memory_space=pltpu.SMEM)


def shape(rows, cols, kind):
    return jax.ShapeDtypeStruct((rows, cols), kind)


def qkv_body(x_ref, w_ref, valid_ref, q_ref, k_ref, v_ref):
    x = x_ref[...]
    q = nn(x, w_ref[0])
    k = nn(x, w_ref[1])
    q_ref[...] = feature(q).astype(BF)
    k_ref[...] = (feature(k) * valid_ref[...]).astype(BF)
    v_ref[...] = nn(x, w_ref[2]).astype(BF)


def project_qkv(x, w, valid):
    rows, width = x.shape[0], w.shape[2]
    return pl.pallas_call(
        qkv_body,
        out_shape=(shape(rows, width, BF),) * 3,
        in_specs=[vmem()] * 3,
        out_specs=(vmem(),) * 3,
        name="project_qkv",
    )(x, w, valid)


def forward_body(
    last_ref, spot_ref, q_ref, k_ref, v_ref, segc_ref, segr_ref, num_ref, den_ref, st_ref, ks_ref
):
    rows, width = q_ref.shape
    size = CHUNK
    block = same_head(width)
    ones_block = block.astype(BF)
    lanes = lane_head(size, width)
    lower = causal(size)
    st_ref[...] = jnp.zeros_like(st_ref)
    ks_ref[...] = jnp.zeros_like(ks_ref)

    def chunk(c):
        spot = spot_ref[c]
        at = pl.ds(pl.multiple_of(spot * size, size), size)
        q, k, v = q_ref[at, :], k_ref[at, :], v_ref[at, :]
        seg = segc_ref[at, :]
        keep = lower & (seg == segr_ref[spot])
        before, after = last_ref[c], last_ref[c + 1]
        carried = (seg == before).astype(F32)
        num = carried * nn(q, st_ref[...].astype(BF))
        den = carried * nn((q.astype(F32) * ks_ref[0:1, :]).astype(BF), ones_block)
        for h in range(width // HEAD):
            mine = lanes == h
            score = pick(keep, nt(pick(mine, q), k)).astype(BF)
            num = num + nn(score, pick(mine, v))
            den = den + nn(score, mine.astype(BF))
        num_ref[at, :] = num
        den_ref[at, :] = den
        kept = pick(seg == after, k)
        cont = (before == after).astype(F32)
        st_ref[...] = cont * st_ref[...] + pick(block, tn(kept, v))
        ks_ref[...] = cont * ks_ref[...] + jnp.sum(kept.astype(F32), axis=0, keepdims=True)

    def step(i, carry):
        for j in range(UNROLL):
            chunk(i * UNROLL + j)
        return carry

    lax.fori_loop(0, rows // size // UNROLL, step, 0)


def attend(last, spot, q, k, v, segc, segr):
    rows, width = q.shape
    return pl.pallas_call(
        forward_body,
        out_shape=(shape(rows, width, F32),) * 2,
        in_specs=[smem()] * 2 + [vmem()] * 5,
        out_specs=(vmem(),) * 2,
        scratch_shapes=[pltpu.VMEM((width, width), F32), pltpu.VMEM((8, width), F32)],
        name="attend",
    )(last, spot, q, k, v, segc, segr)


def tail_body(last_ref, k_ref, v_ref, segc_ref, out_ref):
    rows, width = k_ref.shape
    tail = last_ref[rows // CHUNK]
    kept = pick(segc_ref[...] == tail, k_ref[...])
    state = fold_heads(pick(same_head(width), tn(kept, v_ref[...])), width)
    sums = jnp.sum(kept.astype(F32), axis=0, keepdims=True)
    out_ref[0:HEAD, :] = state.astype(BF)
    out_ref[HEAD:PACK, :] = jnp.broadcast_to(sums, (PACK - HEAD, width)).astype(BF)


def tail_pack(last, k, v, segc):
    return pl.pallas_call(
        tail_body,
        out_shape=shape(PACK, k.shape[1], BF),
        in_specs=[smem()] + [vmem()] * 3,
        out_specs=vmem(),
        name="tail_pack",
    )(last, k, v, segc)


def project_body(
    first_ref, num_ref, den_ref, q_ref, pack_ref, segc_ref, valid_ref, w_ref,
    heads_ref, wide_ref, rinv_ref, out_ref
):
    rows, width = q_ref.shape
    block = same_head(width)
    state = spread_heads(pack_ref[0:HEAD, :], width, block).astype(BF)
    sums = pack_ref[HEAD : HEAD + 1, :]
    q = q_ref[...]
    opening = (segc_ref[...] == first_ref[0]).astype(F32)
    valid = valid_ref[...]
    num = num_ref[...] + opening * nn(q, state)
    den = den_ref[...] + opening * nn((q.astype(F32) * sums).astype(BF), block.astype(BF))
    rinv = valid / (den + 1e-06 + 1.0 - valid)
    wide = num * rinv
    heads = wide.astype(BF)
    heads_ref[...] = heads
    wide_ref[...] = wide
    rinv_ref[...] = rinv
    out_ref[...] = nn(heads, w_ref[...]).astype(BF)


def slot_spec(rows, cols, slot):
    return pl.BlockSpec((rows, cols), lambda i: (slot, 0))


def whole_spec(array):
    rank = array.ndim
    return pl.BlockSpec(array.shape, lambda i: (0,) * rank)


def project(slot, rows, last, num, den, q, pack, segc, valid, w):
    width = q.shape[1]
    at = lambda cols: slot_spec(rows, cols, slot)
    mine = lambda cols: slot_spec(rows, cols, 0)
    return pl.pallas_call(
        project_body,
        grid=(1,),
        out_shape=(shape(rows, width, BF), shape(rows, width, F32), shape(rows, width, F32), shape(rows, D, BF)),
        in_specs=[smem(), at(width), at(width), at(width), whole_spec(pack), at(1), at(1), whole_spec(w)],
        out_specs=(mine(width), mine(width), mine(width), mine(D)),
        name="project",
    )(last, num, den, q, pack, segc, valid, w)


def heads_back_body(
    first_ref, grad_ref, w_ref, wide_ref, rinv_ref, q_ref, segc_ref, ng_ref, dg_ref, pack_ref
):
    width = q_ref.shape[1]
    block = same_head(width)
    ones_block = block.astype(BF)
    hg = nt(grad_ref[...], w_ref[...])
    rinv = rinv_ref[...]
    ng = (hg * rinv).astype(BF)
    prod = hg * wide_ref[...]
    high = prod.astype(BF)
    low = (prod - high.astype(F32)).astype(BF)
    dg = -(nn(high, ones_block) + nn(low, ones_block)) * rinv
    ng_ref[...] = ng
    dg_ref[...] = dg
    opened = pick(segc_ref[...] == first_ref[0], q_ref[...])
    pack_ref[0:HEAD, :] = fold_heads(pick(block, tn(opened, ng)), width)
    sums = jnp.sum(opened.astype(F32) * dg, axis=0, keepdims=True)
    pack_ref[HEAD:PACK, :] = jnp.broadcast_to(sums, (PACK - HEAD, width))


def heads_back(slot, last, grad, w, wide, rinv, q, segc):
    rows, width = grad.shape[0], q.shape[1]
    at = lambda cols: slot_spec(rows, cols, slot)
    mine = lambda cols: slot_spec(rows, cols, 0)
    return pl.pallas_call(
        heads_back_body,
        grid=(1,),
        out_shape=(shape(rows, width, BF), shape(rows, width, F32), shape(PACK, width, F32)),
        in_specs=[smem(), mine(D), whole_spec(w), mine(width), mine(width), at(width), at(1)],
        out_specs=(mine(width), mine(width), slot_spec(PACK, width, 0)),
        name="heads_back",
    )(last, grad, w, wide, rinv, q, segc)


def backward_body(
    last_ref, spot_ref, q_ref, k_ref, v_ref, ng_ref, dg_ref, segc_ref, segr_ref, pack_ref,
    dq_ref, dk_ref, dv_ref, all_ref, sums_ref, st_ref, ks_ref
):
    rows, width = q_ref.shape
    size = CHUNK
    count = rows // size
    block = same_head(width)
    lanes = lane_head(size, width)
    lower = causal(size)
    st_ref[...] = spread_heads(pack_ref[0:HEAD, :], width, block)
    ks_ref[...] = jnp.broadcast_to(pack_ref[HEAD : HEAD + 1, :], ks_ref.shape)

    def collect(c):
        at = pl.ds(pl.multiple_of(spot_ref[c] * size, size), size)
        all_ref[c] = st_ref[...].astype(BF)
        sums_ref[c] = ks_ref[...]
        before, after = last_ref[c], last_ref[c + 1]
        kept = pick(segc_ref[at, :] == after, k_ref[at, :])
        cont = (before == after).astype(F32)
        st_ref[...] = cont * st_ref[...] + pick(block, tn(kept, v_ref[at, :]))
        ks_ref[...] = cont * ks_ref[...] + jnp.sum(kept.astype(F32), axis=0, keepdims=True)

    def collects(i, carry):
        for j in range(UNROLL):
            collect(i * UNROLL + j)
        return carry

    lax.fori_loop(0, count // UNROLL, collects, 0)
    st_ref[...] = jnp.zeros_like(st_ref)
    ks_ref[...] = jnp.zeros_like(ks_ref)

    def chunk(c):
        spot = spot_ref[c]
        at = pl.ds(pl.multiple_of(spot * size, size), size)
        q, k, v, ng, dg = q_ref[at, :], k_ref[at, :], v_ref[at, :], ng_ref[at, :], dg_ref[at, :]
        seg = segc_ref[at, :]
        keep = lower & (seg == segr_ref[spot])
        before, after = last_ref[c], last_ref[c + 1]
        opened = seg == before
        carried = opened.astype(F32)
        tail = (seg == after).astype(F32)
        grad_state = st_ref[...].astype(BF)
        dq = carried * (nt(ng, all_ref[c]) + dg * sums_ref[c][0:1, :])
        dk = tail * (nt(v, grad_state) + ks_ref[0:1, :])
        dv = tail * nn(k, grad_state)
        for h in range(width // HEAD):
            mine = lanes == h
            qh, kh, nh = pick(mine, q), pick(mine, k), pick(mine, ng)
            score = pick(keep, nt(qh, k)).astype(BF)
            lead = dg[:, h * HEAD : h * HEAD + 1]
            back = pick(keep, nt(nh, v) + lead).astype(BF)
            dq = dq + nn(back, kh)
            dk = dk + tn(back, qh)
            dv = dv + tn(score, nh)
        dq_ref[at, :] = (dq * jnp.minimum(q.astype(F32), 1.0)).astype(BF)
        dk_ref[at, :] = dk
        dv_ref[at, :] = dv
        cont = (before == after).astype(F32)
        st_ref[...] = cont * st_ref[...] + pick(block, tn(pick(opened, q), ng))
        ks_ref[...] = cont * ks_ref[...] + jnp.sum(carried * q.astype(F32) * dg, axis=0, keepdims=True)

    def step(i, carry):
        for j in range(UNROLL):
            chunk(count - 1 - i * UNROLL - j)
        return carry

    lax.fori_loop(0, count // UNROLL, step, 0)


def attend_back(last, spot, q, k, v, ng, dg, segc, segr, pack):
    rows, width = q.shape
    count = rows // CHUNK
    return pl.pallas_call(
        backward_body,
        out_shape=(shape(rows, width, BF), shape(rows, width, F32), shape(rows, width, F32)),
        in_specs=[smem()] * 2 + [vmem()] * 8,
        out_specs=(vmem(),) * 3,
        scratch_shapes=[
            pltpu.VMEM((count, width, width), BF),
            pltpu.VMEM((count, 8, width), F32),
            pltpu.VMEM((width, width), F32),
            pltpu.VMEM((8, width), F32),
        ],
        name="attend_back",
    )(last, spot, q, k, v, ng, dg, segc, segr, pack)


def mix_body(
    tail_ref, dq_ref, dk_ref, dv_ref, k_ref, v_ref, segc_ref, valid_ref, pack_ref, w_ref,
    mixed_ref, out_ref
):
    rows, width = k_ref.shape
    block = same_head(width)
    state = spread_heads(pack_ref[0:HEAD, :], width, block).astype(BF)
    sums = pack_ref[HEAD : HEAD + 1, :]
    tail = (segc_ref[...] == tail_ref[0]).astype(F32)
    k = k_ref[...]
    dk = dk_ref[...] + tail * (nt(v_ref[...], state) + sums)
    dv = dv_ref[...] + tail * nn(k, state)
    dq = dq_ref[...]
    dk = (valid_ref[...] * dk * jnp.minimum(k.astype(F32), 1.0)).astype(BF)
    dv = dv.astype(BF)
    mixed_ref[:, 0:width] = dq
    mixed_ref[:, width : 2 * width] = dk
    mixed_ref[:, 2 * width : 3 * width] = dv
    out_ref[...] = (nt(dq, w_ref[0]) + nt(dk, w_ref[1]) + nt(dv, w_ref[2])).astype(BF)


def mix(slot, rows, tail, dq, dk, dv, k, v, segc, valid, pack, w):
    width = k.shape[1]
    at = lambda cols: slot_spec(rows, cols, slot)
    mine = lambda cols: slot_spec(rows, cols, 0)
    return pl.pallas_call(
        mix_body,
        grid=(1,),
        out_shape=(shape(rows, 3 * width, BF), shape(rows, D, BF)),
        in_specs=[smem()] + [at(width)] * 5 + [at(1)] * 2 + [whole_spec(pack), whole_spec(w)],
        out_specs=(mine(3 * width), mine(D)),
        name="mix",
    )(tail, dq, dk, dv, k, v, segc, valid, pack, w)


def layer_norm(values, norm_gain, norm_bias):
    centre = jnp.mean(values, axis=-1, keepdims=True)
    shifted = values - centre
    spread = jnp.mean(shifted * shifted, axis=-1, keepdims=True)
    return shifted * lax.rsqrt(spread + 1e-05) * norm_gain + norm_bias


def feature(values):
    return jnp.where(values > 0, values + 1.0, jnp.exp(jnp.minimum(values, 0.0)))


def gelu_tanh(values):
    return jax.nn.gelu(values, approximate=True)


def bits_of(count):
    return [1 << b for b in range(count.bit_length() - 1)]


def swap(value, axis, bit):
    return lax.ppermute(value, axis, [(i, i ^ bit) for i in range(lax.axis_size(axis))])


def gather_slots(value):
    slots = {0: value}
    for bit in reversed(bits_of(lax.axis_size("feat"))):
        for s in sorted(slots):
            slots[s | bit] = swap(slots[s], "feat", bit)
    return [slots[s] for s in range(len(slots))]


def scatter_slots(parts):
    parts = dict(enumerate(parts))
    for bit in bits_of(lax.axis_size("feat")):
        for s in sorted(parts, reverse=True):
            if s & bit:
                got = swap(parts.pop(s).astype(BF), "feat", bit)
                parts[s ^ bit] = parts[s ^ bit].astype(F32) + got.astype(F32)
    return parts[0]


def sum_everywhere(value):
    for axis in ("feat", "rows"):
        for bit in bits_of(lax.axis_size(axis)):
            value = value + swap(value, axis, bit)
    return value


def sum_rows(value, order):
    here = lax.axis_index("rows")
    for bit in order:
        half = value.shape[0] // 2
        upper = (here & bit) != 0
        low, high = value[:half], value[half:]
        got = swap(jnp.where(upper, low, high), "rows", bit)
        value = (jnp.where(upper, high, low).astype(F32) + got.astype(F32)).astype(BF)
    for bit in reversed(order):
        upper = (here & bit) != 0
        got = swap(value, "rows", bit)
        value = jnp.concatenate([jnp.where(upper, got, value), jnp.where(upper, value, got)], axis=0)
    return value


def shifted(pack, hop, groups, reverse):
    if reverse:
        pairs = [(i, i - hop) for i in range(hop, groups)]
    else:
        pairs = [(i, i + hop) for i in range(groups - hop)]
    return lax.ppermute(pack, "rows", pairs)


def gather_carry(pack, crops_at, here, groups, reach, reverse):
    total = jnp.zeros(pack.shape, F32)
    mine = crops_at[here + 1] if reverse else crops_at[here]
    for hop in range(1, reach + 1):
        got = shifted(pack, hop, groups, reverse).astype(F32)
        other = here + hop if reverse else here - hop
        inside = (other < groups) if reverse else (other >= 0)
        at = jnp.clip(other, 0, groups - 1)
        theirs = crops_at[at] if reverse else crops_at[at + 1]
        total = total + jnp.where(inside & (theirs == mine), got, 0.0)
    return total


def on_device(
    pixels,
    qkv_weight,
    out_weight,
    up_weight,
    down_weight,
    norm1_gain,
    norm1_bias,
    norm2_gain,
    norm2_bias,
    crop_lengths,
    crop_offsets,
    pixel_mask,
    out_grad,
):
    local_rows = pixels.shape[0]
    group_rows = pixel_mask.shape[0]
    width = qkv_weight.shape[2]
    crop_count = crop_offsets.shape[0]
    groups = lax.axis_size("rows")
    members = lax.axis_size("feat")
    here = lax.axis_index("rows")
    member = lax.axis_index("feat")
    reach = min(groups - 1, -(-(CROP_MAX - 1) // group_rows))
    group_start = here * group_rows
    slot_ids = jnp.arange(members, dtype=jnp.int32) ^ member
    in_group = (slot_ids[:, None] * local_rows + jnp.arange(local_rows, dtype=jnp.int32)[None, :]).reshape(-1)
    places = group_start + in_group
    started = crop_offsets[None, :] <= places[:, None]
    crop_ends = crop_offsets + crop_lengths
    segment = jnp.sum(started.astype(jnp.int32), axis=1) - 1
    inside = jnp.sum((started & (places[:, None] < crop_ends[None, :])).astype(jnp.int32), axis=1)
    mask = jnp.concatenate(
        [
            lax.dynamic_slice_in_dim(pixel_mask, (member ^ s) * local_rows, local_rows)
            for s in range(members)
        ]
    )
    pixel_valid = (mask * inside).astype(F32)
    edges = jnp.arange(groups + 1, dtype=jnp.int32) * group_rows - 1
    crops_at = jnp.sum((crop_offsets[None, :] <= edges[:, None]).astype(jnp.int32), axis=1) - 1
    chunks = group_rows // CHUNK
    per = local_rows // CHUNK
    chunk_edges = group_start - 1 + jnp.arange(chunks + 1, dtype=jnp.int32) * CHUNK
    last = jnp.sum((crop_offsets[None, :] <= chunk_edges[:, None]).astype(jnp.int32), axis=1) - 1
    order = jnp.arange(chunks, dtype=jnp.int32)
    spot = ((order // per) ^ member) * per + order % per
    segc = segment[:, None]
    segr = segment.reshape(chunks, 1, CHUNK)
    validc = pixel_valid[:, None]
    local_valid = pixel_valid[:local_rows]
    local_segment = segment[:local_rows]

    inputs = pixels.astype(F32)
    normed, norm1_back = jax.vjp(layer_norm, inputs, norm1_gain, norm1_bias)
    normed_slots = gather_slots(normed.astype(BF))
    late_grad = lax.optimization_barrier((out_grad, normed_slots[members // 2]))[0]
    grad_slots = gather_slots(late_grad)
    made = [
        project_qkv(normed_slots[s], qkv_weight, validc[s * local_rows : (s + 1) * local_rows])
        for s in range(members)
    ]
    q, k, v = (jnp.concatenate([m[i] for m in made], axis=0) for i in range(3))
    pack = tail_pack(last, k, v, segc)
    carry = gather_carry(pack, crops_at, here, groups, reach, False)
    num, den = attend(last, spot, q, k, v, segc, segr)
    sent = {
        s: project(s, local_rows, last, num, den, q, carry, segc, validc, out_weight)
        for s in reversed(range(members))
    }
    heads_slots, wide_slots, rinv_slots, parts = ([sent[s][i] for s in range(members)] for i in range(4))
    attended = scatter_slots(parts)
    middle = inputs + attended
    normed_two, norm2_back = jax.vjp(layer_norm, middle, norm2_gain, norm2_bias)
    two_slots = gather_slots(normed_two.astype(BF))
    active_slots, hidden_slots, two_parts, branch_parts = [], [], [], []
    for s in range(members):
        hidden = nn(two_slots[s], up_weight)
        activated, gelu_back = jax.vjp(gelu_tanh, hidden)
        activated = activated.astype(BF)
        hidden_grad = gelu_back(nt(grad_slots[s], down_weight))[0].astype(BF)
        two_parts.append(nt(hidden_grad, up_weight).astype(BF))
        branch_parts.append(nn(activated, down_weight).astype(BF))
        active_slots.append(activated)
        hidden_slots.append(hidden_grad)
    normed_two_grad = scatter_slots(two_parts)
    branch = scatter_slots(branch_parts)
    grad_all = jnp.concatenate(grad_slots, axis=0)
    down_grad = tn(jnp.concatenate(active_slots, axis=0), grad_all).astype(BF)
    up_grad = tn(jnp.concatenate(two_slots, axis=0), jnp.concatenate(hidden_slots, axis=0)).astype(BF)
    down_grad = lax.psum(down_grad, "rows").astype(F32)
    up_grad = lax.psum(up_grad, "rows").astype(F32)
    result = middle + branch
    middle_part, gain2_grad, bias2_grad = norm2_back(normed_two_grad)
    middle_grad = out_grad.astype(F32) + middle_part
    middle_slots = gather_slots(middle_grad.astype(BF))
    backs = [
        heads_back(s, last, middle_slots[s], out_weight, wide_slots[s], rinv_slots[s], q, segc)
        for s in range(members)
    ]
    ng, dg = (jnp.concatenate([b[i] for b in backs], axis=0) for i in range(2))
    grad_pack = functools.reduce(jnp.add, [b[2] for b in backs]).astype(BF)
    grad_carry = gather_carry(grad_pack, crops_at, here, groups, reach, True)
    out_weight_grad = tn(jnp.concatenate(heads_slots, axis=0), jnp.concatenate(middle_slots, axis=0))
    dq, dk, dv = attend_back(last, spot, q, k, v, ng, dg, segc, segr, carry)
    mixes = {
        s: mix(s, local_rows, last[-1:], dq, dk, dv, k, v, segc, validc, grad_carry, qkv_weight)
        for s in reversed(range(members))
    }
    normed_grad = scatter_slots([mixes[s][1] for s in range(members)])
    mixed_grad = jnp.concatenate([mixes[s][0] for s in range(members)], axis=0)
    qkv_grad = tn(mixed_grad, jnp.concatenate(normed_slots, axis=0)).astype(BF)
    bits = bits_of(groups)
    turned = bits[1:] + bits[:1]
    cut = 3 * width // 2
    qkv_grad = jnp.concatenate([sum_rows(qkv_grad[:cut], bits), sum_rows(qkv_grad[cut:], turned)], axis=0)
    qkv_grad = jnp.swapaxes(qkv_grad.reshape(3, width, D), 1, 2).astype(F32)
    out_weight_grad = sum_rows(out_weight_grad.astype(BF), turned).astype(F32)
    input_part, gain1_grad, bias1_grad = norm1_back(normed_grad)
    pixels_grad = (middle_grad + input_part).astype(BF)
    crop_onehot = (
        local_segment[:, None] == jnp.arange(crop_count, dtype=jnp.int32)[None, :]
    ).astype(F32)
    squares = (
        jnp.stack(
            [
                jnp.sum(result * result, axis=1),
                jnp.sum(attended * attended, axis=1),
                jnp.sum(branch * branch, axis=1),
                jnp.ones((local_rows,), F32),
            ]
        )
        * local_valid[None, :]
    )
    crop_sums = jnp.dot(squares, crop_onehot, precision=precise)
    early = sum_everywhere(jnp.concatenate([gain2_grad, bias2_grad, crop_sums.reshape(-1)]))
    gain2_grad, bias2_grad = early[:D], early[D : 2 * D]
    crop_sums = early[2 * D :].reshape(4, crop_count)
    late = sum_everywhere(jnp.concatenate([gain1_grad, bias1_grad]))
    gain1_grad, bias1_grad = late[:D], late[D:]
    crop_rms = jnp.sqrt(crop_sums[:3] / (D * jnp.maximum(crop_sums[3], 1.0))[None, :])
    return (
        result.astype(BF),
        pixels_grad,
        qkv_grad,
        out_weight_grad,
        up_grad,
        down_grad,
        gain1_grad,
        bias1_grad,
        gain2_grad,
        bias2_grad,
        crop_rms,
    )


def solution(mesh):
    split = P(("rows", "feat"), None)
    qkv, rows_feat, cols_feat = P(None, None, "feat"), P("feat", None), P(None, "feat")
    in_specs = (
        (split, qkv, rows_feat, cols_feat, rows_feat) + (P(),) * 6 + (P("rows"), split)
    )
    out_specs = (split, split, qkv, rows_feat, cols_feat, rows_feat) + (P(),) * 5
    return jax.shard_map(
        on_device, mesh=mesh, in_specs=in_specs, out_specs=out_specs, check_vma=False
    )
```

```python
import functools

import jax
import jax.numpy as jnp
from jax import lax
from jax.experimental import pallas as pl
from jax.experimental.pallas import tpu as pltpu
from jax.sharding import PartitionSpec as P

D = 1024
HEAD = 64
CHUNK = 128
CROP_MAX = 3072
UNROLL = 3
PACK = HEAD + 16

BF = jnp.bfloat16
F32 = jnp.float32
precise = lax.Precision.HIGHEST


def nn(a, b):
    return lax.dot_general(a, b, (((1,), (0,)), ((), ())), preferred_element_type=F32)


def nt(a, b):
    return lax.dot_general(a, b, (((1,), (1,)), ((), ())), preferred_element_type=F32)


def tn(a, b):
    return lax.dot_general(a, b, (((0,), (0,)), ((), ())), preferred_element_type=F32)


def same_head(width):
    row = lax.broadcasted_iota(jnp.int32, (width, width), 0) // HEAD
    col = lax.broadcasted_iota(jnp.int32, (width, width), 1) // HEAD
    return row == col


def lane_head(rows, width):
    return lax.broadcasted_iota(jnp.int32, (rows, width), 1) // HEAD


def causal(rows):
    row = lax.broadcasted_iota(jnp.int32, (rows, rows), 0)
    col = lax.broadcasted_iota(jnp.int32, (rows, rows), 1)
    return row >= col


def fold_heads(full, width):
    out = full[0:HEAD]
    for h in range(1, width // HEAD):
        out = out + full[h * HEAD : (h + 1) * HEAD]
    return out


def spread_heads(part, width, block):
    tall = jnp.concatenate([part] * (width // HEAD), axis=0)
    return jnp.where(block, tall, jnp.zeros_like(tall))


def pick(mask, value):
    return jnp.where(mask, value, jnp.zeros_like(value))


def vmem():
    return pl.BlockSpec(memory_space=pltpu.VMEM)


def smem():
    return pl.BlockSpec(memory_space=pltpu.SMEM)


def anywhere():
    return pl.BlockSpec(memory_space=pl.ANY)


def shape(rows, cols, kind):
    return jax.ShapeDtypeStruct((rows, cols), kind)


def whole_spec(array):
    rank = len(array.shape)
    return pl.BlockSpec(array.shape, lambda i: (0,) * rank)


def row_spec(tile, cols, start=0):
    return pl.BlockSpec((tile, cols), lambda i: (start + i, 0))


def first_spec(tile, cols, half):
    return pl.BlockSpec((tile, cols), lambda i: (jnp.minimum(i, half - 1), 0))


def second_spec(tile, cols, half):
    return pl.BlockSpec((tile, cols), lambda i: (jnp.maximum(i - half, 0), 0))


def either(first_ref, second_ref):
    half = pl.num_programs(0) // 2
    return jnp.where(pl.program_id(0) < half, first_ref[...], second_ref[...])


def put_either(first_ref, second_ref, value):
    half = pl.num_programs(0) // 2

    @pl.when(pl.program_id(0) < half)
    def _():
        first_ref[...] = value

    @pl.when(pl.program_id(0) >= half)
    def _():
        second_ref[...] = value


ROW_TILE = 192


def normal(values):
    centre = jnp.mean(values, axis=-1, keepdims=True)
    moved = values - centre
    scale = lax.rsqrt(jnp.mean(moved * moved, axis=-1, keepdims=True) + 1e-05)
    return moved * scale, scale


def normal_back(grad, gain, xhat, scale):
    g = grad * gain
    return scale * (
        g - jnp.mean(g, axis=-1, keepdims=True) - xhat * jnp.mean(g * xhat, axis=-1, keepdims=True)
    )


def total(refs):
    value = refs[0][...].astype(F32)
    for ref in refs[1:]:
        value = value + ref[...].astype(F32)
    return value


def gain_sums(grad, xhat, gain_ref, bias_ref):
    @pl.when(pl.program_id(0) == 0)
    def _():
        gain_ref[...] = jnp.zeros_like(gain_ref)
        bias_ref[...] = jnp.zeros_like(bias_ref)

    gain_ref[...] += jnp.sum(grad * xhat, axis=0, keepdims=True)
    bias_ref[...] += jnp.sum(grad, axis=0, keepdims=True)


def norm_body(x_ref, gain_ref, bias_ref, out_ref):
    xhat, _ = normal(x_ref[...].astype(F32))
    out_ref[...] = (xhat * gain_ref[...] + bias_ref[...]).astype(BF)


def norm_one(x, gain, bias):
    rows = x.shape[0]
    return pl.pallas_call(
        norm_body,
        grid=(rows // ROW_TILE,),
        out_shape=shape(rows, D, BF),
        in_specs=[row_spec(ROW_TILE, D), whole_spec(gain), whole_spec(bias)],
        out_specs=row_spec(ROW_TILE, D),
        name="norm_one",
    )(x, gain, bias)


def middle_body(*refs):
    x_ref, gain_ref, bias_ref = refs[:3]
    parts = refs[3:-3]
    middle_ref, out_ref, square_ref = refs[-3:]
    attended = total(parts)
    middle = x_ref[...].astype(F32) + attended
    middle_ref[...] = middle
    xhat, _ = normal(middle)
    out_ref[...] = (xhat * gain_ref[...] + bias_ref[...]).astype(BF)
    square_ref[...] = jnp.sum(attended * attended, axis=-1, keepdims=True)


def norm_two(x, gain, bias, parts):
    rows = x.shape[0]
    return pl.pallas_call(
        middle_body,
        grid=(rows // ROW_TILE,),
        out_shape=(shape(rows, D, F32), shape(rows, D, BF), shape(rows, 1, F32)),
        in_specs=[row_spec(ROW_TILE, D), whole_spec(gain), whole_spec(bias)]
        + [row_spec(ROW_TILE, D)] * len(parts),
        out_specs=(row_spec(ROW_TILE, D), row_spec(ROW_TILE, D), row_spec(ROW_TILE, 1)),
        name="norm_two",
    )(x, gain, bias, *parts)


def middle_back_body(*refs):
    grad_ref, middle_ref, gain_ref = refs[:3]
    parts = refs[3:-4]
    wide_ref, low_ref, gain_grad_ref, bias_grad_ref = refs[-4:]
    grad = total(parts)
    xhat, scale = normal(middle_ref[...])
    gain_sums(grad, xhat, gain_grad_ref, bias_grad_ref)
    out = grad_ref[...].astype(F32) + normal_back(grad, gain_ref[...], xhat, scale)
    wide_ref[...] = out
    low_ref[...] = out.astype(BF)


def norm_two_back(grad, middle, gain, parts):
    rows = grad.shape[0]
    return pl.pallas_call(
        middle_back_body,
        grid=(rows // ROW_TILE,),
        out_shape=(shape(rows, D, F32), shape(rows, D, BF), shape(1, D, F32), shape(1, D, F32)),
        in_specs=[row_spec(ROW_TILE, D), row_spec(ROW_TILE, D), whole_spec(gain)]
        + [row_spec(ROW_TILE, D)] * len(parts),
        out_specs=(row_spec(ROW_TILE, D), row_spec(ROW_TILE, D), whole_spec(gain), whole_spec(gain)),
        name="norm_two_back",
    )(grad, middle, gain, *parts)


def pixels_back_body(*refs):
    x_ref, wide_ref, gain_ref = refs[:3]
    parts = refs[3:-3]
    out_ref, gain_grad_ref, bias_grad_ref = refs[-3:]
    grad = total(parts)
    xhat, scale = normal(x_ref[...].astype(F32))
    gain_sums(grad, xhat, gain_grad_ref, bias_grad_ref)
    out_ref[...] = (wide_ref[...] + normal_back(grad, gain_ref[...], xhat, scale)).astype(BF)


def norm_one_back(x, wide, gain, parts):
    rows = x.shape[0]
    return pl.pallas_call(
        pixels_back_body,
        grid=(rows // ROW_TILE,),
        out_shape=(shape(rows, D, BF), shape(1, D, F32), shape(1, D, F32)),
        in_specs=[row_spec(ROW_TILE, D), row_spec(ROW_TILE, D), whole_spec(gain)]
        + [row_spec(ROW_TILE, D)] * len(parts),
        out_specs=(row_spec(ROW_TILE, D), whole_spec(gain), whole_spec(gain)),
        name="norm_one_back",
    )(x, wide, gain, *parts)


def result_body(*refs):
    middle_ref = refs[0]
    parts = refs[1:-3]
    out_ref, result_square_ref, branch_square_ref = refs[-3:]
    branch = total(parts)
    result = middle_ref[...] + branch
    out_ref[...] = result.astype(BF)
    result_square_ref[...] = jnp.sum(result * result, axis=-1, keepdims=True)
    branch_square_ref[...] = jnp.sum(branch * branch, axis=-1, keepdims=True)


def finish(middle, parts):
    rows = middle.shape[0]
    return pl.pallas_call(
        result_body,
        grid=(rows // ROW_TILE,),
        out_shape=(shape(rows, D, BF), shape(rows, 1, F32), shape(rows, 1, F32)),
        in_specs=[row_spec(ROW_TILE, D)] * (1 + len(parts)),
        out_specs=(row_spec(ROW_TILE, D), row_spec(ROW_TILE, 1), row_spec(ROW_TILE, 1)),
        name="finish",
    )(middle, *parts)


def qkv_body(tail_ref, xa_ref, xb_ref, w_ref, valid_ref, seg_ref, was_ref, *rest):
    q_ref, k_ref, v_ref, pack_ref = rest[-4:]
    width = q_ref.shape[1]
    x = either(xa_ref, xb_ref)
    q_ref[...] = feature(nn(x, w_ref[0])).astype(BF)
    k = (feature(nn(x, w_ref[1])) * valid_ref[...]).astype(BF)
    v = nn(x, w_ref[2]).astype(BF)
    k_ref[...] = k
    v_ref[...] = v
    kept = pick(seg_ref[...] == tail_ref[0], k)
    state = fold_heads(pick(same_head(width), tn(kept, v)), width)
    sums = jnp.sum(kept.astype(F32), axis=0, keepdims=True)

    @pl.when(pl.program_id(0) == 0)
    def _():
        pack_ref[...] = was_ref[...]

    pack_ref[0:HEAD, :] += state
    pack_ref[HEAD:PACK, :] += jnp.broadcast_to(sums, (PACK - HEAD, width))


def project_qkv(pair, tail, xa, xb, w, valid, seg, was, made):
    rows, width = xa.shape[0], w.shape[2]
    half = rows // ROW_TILE
    at = lambda cols: row_spec(ROW_TILE, cols, pair * 2 * half)
    whole = valid.shape[0]
    return pl.pallas_call(
        qkv_body,
        grid=(2 * half,),
        out_shape=(shape(whole, width, BF),) * 3 + (shape(PACK, width, F32),),
        in_specs=[
            smem(), first_spec(ROW_TILE, D, half), second_spec(ROW_TILE, D, half), whole_spec(w),
            at(1), at(1), whole_spec(was),
        ]
        + [anywhere()] * len(made),
        out_specs=(at(width), at(width), at(width), whole_spec(was)),
        input_output_aliases={7 + i: i for i in range(len(made))},
        name="project_qkv",
    )(tail, xa, xb, w, valid, seg, was, *made)


def forward_body(
    last_ref, spot_ref, q_ref, k_ref, v_ref, segc_ref, segr_ref, num_ref, den_ref, st_ref, ks_ref
):
    rows, width = q_ref.shape
    size = CHUNK
    block = same_head(width)
    ones_block = block.astype(BF)
    lanes = lane_head(size, width)
    lower = causal(size)
    st_ref[...] = jnp.zeros_like(st_ref)
    ks_ref[...] = jnp.zeros_like(ks_ref)

    def chunk(c):
        spot = spot_ref[c]
        at = pl.ds(pl.multiple_of(spot * size, size), size)
        q, k, v = q_ref[at, :], k_ref[at, :], v_ref[at, :]
        seg = segc_ref[at, :]
        keep = lower & (seg == segr_ref[spot])
        before, after = last_ref[c], last_ref[c + 1]
        carried = (seg == before).astype(F32)
        num = carried * nn(q, st_ref[...].astype(BF))
        den = carried * nn((q.astype(F32) * ks_ref[0:1, :]).astype(BF), ones_block)
        for h in range(width // HEAD):
            mine = lanes == h
            score = pick(keep, nt(pick(mine, q), k)).astype(BF)
            num = num + nn(score, pick(mine, v))
            den = den + nn(score, mine.astype(BF))
        num_ref[at, :] = num
        den_ref[at, :] = den
        kept = pick(seg == after, k)
        cont = (before == after).astype(F32)
        st_ref[...] = cont * st_ref[...] + pick(block, tn(kept, v))
        ks_ref[...] = cont * ks_ref[...] + jnp.sum(kept.astype(F32), axis=0, keepdims=True)

    def step(i, carry):
        for j in range(UNROLL):
            chunk(i * UNROLL + j)
        return carry

    lax.fori_loop(0, rows // size // UNROLL, step, 0)


def attend(last, spot, q, k, v, segc, segr):
    rows, width = q.shape
    return pl.pallas_call(
        forward_body,
        out_shape=(shape(rows, width, F32),) * 2,
        in_specs=[smem()] * 2 + [vmem()] * 5,
        out_specs=(vmem(),) * 2,
        scratch_shapes=[pltpu.VMEM((width, width), F32), pltpu.VMEM((8, width), F32)],
        name="attend",
    )(last, spot, q, k, v, segc, segr)


def project_body(
    first_ref, num_ref, den_ref, q_ref, pack_ref, segc_ref, valid_ref, w_ref,
    heads_ref, wide_ref, rinv_ref, a_ref, b_ref
):
    rows, width = q_ref.shape
    block = same_head(width)
    state = spread_heads(pack_ref[0:HEAD, :], width, block).astype(BF)
    sums = pack_ref[HEAD : HEAD + 1, :]
    q = q_ref[...]
    opening = (segc_ref[...] == first_ref[0]).astype(F32)
    valid = valid_ref[...]
    num = num_ref[...] + opening * nn(q, state)
    den = den_ref[...] + opening * nn((q.astype(F32) * sums).astype(BF), block.astype(BF))
    rinv = valid / (den + 1e-06 + 1.0 - valid)
    wide = num * rinv
    heads = wide.astype(BF)
    heads_ref[...] = heads
    wide_ref[...] = wide
    rinv_ref[...] = rinv
    put_either(a_ref, b_ref, nn(heads, w_ref[...]).astype(BF))


def project(pair, rows, last, num, den, q, pack, segc, valid, w):
    width = q.shape[1]
    half = rows // ROW_TILE
    at = lambda cols: row_spec(ROW_TILE, cols, pair * 2 * half)
    mine = lambda cols: row_spec(ROW_TILE, cols)
    return pl.pallas_call(
        project_body,
        grid=(2 * half,),
        out_shape=(shape(2 * rows, width, BF), shape(2 * rows, width, F32), shape(2 * rows, width, F32))
        + (shape(rows, D, BF),) * 2,
        in_specs=[smem(), at(width), at(width), at(width), whole_spec(pack), at(1), at(1), whole_spec(w)],
        out_specs=(
            mine(width), mine(width), mine(width),
            first_spec(ROW_TILE, D, half), second_spec(ROW_TILE, D, half),
        ),
        name="project",
    )(last, num, den, q, pack, segc, valid, w)


HIDDEN_TILE = 256


def mlp_body(
    xa_ref, xb_ref, ga_ref, gb_ref, up_ref, down_ref,
    act_ref, hid_ref, na_ref, nb_ref, ba_ref, bb_ref, nacc_ref, bacc_ref
):
    rows = xa_ref.shape[0]
    up, down = up_ref[...], down_ref[...]
    root = 0.7978845608028654
    first = pl.program_id(0) == 0

    @pl.when(first)
    def _():
        nacc_ref[...] = jnp.zeros_like(nacc_ref)
        bacc_ref[...] = jnp.zeros_like(bacc_ref)

    for i, (x_ref, g_ref) in enumerate(((xa_ref, ga_ref), (xb_ref, gb_ref))):
        at = slice(i * rows, (i + 1) * rows)
        h = nn(x_ref[...], up)
        grad = nt(g_ref[...], down)
        square = h * h
        t = jnp.tanh(root * h * (1.0 + 0.044715 * square))
        act = (0.5 * h * (1.0 + t)).astype(BF)
        slope = 0.5 * (1.0 + t) + 0.5 * h * (1.0 - t * t) * (root * (1.0 + 3.0 * 0.044715 * square))
        hid = (grad * slope).astype(BF)
        act_ref[at, :] = act
        hid_ref[at, :] = hid
        nacc_ref[at, :] += nt(hid, up)
        bacc_ref[at, :] += nn(act, down)

    @pl.when(pl.program_id(0) == pl.num_programs(0) - 1)
    def _():
        na_ref[...] = nacc_ref[0:rows, :].astype(BF)
        nb_ref[...] = nacc_ref[rows:, :].astype(BF)
        ba_ref[...] = bacc_ref[0:rows, :].astype(BF)
        bb_ref[...] = bacc_ref[rows:, :].astype(BF)


def mlp(xa, xb, ga, gb, up, down):
    rows, hidden = xa.shape[0], up.shape[1]
    col = pl.BlockSpec((2 * rows, HIDDEN_TILE), lambda i: (0, i))
    return pl.pallas_call(
        mlp_body,
        grid=(hidden // HIDDEN_TILE,),
        out_shape=(shape(2 * rows, hidden, BF),) * 2 + (shape(rows, D, BF),) * 4,
        in_specs=[whole_spec(xa)] * 4
        + [pl.BlockSpec((D, HIDDEN_TILE), lambda i: (0, i)), row_spec(HIDDEN_TILE, D)],
        out_specs=(col, col) + (whole_spec(xa),) * 4,
        scratch_shapes=[pltpu.VMEM((2 * rows, D), F32)] * 2,
        name="mlp",
    )(xa, xb, ga, gb, up, down)


def heads_back_body(
    first_ref, ga_ref, gb_ref, w_ref, wide_ref, rinv_ref, q_ref, segc_ref, was_ref, *rest
):
    ng_ref, dg_ref, pack_ref = rest[-3:]
    width = q_ref.shape[1]
    block = same_head(width)
    ones_block = block.astype(BF)
    hg = nt(either(ga_ref, gb_ref), w_ref[...])
    rinv = rinv_ref[...]
    ng = (hg * rinv).astype(BF)
    prod = hg * wide_ref[...]
    high = prod.astype(BF)
    low = (prod - high.astype(F32)).astype(BF)
    dg = -(nn(high, ones_block) + nn(low, ones_block)) * rinv
    ng_ref[...] = ng
    dg_ref[...] = dg
    opened = pick(segc_ref[...] == first_ref[0], q_ref[...])

    @pl.when(pl.program_id(0) == 0)
    def _():
        pack_ref[...] = was_ref[...]

    pack_ref[0:HEAD, :] += fold_heads(pick(block, tn(opened, ng)), width)
    sums = jnp.sum(opened.astype(F32) * dg, axis=0, keepdims=True)
    pack_ref[HEAD:PACK, :] += jnp.broadcast_to(sums, (PACK - HEAD, width))


def heads_back(pair, last, ga, gb, w, wide, rinv, q, segc, was, made):
    rows, width = ga.shape[0], q.shape[1]
    half = rows // ROW_TILE
    at = lambda cols: row_spec(ROW_TILE, cols, pair * 2 * half)
    mine = lambda cols: row_spec(ROW_TILE, cols)
    return pl.pallas_call(
        heads_back_body,
        grid=(2 * half,),
        out_shape=(shape(q.shape[0], width, BF), shape(q.shape[0], width, F32), shape(PACK, width, F32)),
        in_specs=[
            smem(), first_spec(ROW_TILE, D, half), second_spec(ROW_TILE, D, half), whole_spec(w),
            mine(width), mine(width), at(width), at(1), whole_spec(was),
        ]
        + [anywhere()] * len(made),
        out_specs=(at(width), at(width), whole_spec(was)),
        input_output_aliases={9 + i: i for i in range(len(made))},
        name="heads_back",
    )(last, ga, gb, w, wide, rinv, q, segc, was, *made)


def backward_body(
    last_ref, spot_ref, q_ref, k_ref, v_ref, ng_ref, dg_ref, segc_ref, segr_ref, pack_ref,
    dq_ref, dk_ref, dv_ref, all_ref, sums_ref, st_ref, ks_ref
):
    rows, width = q_ref.shape
    size = CHUNK
    count = rows // size
    block = same_head(width)
    lanes = lane_head(size, width)
    lower = causal(size)
    st_ref[...] = spread_heads(pack_ref[0:HEAD, :], width, block)
    ks_ref[...] = jnp.broadcast_to(pack_ref[HEAD : HEAD + 1, :], ks_ref.shape)

    def collect(c):
        at = pl.ds(pl.multiple_of(spot_ref[c] * size, size), size)
        all_ref[c] = st_ref[...].astype(BF)
        sums_ref[c] = ks_ref[...]
        before, after = last_ref[c], last_ref[c + 1]
        kept = pick(segc_ref[at, :] == after, k_ref[at, :])
        cont = (before == after).astype(F32)
        st_ref[...] = cont * st_ref[...] + pick(block, tn(kept, v_ref[at, :]))
        ks_ref[...] = cont * ks_ref[...] + jnp.sum(kept.astype(F32), axis=0, keepdims=True)

    def collects(i, carry):
        for j in range(UNROLL):
            collect(i * UNROLL + j)
        return carry

    lax.fori_loop(0, count // UNROLL, collects, 0)
    st_ref[...] = jnp.zeros_like(st_ref)
    ks_ref[...] = jnp.zeros_like(ks_ref)

    def chunk(c):
        spot = spot_ref[c]
        at = pl.ds(pl.multiple_of(spot * size, size), size)
        q, k, v, ng, dg = q_ref[at, :], k_ref[at, :], v_ref[at, :], ng_ref[at, :], dg_ref[at, :]
        seg = segc_ref[at, :]
        keep = lower & (seg == segr_ref[spot])
        before, after = last_ref[c], last_ref[c + 1]
        opened = seg == before
        carried = opened.astype(F32)
        tail = (seg == after).astype(F32)
        grad_state = st_ref[...].astype(BF)
        dq = carried * (nt(ng, all_ref[c]) + dg * sums_ref[c][0:1, :])
        dk = tail * (nt(v, grad_state) + ks_ref[0:1, :])
        dv = tail * nn(k, grad_state)
        for h in range(width // HEAD):
            mine = lanes == h
            qh, kh, nh = pick(mine, q), pick(mine, k), pick(mine, ng)
            score = pick(keep, nt(qh, k)).astype(BF)
            lead = dg[:, h * HEAD : h * HEAD + 1]
            back = pick(keep, nt(nh, v) + lead).astype(BF)
            dq = dq + nn(back, kh)
            dk = dk + tn(back, qh)
            dv = dv + tn(score, nh)
        dq_ref[at, :] = (dq * jnp.minimum(q.astype(F32), 1.0)).astype(BF)
        dk_ref[at, :] = dk
        dv_ref[at, :] = dv
        cont = (before == after).astype(F32)
        st_ref[...] = cont * st_ref[...] + pick(block, tn(pick(opened, q), ng))
        ks_ref[...] = cont * ks_ref[...] + jnp.sum(carried * q.astype(F32) * dg, axis=0, keepdims=True)

    def step(i, carry):
        for j in range(UNROLL):
            chunk(count - 1 - i * UNROLL - j)
        return carry

    lax.fori_loop(0, count // UNROLL, step, 0)


def attend_back(last, spot, q, k, v, ng, dg, segc, segr, pack):
    rows, width = q.shape
    count = rows // CHUNK
    return pl.pallas_call(
        backward_body,
        out_shape=(shape(rows, width, BF), shape(rows, width, F32), shape(rows, width, F32)),
        in_specs=[smem()] * 2 + [vmem()] * 8,
        out_specs=(vmem(),) * 3,
        scratch_shapes=[
            pltpu.VMEM((count, width, width), BF),
            pltpu.VMEM((count, 8, width), F32),
            pltpu.VMEM((width, width), F32),
            pltpu.VMEM((8, width), F32),
        ],
        name="attend_back",
    )(last, spot, q, k, v, ng, dg, segc, segr, pack)


def mix_body(
    tail_ref, dq_ref, dk_ref, dv_ref, k_ref, v_ref, segc_ref, valid_ref, pack_ref, w_ref,
    mixed_ref, a_ref, b_ref
):
    rows, width = k_ref.shape
    block = same_head(width)
    state = spread_heads(pack_ref[0:HEAD, :], width, block).astype(BF)
    sums = pack_ref[HEAD : HEAD + 1, :]
    tail = (segc_ref[...] == tail_ref[0]).astype(F32)
    k = k_ref[...]
    dk = dk_ref[...] + tail * (nt(v_ref[...], state) + sums)
    dv = dv_ref[...] + tail * nn(k, state)
    dq = dq_ref[...]
    dk = (valid_ref[...] * dk * jnp.minimum(k.astype(F32), 1.0)).astype(BF)
    dv = dv.astype(BF)
    mixed_ref[:, 0:width] = dq
    mixed_ref[:, width : 2 * width] = dk
    mixed_ref[:, 2 * width : 3 * width] = dv
    out = nt(dq, w_ref[0]) + nt(dk, w_ref[1]) + nt(dv, w_ref[2])
    put_either(a_ref, b_ref, out.astype(BF))


def mix(pair, rows, tail, dq, dk, dv, k, v, segc, valid, pack, w):
    width = k.shape[1]
    half = rows // ROW_TILE
    at = lambda cols: row_spec(ROW_TILE, cols, pair * 2 * half)
    return pl.pallas_call(
        mix_body,
        grid=(2 * half,),
        out_shape=(shape(2 * rows, 3 * width, BF),) + (shape(rows, D, BF),) * 2,
        in_specs=[smem()] + [at(width)] * 5 + [at(1)] * 2 + [whole_spec(pack), whole_spec(w)],
        out_specs=(
            row_spec(ROW_TILE, 3 * width),
            first_spec(ROW_TILE, D, half), second_spec(ROW_TILE, D, half),
        ),
        name="mix",
    )(tail, dq, dk, dv, k, v, segc, valid, pack, w)


def feature(values):
    return jnp.where(values > 0, values + 1.0, jnp.exp(jnp.minimum(values, 0.0)))


def bits_of(count):
    return [1 << b for b in range(count.bit_length() - 1)]


def swap(value, axis, bit):
    return lax.ppermute(value, axis, [(i, i ^ bit) for i in range(lax.axis_size(axis))])


def gather_slots(value):
    slots = {0: value}
    for bit in reversed(bits_of(lax.axis_size("feat"))):
        for s in sorted(slots):
            slots[s | bit] = swap(slots[s], "feat", bit)
    return [slots[s] for s in range(len(slots))]


def scatter_slots(parts, after=None):
    parts = {s: [part] for s, part in enumerate(parts)}
    for bit in bits_of(lax.axis_size("feat")):
        for s in sorted(parts, reverse=True):
            if s & bit:
                pieces = parts.pop(s)
                value = pieces[0]
                if len(pieces) > 1:
                    value = functools.reduce(jnp.add, [p.astype(F32) for p in pieces]).astype(BF)
                if after is not None and bit > 1:
                    value = lax.optimization_barrier((value, after))[0]
                parts[s ^ bit].append(swap(value, "feat", bit))
    return parts[0]


def sum_everywhere(value):
    for axis in ("feat", "rows"):
        for bit in bits_of(lax.axis_size(axis)):
            value = value + swap(value, axis, bit)
    return value


def sum_rows(value, order):
    here = lax.axis_index("rows")
    for bit in order:
        half = value.shape[0] // 2
        upper = (here & bit) != 0
        low, high = value[:half], value[half:]
        got = swap(jnp.where(upper, low, high), "rows", bit)
        value = (jnp.where(upper, high, low).astype(F32) + got.astype(F32)).astype(BF)
    for bit in reversed(order):
        upper = (here & bit) != 0
        got = swap(value, "rows", bit)
        value = jnp.concatenate([jnp.where(upper, got, value), jnp.where(upper, value, got)], axis=0)
    return value


def sum_pieces(value, count, order, turned):
    size = value.shape[0] // count
    return jnp.concatenate(
        [
            sum_rows(value[i * size : (i + 1) * size], turned if i % 2 else order)
            for i in range(count)
        ],
        axis=0,
    )


def shifted(pack, hop, groups, reverse):
    if reverse:
        pairs = [(i, i - hop) for i in range(hop, groups)]
    else:
        pairs = [(i, i + hop) for i in range(groups - hop)]
    return lax.ppermute(pack, "rows", pairs)


def gather_carry(pack, crops_at, here, groups, reach, reverse):
    total = jnp.zeros(pack.shape, F32)
    mine = crops_at[here + 1] if reverse else crops_at[here]
    for hop in range(1, reach + 1):
        got = shifted(pack, hop, groups, reverse).astype(F32)
        other = here + hop if reverse else here - hop
        inside = (other < groups) if reverse else (other >= 0)
        at = jnp.clip(other, 0, groups - 1)
        theirs = crops_at[at] if reverse else crops_at[at + 1]
        total = total + jnp.where(inside & (theirs == mine), got, 0.0)
    return total


def on_device(
    pixels,
    qkv_weight,
    out_weight,
    up_weight,
    down_weight,
    norm1_gain,
    norm1_bias,
    norm2_gain,
    norm2_bias,
    crop_lengths,
    crop_offsets,
    pixel_mask,
    out_grad,
):
    local_rows = pixels.shape[0]
    group_rows = pixel_mask.shape[0]
    width = qkv_weight.shape[2]
    crop_count = crop_offsets.shape[0]
    groups = lax.axis_size("rows")
    members = lax.axis_size("feat")
    pairs = members // 2
    here = lax.axis_index("rows")
    member = lax.axis_index("feat")
    reach = min(groups - 1, -(-(CROP_MAX - 1) // group_rows))
    group_start = here * group_rows
    slot_ids = jnp.arange(members, dtype=jnp.int32) ^ member
    in_group = (slot_ids[:, None] * local_rows + jnp.arange(local_rows, dtype=jnp.int32)[None, :]).reshape(-1)
    places = group_start + in_group
    started = crop_offsets[None, :] <= places[:, None]
    crop_ends = crop_offsets + crop_lengths
    segment = jnp.sum(started.astype(jnp.int32), axis=1) - 1
    inside = jnp.sum((started & (places[:, None] < crop_ends[None, :])).astype(jnp.int32), axis=1)
    mask = jnp.concatenate(
        [
            lax.dynamic_slice_in_dim(pixel_mask, (member ^ s) * local_rows, local_rows)
            for s in range(members)
        ]
    )
    pixel_valid = (mask * inside).astype(F32)
    edges = jnp.arange(groups + 1, dtype=jnp.int32) * group_rows - 1
    crops_at = jnp.sum((crop_offsets[None, :] <= edges[:, None]).astype(jnp.int32), axis=1) - 1
    chunks = group_rows // CHUNK
    per = local_rows // CHUNK
    chunk_edges = group_start - 1 + jnp.arange(chunks + 1, dtype=jnp.int32) * CHUNK
    last = jnp.sum((crop_offsets[None, :] <= chunk_edges[:, None]).astype(jnp.int32), axis=1) - 1
    tail = last[-1:]
    order = jnp.arange(chunks, dtype=jnp.int32)
    spot = ((order // per) ^ member) * per + order % per
    segc = segment[:, None]
    segr = segment.reshape(chunks, 1, CHUNK)
    validc = pixel_valid[:, None]
    gain1, bias1, gain2, bias2 = (
        a[None, :] for a in (norm1_gain, norm1_bias, norm2_gain, norm2_bias)
    )
    no_pack = jnp.zeros((PACK, width), F32)

    normed_slots = gather_slots(norm_one(pixels, gain1, bias1))
    late_grad = lax.optimization_barrier((out_grad, normed_slots[members // 2]))[0]
    grad_slots = gather_slots(late_grad)
    made, pack = (), no_pack
    for p in range(pairs):
        *made, pack = project_qkv(
            p, tail, normed_slots[2 * p], normed_slots[2 * p + 1], qkv_weight, validc, segc, pack, made
        )
    q, k, v = made
    carry = gather_carry(pack.astype(BF), crops_at, here, groups, reach, False)
    num, den = attend(last, spot, q, k, v, segc, segr)
    sent = {
        p: project(p, local_rows, last, num, den, q, carry, segc, validc, out_weight)
        for p in reversed(range(pairs))
    }
    parts = [sent[s // 2][3 + s % 2] for s in range(members)]
    middle, normed_two, attended_square = norm_two(pixels, gain2, bias2, scatter_slots(parts))
    two_slots = gather_slots(normed_two)
    hidden = [
        mlp(*two_slots[2 * p : 2 * p + 2], *grad_slots[2 * p : 2 * p + 2], up_weight, down_weight)
        for p in range(pairs)
    ]
    two_parts = scatter_slots([hidden[s // 2][2 + s % 2] for s in range(members)])
    branch_parts = scatter_slots([hidden[s // 2][4 + s % 2] for s in range(members)], two_parts[-1])
    grad_all = jnp.concatenate(grad_slots, axis=0)
    down_grad = tn(jnp.concatenate([h[0] for h in hidden], axis=0), grad_all).astype(BF)
    up_grad = tn(jnp.concatenate(two_slots, axis=0), jnp.concatenate([h[1] for h in hidden], axis=0)).astype(BF)
    middle_grad, middle_low, gain2_grad, bias2_grad = norm_two_back(out_grad, middle, gain2, two_parts)
    middle_slots = gather_slots(middle_low)
    made, grad_pack = (), no_pack
    for p in range(pairs):
        *made, grad_pack = heads_back(
            p, last, middle_slots[2 * p], middle_slots[2 * p + 1], out_weight,
            sent[p][1], sent[p][2], q, segc, grad_pack, made
        )
    ng, dg = made
    grad_carry = gather_carry(grad_pack.astype(BF), crops_at, here, groups, reach, True)
    out_weight_grad = tn(
        jnp.concatenate([sent[p][0] for p in range(pairs)], axis=0), jnp.concatenate(middle_slots, axis=0)
    ).astype(BF)
    dq, dk, dv = attend_back(last, spot, q, k, v, ng, dg, segc, segr, carry)
    mixes = {
        p: mix(p, local_rows, tail, dq, dk, dv, k, v, segc, validc, grad_carry, qkv_weight)
        for p in reversed(range(pairs))
    }
    normed_parts = scatter_slots([mixes[s // 2][1 + s % 2] for s in range(members)])
    mixed_grad = jnp.concatenate([mixes[p][0] for p in range(pairs)], axis=0)
    qkv_grad = tn(mixed_grad, jnp.concatenate(normed_slots, axis=0)).astype(BF)
    output, result_square, branch_square = finish(middle, branch_parts)
    pixels_grad, gain1_grad, bias1_grad = norm_one_back(pixels, middle_grad, gain1, normed_parts)

    bits = bits_of(groups)
    turned = bits[1:] + bits[:1]
    down_grad = lax.psum(down_grad, "rows").astype(F32)
    up_grad = sum_pieces(up_grad, 4, bits, turned).astype(F32)
    out_weight_grad = sum_rows(out_weight_grad, turned).astype(F32)
    qkv_grad = sum_pieces(qkv_grad, 2, bits, turned)
    qkv_grad = jnp.swapaxes(qkv_grad.reshape(3, width, D), 1, 2).astype(F32)

    crop_onehot = (
        segment[:local_rows, None] == jnp.arange(crop_count, dtype=jnp.int32)[None, :]
    ).astype(F32)
    squares = (
        jnp.concatenate(
            [result_square, attended_square, branch_square, jnp.ones((local_rows, 1), F32)], axis=1
        )
        * validc[:local_rows]
    )
    crop_sums = lax.dot_general(
        squares, crop_onehot, (((0,), (0,)), ((), ())), precision=precise, preferred_element_type=F32
    )
    sums = jnp.concatenate(
        [gain1_grad[0], bias1_grad[0], gain2_grad[0], bias2_grad[0], crop_sums.reshape(-1)]
    )
    sums = sum_everywhere(sums)
    gain1_grad, bias1_grad, gain2_grad, bias2_grad = sums[: 4 * D].reshape(4, D)
    crop_sums = sums[4 * D :].reshape(4, crop_count)
    crop_rms = jnp.sqrt(crop_sums[:3] / (D * jnp.maximum(crop_sums[3], 1.0))[None, :])
    return (
        output,
        pixels_grad,
        qkv_grad,
        out_weight_grad,
        up_grad,
        down_grad,
        gain1_grad,
        bias1_grad,
        gain2_grad,
        bias2_grad,
        crop_rms,
    )


def solution(mesh):
    split = P(("rows", "feat"), None)
    qkv, rows_feat, cols_feat = P(None, None, "feat"), P("feat", None), P(None, "feat")
    in_specs = (
        (split, qkv, rows_feat, cols_feat, rows_feat) + (P(),) * 6 + (P("rows"), split)
    )
    out_specs = (split, split, qkv, rows_feat, cols_feat, rows_feat) + (P(),) * 5
    return jax.shard_map(
        on_device, mesh=mesh, in_specs=in_specs, out_specs=out_specs, check_vma=False
    )
```

```python
import functools

import jax
import jax.numpy as jnp
from jax import lax
from jax.experimental import pallas as pl
from jax.experimental.pallas import tpu as pltpu
from jax.sharding import PartitionSpec as P

D = 1024
HEAD = 64
CHUNK = 384
CROP_MAX = 3072
PACK = HEAD + 16

BF = jnp.bfloat16
F32 = jnp.float32
precise = lax.Precision.HIGHEST


def nn(a, b):
    return lax.dot_general(a, b, (((1,), (0,)), ((), ())), preferred_element_type=F32)


def nt(a, b):
    return lax.dot_general(a, b, (((1,), (1,)), ((), ())), preferred_element_type=F32)


def tn(a, b):
    return lax.dot_general(a, b, (((0,), (0,)), ((), ())), preferred_element_type=F32)


def same_head(width):
    row = lax.broadcasted_iota(jnp.int32, (width, width), 0) // HEAD
    col = lax.broadcasted_iota(jnp.int32, (width, width), 1) // HEAD
    return row == col


def lane_head(rows, width):
    return lax.broadcasted_iota(jnp.int32, (rows, width), 1) // HEAD


def causal(rows):
    row = lax.broadcasted_iota(jnp.int32, (rows, rows), 0)
    col = lax.broadcasted_iota(jnp.int32, (rows, rows), 1)
    return row >= col


def fold_heads(full, width):
    out = full[0:HEAD]
    for h in range(1, width // HEAD):
        out = out + full[h * HEAD : (h + 1) * HEAD]
    return out


def spread_heads(part, width, block):
    tall = jnp.concatenate([part] * (width // HEAD), axis=0)
    return jnp.where(block, tall, jnp.zeros_like(tall))


def pick(mask, value):
    return jnp.where(mask, value, jnp.zeros_like(value))


def vmem():
    return pl.BlockSpec(memory_space=pltpu.VMEM)


def smem():
    return pl.BlockSpec(memory_space=pltpu.SMEM)


def shape(rows, cols, kind):
    return jax.ShapeDtypeStruct((rows, cols), kind)


ROW_TILE = 192


def tiles(rows):
    return [slice(i, i + ROW_TILE) for i in range(0, rows, ROW_TILE)]


def kernel(body, name, out_shape, in_specs, megabytes, flops=0, scratch=(), aliases=None):
    outs = vmem() if not isinstance(out_shape, tuple) else (vmem(),) * len(out_shape)
    return pl.pallas_call(
        body,
        out_shape=out_shape,
        in_specs=in_specs,
        out_specs=outs,
        scratch_shapes=list(scratch),
        input_output_aliases=aliases or {},
        compiler_params=pltpu.CompilerParams(vmem_limit_bytes=megabytes << 20),
        cost_estimate=pl.CostEstimate(flops=int(flops), bytes_accessed=0, transcendentals=0),
        name=name,
    )


US = 10**9


def normal(values):
    centre = jnp.mean(values, axis=-1, keepdims=True)
    moved = values - centre
    scale = lax.rsqrt(jnp.mean(moved * moved, axis=-1, keepdims=True) + 1e-05)
    return moved * scale, scale


def normal_back(grad, gain, xhat, scale):
    g = grad * gain
    return scale * (
        g - jnp.mean(g, axis=-1, keepdims=True) - xhat * jnp.mean(g * xhat, axis=-1, keepdims=True)
    )


def total(refs):
    value = refs[0][...].astype(F32)
    for ref in refs[1:]:
        value = value + ref[...].astype(F32)
    return value


def norm_body(x_ref, gain_ref, bias_ref, out_ref):
    for at in tiles(x_ref.shape[0]):
        xhat, _ = normal(x_ref[at, :].astype(F32))
        out_ref[at, :] = (xhat * gain_ref[...] + bias_ref[...]).astype(BF)


def norm_one(x, gain, bias):
    call = kernel(norm_body, "norm_one", shape(x.shape[0], D, BF), [vmem()] * 3, 8, 2 * US)
    return call(x, gain, bias)


def total(refs, at):
    value = refs[0][at, :].astype(F32)
    for ref in refs[1:]:
        value = value + ref[at, :].astype(F32)
    return value


def middle_body(*refs):
    x_ref, gain_ref, bias_ref = refs[:3]
    parts = refs[3:-3]
    middle_ref, out_ref, square_ref = refs[-3:]
    for at in tiles(x_ref.shape[0]):
        attended = total(parts, at)
        middle = x_ref[at, :].astype(F32) + attended
        middle_ref[at, :] = middle
        xhat, _ = normal(middle)
        out_ref[at, :] = (xhat * gain_ref[...] + bias_ref[...]).astype(BF)
        square_ref[at, :] = jnp.sum(attended * attended, axis=-1, keepdims=True)


def norm_two(x, gain, bias, parts):
    rows = x.shape[0]
    call = kernel(
        middle_body, "norm_two", (shape(rows, D, F32), shape(rows, D, BF), shape(rows, 1, F32)),
        [vmem()] * (3 + len(parts)), 12, 3 * US,
    )
    return call(x, gain, bias, *parts)


def middle_back_body(*refs):
    grad_ref, middle_ref, gain_ref = refs[:3]
    parts = refs[3:-4]
    wide_ref, low_ref, gain_grad_ref, bias_grad_ref = refs[-4:]
    gain_grad = bias_grad = jnp.zeros(gain_ref.shape, F32)
    for at in tiles(grad_ref.shape[0]):
        grad = total(parts, at)
        xhat, scale = normal(middle_ref[at, :])
        gain_grad = gain_grad + jnp.sum(grad * xhat, axis=0, keepdims=True)
        bias_grad = bias_grad + jnp.sum(grad, axis=0, keepdims=True)
        out = grad_ref[at, :].astype(F32) + normal_back(grad, gain_ref[...], xhat, scale)
        wide_ref[at, :] = out
        low_ref[at, :] = out.astype(BF)
    gain_grad_ref[...] = gain_grad
    bias_grad_ref[...] = bias_grad


def norm_two_back(grad, middle, gain, parts):
    rows = grad.shape[0]
    call = kernel(
        middle_back_body, "norm_two_back",
        (shape(rows, D, F32), shape(rows, D, BF), shape(1, D, F32), shape(1, D, F32)),
        [vmem()] * (3 + len(parts)), 16, 4 * US,
    )
    return call(grad, middle, gain, *parts)


def pixels_back_body(*refs):
    x_ref, wide_ref, gain_ref = refs[:3]
    parts = refs[3:-3]
    out_ref, gain_grad_ref, bias_grad_ref = refs[-3:]
    gain_grad = bias_grad = jnp.zeros(gain_ref.shape, F32)
    for at in tiles(x_ref.shape[0]):
        grad = total(parts, at)
        xhat, scale = normal(x_ref[at, :].astype(F32))
        gain_grad = gain_grad + jnp.sum(grad * xhat, axis=0, keepdims=True)
        bias_grad = bias_grad + jnp.sum(grad, axis=0, keepdims=True)
        out_ref[at, :] = (wide_ref[at, :] + normal_back(grad, gain_ref[...], xhat, scale)).astype(BF)
    gain_grad_ref[...] = gain_grad
    bias_grad_ref[...] = bias_grad


def norm_one_back(x, wide, gain, parts):
    rows = x.shape[0]
    call = kernel(
        pixels_back_body, "norm_one_back", (shape(rows, D, BF), shape(1, D, F32), shape(1, D, F32)),
        [vmem()] * (3 + len(parts)), 16, 4 * US,
    )
    return call(x, wide, gain, *parts)


def result_body(*refs):
    middle_ref = refs[0]
    parts = refs[1:-3]
    out_ref, result_square_ref, branch_square_ref = refs[-3:]
    for at in tiles(middle_ref.shape[0]):
        branch = total(parts, at)
        result = middle_ref[at, :] + branch
        out_ref[at, :] = result.astype(BF)
        result_square_ref[at, :] = jnp.sum(result * result, axis=-1, keepdims=True)
        branch_square_ref[at, :] = jnp.sum(branch * branch, axis=-1, keepdims=True)


def finish(middle, parts):
    rows = middle.shape[0]
    call = kernel(
        result_body, "finish", (shape(rows, D, BF), shape(rows, 1, F32), shape(rows, 1, F32)),
        [vmem()] * (1 + len(parts)), 12, 2 * US,
    )
    return call(middle, *parts)


def pair_slices(pair, rows):
    for i in range(2):
        yield i, slice(i * rows, (i + 1) * rows), slice((2 * pair + i) * rows, (2 * pair + i + 1) * rows)


def qkv_body(pair, tail_ref, xa_ref, xb_ref, w_ref, valid_ref, seg_ref, was_ref, *rest):
    q_ref, k_ref, v_ref, pack_ref = rest[-4:]
    width = q_ref.shape[1]
    block = same_head(width)
    state, sums = was_ref[0:HEAD, :], was_ref[HEAD:PACK, :]
    for i, _, at in pair_slices(pair, xa_ref.shape[0]):
        x = (xa_ref, xb_ref)[i][...]
        q_ref[at, :] = feature(nn(x, w_ref[0])).astype(BF)
        k = (feature(nn(x, w_ref[1])) * valid_ref[at, :]).astype(BF)
        v = nn(x, w_ref[2]).astype(BF)
        k_ref[at, :] = k
        v_ref[at, :] = v
        kept = pick(seg_ref[at, :] == tail_ref[0], k)
        state = state + fold_heads(pick(block, tn(kept, v)), width)
        sums = sums + jnp.sum(kept.astype(F32), axis=0, keepdims=True)
    pack_ref[0:HEAD, :] = state
    pack_ref[HEAD:PACK, :] = sums


def project_qkv(pair, tail, xa, xb, w, valid, seg, was, made):
    width, whole = w.shape[2], valid.shape[0]
    call = kernel(
        functools.partial(qkv_body, pair), "project_qkv",
        (shape(whole, width, BF),) * 3 + (shape(PACK, width, F32),),
        [smem()] + [vmem()] * (6 + len(made)), 16, 4 * US,
        aliases={7 + i: i for i in range(len(made))},
    )
    return call(tail, xa, xb, w, valid, seg, was, *made)


def swap_heads(x):
    return jnp.concatenate(
        [pltpu.roll(x[:, i : i + 2 * HEAD], HEAD, 1) for i in range(0, x.shape[1], 2 * HEAD)], axis=1
    )


def forward_body(
    last_ref, spot_ref, q_ref, k_ref, v_ref, segc_ref, segr_ref, num_ref, den_ref, st_ref, ks_ref
):
    rows, width = q_ref.shape
    size = CHUNK
    block = same_head(width)
    ones_block = block.astype(BF)
    lanes = lane_head(size, width)
    even = (lanes % 2) == 0
    lower = causal(size)
    st_ref[...] = jnp.zeros_like(st_ref)
    ks_ref[...] = jnp.zeros_like(ks_ref)

    def step(c, carry):
        spot = spot_ref[c]
        at = pl.ds(pl.multiple_of(spot * size, size), size)
        q, k, v = q_ref[at, :], k_ref[at, :], v_ref[at, :]
        seg = segc_ref[at, :]
        keep = (lower & (seg == segr_ref[spot])).astype(BF)
        before, after = last_ref[c], last_ref[c + 1]
        carried = (seg == before).astype(F32)
        sums = [jnp.zeros((size, width), F32)] * 2
        for h in range(width // HEAD):
            mine = lanes == h
            score = nt(pick(mine, q), k).astype(BF) * keep
            both = jnp.where(mine, v, (lanes == (h ^ 1)).astype(BF))
            sums[h % 2] = sums[h % 2] + nn(score, both)
        num = jnp.where(even, sums[0], sums[1])
        den = swap_heads(jnp.where(even, sums[1], sums[0]))
        num_ref[at, :] = num + carried * nn(q, st_ref[...].astype(BF))
        den_ref[at, :] = den + carried * nn((q.astype(F32) * ks_ref[0:1, :]).astype(BF), ones_block)
        kept = pick(seg == after, k)
        cont = (before == after).astype(F32)
        st_ref[...] = cont * st_ref[...] + pick(block, tn(kept, v))
        ks_ref[...] = cont * ks_ref[...] + jnp.sum(kept.astype(F32), axis=0, keepdims=True)
        return carry

    lax.fori_loop(0, rows // size, step, 0)


def attend(last, spot, q, k, v, segc, segr):
    rows, width = q.shape
    call = kernel(
        forward_body, "attend", (shape(rows, width, F32),) * 2, [smem()] * 2 + [vmem()] * 5, 24, 7 * US,
        scratch=[pltpu.VMEM((width, width), F32), pltpu.VMEM((8, width), F32)],
    )
    return call(last, spot, q, k, v, segc, segr)


def project_body(
    pair, first_ref, num_ref, den_ref, q_ref, pack_ref, segc_ref, valid_ref, w_ref,
    heads_ref, wide_ref, rinv_ref, a_ref, b_ref
):
    width = q_ref.shape[1]
    block = same_head(width)
    state = spread_heads(pack_ref[0:HEAD, :], width, block).astype(BF)
    sums = pack_ref[HEAD : HEAD + 1, :]
    for i, own, at in pair_slices(pair, a_ref.shape[0]):
        q = q_ref[at, :]
        opening = (segc_ref[at, :] == first_ref[0]).astype(F32)
        valid = valid_ref[at, :]
        num = num_ref[at, :] + opening * nn(q, state)
        den = den_ref[at, :] + opening * nn((q.astype(F32) * sums).astype(BF), block.astype(BF))
        rinv = valid / (den + 1e-06 + 1.0 - valid)
        wide = num * rinv
        heads = wide.astype(BF)
        heads_ref[own, :] = heads
        wide_ref[own, :] = wide
        rinv_ref[own, :] = rinv
        (a_ref, b_ref)[i][...] = nn(heads, w_ref[...]).astype(BF)


def project(pair, rows, last, num, den, q, pack, segc, valid, w):
    width = q.shape[1]
    call = kernel(
        functools.partial(project_body, pair), "project",
        (shape(2 * rows, width, BF), shape(2 * rows, width, F32), shape(2 * rows, width, F32))
        + (shape(rows, D, BF),) * 2,
        [smem()] + [vmem()] * 7, 12, 3 * US,
    )
    return call(last, num, den, q, pack, segc, valid, w)


def mlp_body(
    xa_ref, xb_ref, ga_ref, gb_ref, up_ref, down_ref, act_ref, hid_ref, na_ref, nb_ref, ba_ref, bb_ref
):
    root = 0.7978845608028654
    tile = min(512, up_ref.shape[1])
    for i, own, _ in pair_slices(0, xa_ref.shape[0]):
        x, g = (xa_ref, xb_ref)[i][...], (ga_ref, gb_ref)[i][...]
        for j in range(0, up_ref.shape[1], tile):
            cols = slice(j, j + tile)
            h = nn(x, up_ref[:, cols])
            grad = nt(g, down_ref[cols, :])
            square = h * h
            t = jnp.tanh(root * h * (1.0 + 0.044715 * square))
            plus = 0.5 * (1.0 + t)
            slope = plus + 0.5 * h * (1.0 - t * t) * (root + (3.0 * 0.044715 * root) * square)
            act_ref[own, cols] = (h * plus).astype(BF)
            hid_ref[own, cols] = (grad * slope).astype(BF)
        (na_ref, nb_ref)[i][...] = nt(hid_ref[own, :], up_ref[...]).astype(BF)
        (ba_ref, bb_ref)[i][...] = nn(act_ref[own, :], down_ref[...]).astype(BF)


def mlp(xa, xb, ga, gb, up, down):
    rows, hidden = xa.shape[0], up.shape[1]
    call = kernel(
        mlp_body, "mlp", (shape(2 * rows, hidden, BF),) * 2 + (shape(rows, D, BF),) * 4,
        [vmem()] * 6, 32, 9 * US,
    )
    return call(xa, xb, ga, gb, up, down)


def heads_back_body(
    pair, first_ref, ga_ref, gb_ref, w_ref, wide_ref, rinv_ref, q_ref, segc_ref, was_ref, *rest
):
    ng_ref, dg_ref, pack_ref = rest[-3:]
    width = q_ref.shape[1]
    block = same_head(width)
    ones_block = block.astype(BF)
    state, sums = was_ref[0:HEAD, :], was_ref[HEAD:PACK, :]
    for i, own, at in pair_slices(pair, ga_ref.shape[0]):
        hg = nt((ga_ref, gb_ref)[i][...], w_ref[...])
        rinv = rinv_ref[own, :]
        ng = (hg * rinv).astype(BF)
        prod = hg * wide_ref[own, :]
        high = prod.astype(BF)
        low = (prod - high.astype(F32)).astype(BF)
        dg = -(nn(high, ones_block) + nn(low, ones_block)) * rinv
        ng_ref[at, :] = ng
        dg_ref[at, :] = dg
        opened = pick(segc_ref[at, :] == first_ref[0], q_ref[at, :])
        state = state + fold_heads(pick(block, tn(opened, ng)), width)
        sums = sums + jnp.sum(opened.astype(F32) * dg, axis=0, keepdims=True)
    pack_ref[0:HEAD, :] = state
    pack_ref[HEAD:PACK, :] = sums


def heads_back(pair, last, ga, gb, w, wide, rinv, q, segc, was, made):
    whole, width = q.shape
    call = kernel(
        functools.partial(heads_back_body, pair), "heads_back",
        (shape(whole, width, BF), shape(whole, width, F32), shape(PACK, width, F32)),
        [smem()] + [vmem()] * (8 + len(made)), 16, 4 * US,
        aliases={9 + i: i for i in range(len(made))},
    )
    return call(last, ga, gb, w, wide, rinv, q, segc, was, *made)


def backward_body(
    last_ref, spot_ref, q_ref, k_ref, v_ref, ng_ref, dg_ref, segc_ref, segr_ref, pack_ref,
    dq_ref, dk_ref, dv_ref, all_ref, sums_ref, st_ref, ks_ref
):
    rows, width = q_ref.shape
    size = CHUNK
    count = rows // size
    block = same_head(width)
    lanes = lane_head(size, width)
    half = (lax.broadcasted_iota(jnp.int32, (size, width), 1) % HEAD) < HEAD // 2
    lower = causal(size)
    st_ref[...] = spread_heads(pack_ref[0:HEAD, :], width, block)
    ks_ref[...] = jnp.broadcast_to(pack_ref[HEAD : HEAD + 1, :], ks_ref.shape)

    def collect(c, carry):
        at = pl.ds(pl.multiple_of(spot_ref[c] * size, size), size)
        all_ref[c] = st_ref[...].astype(BF)
        sums_ref[c] = ks_ref[...]
        before, after = last_ref[c], last_ref[c + 1]
        kept = pick(segc_ref[at, :] == after, k_ref[at, :])
        cont = (before == after).astype(F32)
        st_ref[...] = cont * st_ref[...] + pick(block, tn(kept, v_ref[at, :]))
        ks_ref[...] = cont * ks_ref[...] + jnp.sum(kept.astype(F32), axis=0, keepdims=True)
        return carry

    lax.fori_loop(0, count, collect, 0)
    st_ref[...] = jnp.zeros_like(st_ref)
    ks_ref[...] = jnp.zeros_like(ks_ref)

    def step(i, carry):
        c = count - 1 - i
        spot = spot_ref[c]
        at = pl.ds(pl.multiple_of(spot * size, size), size)
        q, k, v, ng, dg = q_ref[at, :], k_ref[at, :], v_ref[at, :], ng_ref[at, :], dg_ref[at, :]
        seg = segc_ref[at, :]
        keep = (lower & (seg == segr_ref[spot])).astype(BF)
        before, after = last_ref[c], last_ref[c + 1]
        opened = seg == before
        carried = opened.astype(F32)
        tail = (seg == after).astype(F32)
        grad_state = st_ref[...].astype(BF)
        moved = swap_heads(dg)
        high = moved.astype(BF)
        low = (moved - high.astype(F32)).astype(BF)
        terms = jnp.where(half, high, low) * jnp.asarray(2.0 / HEAD, BF)
        one = jnp.ones((), BF)
        dq = carried * (nt(ng, all_ref[c]) + dg * sums_ref[c][0:1, :])
        dk = tail * (nt(v, grad_state) + ks_ref[0:1, :])
        dv = tail * nn(k, grad_state)
        for h in range(width // HEAD):
            mine = lanes == h
            qh, kh, nh = pick(mine, q), pick(mine, k), pick(mine, ng)
            score = nt(qh, k).astype(BF) * keep
            left = jnp.where(mine, ng, pick(lanes == (h ^ 1), terms))
            back = nt(left, jnp.where(mine, v, one)).astype(BF) * keep
            dq = dq + nn(back, kh)
            dk = dk + tn(back, qh)
            dv = dv + tn(score, nh)
        dq_ref[at, :] = (dq * jnp.minimum(q.astype(F32), 1.0)).astype(BF)
        dk_ref[at, :] = dk
        dv_ref[at, :] = dv
        cont = (before == after).astype(F32)
        st_ref[...] = cont * st_ref[...] + pick(block, tn(pick(opened, q), ng))
        ks_ref[...] = cont * ks_ref[...] + jnp.sum(carried * q.astype(F32) * dg, axis=0, keepdims=True)
        return carry

    lax.fori_loop(0, count, step, 0)


def attend_back(last, spot, q, k, v, ng, dg, segc, segr, pack):
    rows, width = q.shape
    count = rows // CHUNK
    call = kernel(
        backward_body, "attend_back",
        (shape(rows, width, BF), shape(rows, width, F32), shape(rows, width, F32)),
        [smem()] * 2 + [vmem()] * 8, 32, 15 * US,
        scratch=[
            pltpu.VMEM((count, width, width), BF),
            pltpu.VMEM((count, 8, width), F32),
            pltpu.VMEM((width, width), F32),
            pltpu.VMEM((8, width), F32),
        ],
    )
    return call(last, spot, q, k, v, ng, dg, segc, segr, pack)


def mix_body(
    pair, tail_ref, dq_ref, dk_ref, dv_ref, k_ref, v_ref, segc_ref, valid_ref, pack_ref, w_ref,
    mixed_ref, a_ref, b_ref
):
    width = k_ref.shape[1]
    block = same_head(width)
    state = spread_heads(pack_ref[0:HEAD, :], width, block).astype(BF)
    sums = pack_ref[HEAD : HEAD + 1, :]
    for i, own, at in pair_slices(pair, a_ref.shape[0]):
        tail = (segc_ref[at, :] == tail_ref[0]).astype(F32)
        k = k_ref[at, :]
        dk = dk_ref[at, :] + tail * (nt(v_ref[at, :], state) + sums)
        dv = dv_ref[at, :] + tail * nn(k, state)
        dq = dq_ref[at, :]
        dk = (valid_ref[at, :] * dk * jnp.minimum(k.astype(F32), 1.0)).astype(BF)
        dv = dv.astype(BF)
        mixed_ref[own, 0:width] = dq
        mixed_ref[own, width : 2 * width] = dk
        mixed_ref[own, 2 * width : 3 * width] = dv
        out = nt(dq, w_ref[0]) + nt(dk, w_ref[1]) + nt(dv, w_ref[2])
        (a_ref, b_ref)[i][...] = out.astype(BF)


def mix(pair, rows, tail, dq, dk, dv, k, v, segc, valid, pack, w):
    width = k.shape[1]
    call = kernel(
        functools.partial(mix_body, pair), "mix",
        (shape(2 * rows, 3 * width, BF),) + (shape(rows, D, BF),) * 2,
        [smem()] + [vmem()] * 9, 16, 4 * US,
    )
    return call(tail, dq, dk, dv, k, v, segc, valid, pack, w)


def feature(values):
    return jnp.where(values > 0, values + 1.0, jnp.exp(jnp.minimum(values, 0.0)))


def bits_of(count):
    return [1 << b for b in range(count.bit_length() - 1)]


def swap(value, axis, bit):
    return lax.ppermute(value, axis, [(i, i ^ bit) for i in range(lax.axis_size(axis))])


def gather_slots(value):
    slots = {0: value}
    for bit in reversed(bits_of(lax.axis_size("feat"))):
        for s in sorted(slots):
            slots[s | bit] = swap(slots[s], "feat", bit)
    return [slots[s] for s in range(len(slots))]


def scatter_slots(parts, after=None):
    parts = {s: [part] for s, part in enumerate(parts)}
    for bit in bits_of(lax.axis_size("feat")):
        for s in sorted(parts, reverse=True):
            if s & bit:
                pieces = parts.pop(s)
                value = pieces[0]
                if len(pieces) > 1:
                    value = functools.reduce(jnp.add, [p.astype(F32) for p in pieces]).astype(BF)
                if after is not None and bit > 1:
                    value = lax.optimization_barrier((value, after))[0]
                parts[s ^ bit].append(swap(value, "feat", bit))
    return parts[0]


def sum_everywhere(value):
    for axis in ("feat", "rows"):
        for bit in bits_of(lax.axis_size(axis)):
            value = value + swap(value, axis, bit)
    return value


def sum_rows(value, order):
    here = lax.axis_index("rows")
    for bit in order:
        half = value.shape[0] // 2
        upper = (here & bit) != 0
        low, high = value[:half], value[half:]
        got = swap(jnp.where(upper, low, high), "rows", bit)
        value = (jnp.where(upper, high, low).astype(F32) + got.astype(F32)).astype(BF)
    for bit in reversed(order):
        upper = (here & bit) != 0
        got = swap(value, "rows", bit)
        value = jnp.concatenate([jnp.where(upper, got, value), jnp.where(upper, value, got)], axis=0)
    return value


def sum_pieces(value, count, order, turned):
    size = value.shape[0] // count
    return jnp.concatenate(
        [
            sum_rows(value[i * size : (i + 1) * size], turned if i % 2 else order)
            for i in range(count)
        ],
        axis=0,
    )


def shifted(pack, hop, groups, reverse):
    if reverse:
        pairs = [(i, i - hop) for i in range(hop, groups)]
    else:
        pairs = [(i, i + hop) for i in range(groups - hop)]
    return lax.ppermute(pack, "rows", pairs)


def gather_carry(pack, crops_at, here, groups, reach, reverse):
    total = jnp.zeros(pack.shape, F32)
    mine = crops_at[here + 1] if reverse else crops_at[here]
    for hop in range(1, reach + 1):
        got = shifted(pack, hop, groups, reverse).astype(F32)
        other = here + hop if reverse else here - hop
        inside = (other < groups) if reverse else (other >= 0)
        at = jnp.clip(other, 0, groups - 1)
        theirs = crops_at[at] if reverse else crops_at[at + 1]
        total = total + jnp.where(inside & (theirs == mine), got, 0.0)
    return total


def on_device(
    pixels,
    qkv_weight,
    out_weight,
    up_weight,
    down_weight,
    norm1_gain,
    norm1_bias,
    norm2_gain,
    norm2_bias,
    crop_lengths,
    crop_offsets,
    pixel_mask,
    out_grad,
):
    local_rows = pixels.shape[0]
    group_rows = pixel_mask.shape[0]
    width = qkv_weight.shape[2]
    crop_count = crop_offsets.shape[0]
    groups = lax.axis_size("rows")
    members = lax.axis_size("feat")
    pairs = members // 2
    here = lax.axis_index("rows")
    member = lax.axis_index("feat")
    reach = min(groups - 1, -(-(CROP_MAX - 1) // group_rows))
    group_start = here * group_rows
    slot_ids = jnp.arange(members, dtype=jnp.int32) ^ member
    in_group = (slot_ids[:, None] * local_rows + jnp.arange(local_rows, dtype=jnp.int32)[None, :]).reshape(-1)
    places = group_start + in_group
    started = crop_offsets[None, :] <= places[:, None]
    crop_ends = crop_offsets + crop_lengths
    segment = jnp.sum(started.astype(jnp.int32), axis=1) - 1
    inside = jnp.sum((started & (places[:, None] < crop_ends[None, :])).astype(jnp.int32), axis=1)
    mask = jnp.concatenate(
        [
            lax.dynamic_slice_in_dim(pixel_mask, (member ^ s) * local_rows, local_rows)
            for s in range(members)
        ]
    )
    pixel_valid = (mask * inside).astype(F32)
    edges = jnp.arange(groups + 1, dtype=jnp.int32) * group_rows - 1
    crops_at = jnp.sum((crop_offsets[None, :] <= edges[:, None]).astype(jnp.int32), axis=1) - 1
    chunks = group_rows // CHUNK
    per = local_rows // CHUNK
    chunk_edges = group_start - 1 + jnp.arange(chunks + 1, dtype=jnp.int32) * CHUNK
    last = jnp.sum((crop_offsets[None, :] <= chunk_edges[:, None]).astype(jnp.int32), axis=1) - 1
    tail = last[-1:]
    order = jnp.arange(chunks, dtype=jnp.int32)
    spot = ((order // per) ^ member) * per + order % per
    segc = segment[:, None]
    segr = segment.reshape(chunks, 1, CHUNK)
    validc = pixel_valid[:, None]
    gain1, bias1, gain2, bias2 = (
        a[None, :] for a in (norm1_gain, norm1_bias, norm2_gain, norm2_bias)
    )
    no_pack = jnp.zeros((PACK, width), F32)

    normed_slots = gather_slots(norm_one(pixels, gain1, bias1))
    late_grad = lax.optimization_barrier((out_grad, normed_slots[members // 2]))[0]
    grad_slots = gather_slots(late_grad)
    made, pack = (), no_pack
    for p in range(pairs):
        *made, pack = project_qkv(
            p, tail, normed_slots[2 * p], normed_slots[2 * p + 1], qkv_weight, validc, segc, pack, made
        )
    q, k, v = made
    carry = gather_carry(pack.astype(BF), crops_at, here, groups, reach, False)
    num, den = attend(last, spot, q, k, v, segc, segr)
    sent = {
        p: project(p, local_rows, last, num, den, q, carry, segc, validc, out_weight)
        for p in reversed(range(pairs))
    }
    parts = [sent[s // 2][3 + s % 2] for s in range(members)]
    middle, normed_two, attended_square = norm_two(pixels, gain2, bias2, scatter_slots(parts))
    two_slots = gather_slots(normed_two)
    hidden = [
        mlp(*two_slots[2 * p : 2 * p + 2], *grad_slots[2 * p : 2 * p + 2], up_weight, down_weight)
        for p in range(pairs)
    ]
    two_parts = scatter_slots([hidden[s // 2][2 + s % 2] for s in range(members)])
    branch_parts = scatter_slots([hidden[s // 2][4 + s % 2] for s in range(members)], two_parts[-1])
    grad_all = jnp.concatenate(grad_slots, axis=0)
    down_grad = tn(jnp.concatenate([h[0] for h in hidden], axis=0), grad_all).astype(BF)
    up_grad = tn(jnp.concatenate(two_slots, axis=0), jnp.concatenate([h[1] for h in hidden], axis=0)).astype(BF)
    middle_grad, middle_low, gain2_grad, bias2_grad = norm_two_back(out_grad, middle, gain2, two_parts)
    middle_slots = gather_slots(middle_low)
    made, grad_pack = (), no_pack
    for p in range(pairs):
        *made, grad_pack = heads_back(
            p, last, middle_slots[2 * p], middle_slots[2 * p + 1], out_weight,
            sent[p][1], sent[p][2], q, segc, grad_pack, made
        )
    ng, dg = made
    grad_carry = gather_carry(grad_pack.astype(BF), crops_at, here, groups, reach, True)
    out_weight_grad = tn(
        jnp.concatenate([sent[p][0] for p in range(pairs)], axis=0), jnp.concatenate(middle_slots, axis=0)
    ).astype(BF)
    dq, dk, dv = attend_back(last, spot, q, k, v, ng, dg, segc, segr, carry)
    mixes = {
        p: mix(p, local_rows, tail, dq, dk, dv, k, v, segc, validc, grad_carry, qkv_weight)
        for p in reversed(range(pairs))
    }
    normed_parts = scatter_slots([mixes[s // 2][1 + s % 2] for s in range(members)])
    mixed_grad = jnp.concatenate([mixes[p][0] for p in range(pairs)], axis=0)
    qkv_grad = tn(mixed_grad, jnp.concatenate(normed_slots, axis=0)).astype(BF)
    output, result_square, branch_square = finish(middle, branch_parts)
    pixels_grad, gain1_grad, bias1_grad = norm_one_back(pixels, middle_grad, gain1, normed_parts)

    bits = bits_of(groups)
    turned = bits[1:] + bits[:1]
    down_grad = lax.psum(down_grad, "rows").astype(F32)
    up_grad = lax.psum(up_grad, "rows").astype(F32)
    out_weight_grad = sum_rows(out_weight_grad, turned).astype(F32)
    qkv_grad = sum_pieces(qkv_grad, 2, bits, turned)
    qkv_grad = jnp.swapaxes(qkv_grad.reshape(3, width, D), 1, 2).astype(F32)

    crop_onehot = (
        segment[:local_rows, None] == jnp.arange(crop_count, dtype=jnp.int32)[None, :]
    ).astype(F32)
    squares = (
        jnp.concatenate(
            [result_square, attended_square, branch_square, jnp.ones((local_rows, 1), F32)], axis=1
        )
        * validc[:local_rows]
    )
    crop_sums = lax.dot_general(
        squares, crop_onehot, (((0,), (0,)), ((), ())), precision=precise, preferred_element_type=F32
    )
    sums = jnp.concatenate(
        [gain1_grad[0], bias1_grad[0], gain2_grad[0], bias2_grad[0], crop_sums.reshape(-1)]
    )
    sums = sum_everywhere(sums)
    gain1_grad, bias1_grad, gain2_grad, bias2_grad = sums[: 4 * D].reshape(4, D)
    crop_sums = sums[4 * D :].reshape(4, crop_count)
    crop_rms = jnp.sqrt(crop_sums[:3] / (D * jnp.maximum(crop_sums[3], 1.0))[None, :])
    return (
        output,
        pixels_grad,
        qkv_grad,
        out_weight_grad,
        up_grad,
        down_grad,
        gain1_grad,
        bias1_grad,
        gain2_grad,
        bias2_grad,
        crop_rms,
    )


def solution(mesh):
    split = P(("rows", "feat"), None)
    qkv, rows_feat, cols_feat = P(None, None, "feat"), P("feat", None), P(None, "feat")
    in_specs = (
        (split, qkv, rows_feat, cols_feat, rows_feat) + (P(),) * 6 + (P("rows"), split)
    )
    out_specs = (split, split, qkv, rows_feat, cols_feat, rows_feat) + (P(),) * 5
    return jax.shard_map(
        on_device, mesh=mesh, in_specs=in_specs, out_specs=out_specs, check_vma=False
    )
```

```python
import functools

import jax
import jax.numpy as jnp
from jax import lax
from jax.experimental import pallas as pl
from jax.experimental.pallas import tpu as pltpu
from jax.sharding import PartitionSpec as P

D = 1024
HEAD = 64
CHUNK = 384
CROP_MAX = 3072
PACK = HEAD + 16

BF = jnp.bfloat16
F32 = jnp.float32
precise = lax.Precision.HIGHEST


def nn(a, b):
    return lax.dot_general(a, b, (((1,), (0,)), ((), ())), preferred_element_type=F32)


def nt(a, b):
    return lax.dot_general(a, b, (((1,), (1,)), ((), ())), preferred_element_type=F32)


def tn(a, b):
    return lax.dot_general(a, b, (((0,), (0,)), ((), ())), preferred_element_type=F32)


def same_head(width):
    row = lax.broadcasted_iota(jnp.int32, (width, width), 0) // HEAD
    col = lax.broadcasted_iota(jnp.int32, (width, width), 1) // HEAD
    return row == col


def lane_head(rows, width):
    return lax.broadcasted_iota(jnp.int32, (rows, width), 1) // HEAD


def causal(rows):
    row = lax.broadcasted_iota(jnp.int32, (rows, rows), 0)
    col = lax.broadcasted_iota(jnp.int32, (rows, rows), 1)
    return row >= col


def fold_heads(full, width):
    out = full[0:HEAD]
    for h in range(1, width // HEAD):
        out = out + full[h * HEAD : (h + 1) * HEAD]
    return out


def spread_heads(part, width, block):
    tall = jnp.concatenate([part] * (width // HEAD), axis=0)
    return jnp.where(block, tall, jnp.zeros_like(tall))


def pick(mask, value):
    return jnp.where(mask, value, jnp.zeros_like(value))


def vmem():
    return pl.BlockSpec(memory_space=pltpu.VMEM)


def smem():
    return pl.BlockSpec(memory_space=pltpu.SMEM)


def shape(rows, cols, kind):
    return jax.ShapeDtypeStruct((rows, cols), kind)


ROW_TILE = 192


def tiles(rows):
    return [slice(i, i + ROW_TILE) for i in range(0, rows, ROW_TILE)]


def kernel(body, name, out_shape, in_specs, megabytes, scratch=(), aliases=None, tokens=()):
    outs = vmem() if not isinstance(out_shape, tuple) else (vmem(),) * len(out_shape)
    count = len(in_specs)

    def run(*refs):
        body(*refs[:count], *refs[count + len(tokens) :])

    call = pl.pallas_call(
        run,
        out_shape=out_shape,
        in_specs=in_specs + [pl.BlockSpec(memory_space=pl.ANY)] * len(tokens),
        out_specs=outs,
        scratch_shapes=list(scratch),
        input_output_aliases=aliases or {},
        compiler_params=pltpu.CompilerParams(vmem_limit_bytes=megabytes << 20),
        name=name,
    )
    return lambda *args: call(*args, *tokens)


def normal(values):
    centre = jnp.mean(values, axis=-1, keepdims=True)
    moved = values - centre
    scale = lax.rsqrt(jnp.mean(moved * moved, axis=-1, keepdims=True) + 1e-05)
    return moved * scale, scale


def normal_back(grad, gain, xhat, scale):
    g = grad * gain
    return scale * (
        g - jnp.mean(g, axis=-1, keepdims=True) - xhat * jnp.mean(g * xhat, axis=-1, keepdims=True)
    )


def total(refs):
    value = refs[0][...].astype(F32)
    for ref in refs[1:]:
        value = value + ref[...].astype(F32)
    return value


def norm_body(x_ref, gain_ref, bias_ref, out_ref):
    for at in tiles(x_ref.shape[0]):
        xhat, _ = normal(x_ref[at, :].astype(F32))
        out_ref[at, :] = (xhat * gain_ref[...] + bias_ref[...]).astype(BF)


def norm_one(x, gain, bias):
    call = kernel(norm_body, "norm_one", shape(x.shape[0], D, BF), [vmem()] * 3, 8)
    return call(x, gain, bias)


def total(refs, at):
    value = refs[0][at, :].astype(F32)
    for ref in refs[1:]:
        value = value + ref[at, :].astype(F32)
    return value


def middle_body(*refs):
    x_ref, gain_ref, bias_ref = refs[:3]
    parts = refs[3:-3]
    middle_ref, out_ref, square_ref = refs[-3:]
    for at in tiles(x_ref.shape[0]):
        attended = total(parts, at)
        middle = x_ref[at, :].astype(F32) + attended
        middle_ref[at, :] = middle
        xhat, _ = normal(middle)
        out_ref[at, :] = (xhat * gain_ref[...] + bias_ref[...]).astype(BF)
        square_ref[at, :] = jnp.sum(attended * attended, axis=-1, keepdims=True)


def norm_two(x, gain, bias, parts):
    rows = x.shape[0]
    call = kernel(
        middle_body, "norm_two", (shape(rows, D, F32), shape(rows, D, BF), shape(rows, 1, F32)),
        [vmem()] * (3 + len(parts)), 12,
    )
    return call(x, gain, bias, *parts)


def middle_back_body(*refs):
    grad_ref, middle_ref, gain_ref = refs[:3]
    parts = refs[3:-4]
    wide_ref, low_ref, gain_grad_ref, bias_grad_ref = refs[-4:]
    gain_grad = bias_grad = jnp.zeros(gain_ref.shape, F32)
    for at in tiles(grad_ref.shape[0]):
        grad = total(parts, at)
        xhat, scale = normal(middle_ref[at, :])
        gain_grad = gain_grad + jnp.sum(grad * xhat, axis=0, keepdims=True)
        bias_grad = bias_grad + jnp.sum(grad, axis=0, keepdims=True)
        out = grad_ref[at, :].astype(F32) + normal_back(grad, gain_ref[...], xhat, scale)
        wide_ref[at, :] = out
        low_ref[at, :] = out.astype(BF)
    gain_grad_ref[...] = gain_grad
    bias_grad_ref[...] = bias_grad


def norm_two_back(grad, middle, gain, parts, tokens):
    rows = grad.shape[0]
    call = kernel(
        middle_back_body, "norm_two_back",
        (shape(rows, D, F32), shape(rows, D, BF), shape(1, D, F32), shape(1, D, F32)),
        [vmem()] * (3 + len(parts)), 16, tokens=tokens,
    )
    return call(grad, middle, gain, *parts)


def pixels_back_body(*refs):
    x_ref, wide_ref, gain_ref = refs[:3]
    parts = refs[3:-3]
    out_ref, gain_grad_ref, bias_grad_ref = refs[-3:]
    gain_grad = bias_grad = jnp.zeros(gain_ref.shape, F32)
    for at in tiles(x_ref.shape[0]):
        grad = total(parts, at)
        xhat, scale = normal(x_ref[at, :].astype(F32))
        gain_grad = gain_grad + jnp.sum(grad * xhat, axis=0, keepdims=True)
        bias_grad = bias_grad + jnp.sum(grad, axis=0, keepdims=True)
        out_ref[at, :] = (wide_ref[at, :] + normal_back(grad, gain_ref[...], xhat, scale)).astype(BF)
    gain_grad_ref[...] = gain_grad
    bias_grad_ref[...] = bias_grad


def norm_one_back(x, wide, gain, parts):
    rows = x.shape[0]
    call = kernel(
        pixels_back_body, "norm_one_back", (shape(rows, D, BF), shape(1, D, F32), shape(1, D, F32)),
        [vmem()] * (3 + len(parts)), 16,
    )
    return call(x, wide, gain, *parts)


def result_body(*refs):
    middle_ref = refs[0]
    parts = refs[1:-3]
    out_ref, result_square_ref, branch_square_ref = refs[-3:]
    for at in tiles(middle_ref.shape[0]):
        branch = total(parts, at)
        result = middle_ref[at, :] + branch
        out_ref[at, :] = result.astype(BF)
        result_square_ref[at, :] = jnp.sum(result * result, axis=-1, keepdims=True)
        branch_square_ref[at, :] = jnp.sum(branch * branch, axis=-1, keepdims=True)


def finish(middle, parts, tokens):
    rows = middle.shape[0]
    call = kernel(
        result_body, "finish", (shape(rows, D, BF), shape(rows, 1, F32), shape(rows, 1, F32)),
        [vmem()] * (1 + len(parts)), 12, tokens=tokens,
    )
    return call(middle, *parts)


def pair_slices(pair, rows):
    for i in range(2):
        yield i, slice(i * rows, (i + 1) * rows), slice((2 * pair + i) * rows, (2 * pair + i + 1) * rows)


def qkv_body(pair, tail_ref, xa_ref, xb_ref, w_ref, valid_ref, seg_ref, was_ref, *rest):
    q_ref, k_ref, v_ref, pack_ref = rest[-4:]
    width = q_ref.shape[1]
    block = same_head(width)
    state, sums = was_ref[0:HEAD, :], was_ref[HEAD:PACK, :]
    for i, _, at in pair_slices(pair, xa_ref.shape[0]):
        x = (xa_ref, xb_ref)[i][...]
        q_ref[at, :] = feature(nn(x, w_ref[0])).astype(BF)
        k = (feature(nn(x, w_ref[1])) * valid_ref[at, :]).astype(BF)
        v = nn(x, w_ref[2]).astype(BF)
        k_ref[at, :] = k
        v_ref[at, :] = v
        kept = pick(seg_ref[at, :] == tail_ref[0], k)
        state = state + fold_heads(pick(block, tn(kept, v)), width)
        sums = sums + jnp.sum(kept.astype(F32), axis=0, keepdims=True)
    pack_ref[0:HEAD, :] = state
    pack_ref[HEAD:PACK, :] = sums


def project_qkv(pair, tail, xa, xb, w, valid, seg, was, made):
    width, whole = w.shape[2], valid.shape[0]
    call = kernel(
        functools.partial(qkv_body, pair), "project_qkv",
        (shape(whole, width, BF),) * 3 + (shape(PACK, width, F32),),
        [smem()] + [vmem()] * (6 + len(made)), 16,
        aliases={7 + i: i for i in range(len(made))},
    )
    return call(tail, xa, xb, w, valid, seg, was, *made)


def swap_heads(x):
    return jnp.concatenate(
        [pltpu.roll(x[:, i : i + 2 * HEAD], HEAD, 1) for i in range(0, x.shape[1], 2 * HEAD)], axis=1
    )


def forward_body(
    last_ref, spot_ref, q_ref, k_ref, v_ref, segc_ref, segr_ref, num_ref, den_ref, st_ref, ks_ref
):
    rows, width = q_ref.shape
    size = CHUNK
    block = same_head(width)
    ones_block = block.astype(BF)
    lanes = lane_head(size, width)
    even = (lanes % 2) == 0
    lower = causal(size)
    st_ref[...] = jnp.zeros_like(st_ref)
    ks_ref[...] = jnp.zeros_like(ks_ref)

    def step(c, carry):
        spot = spot_ref[c]
        at = pl.ds(pl.multiple_of(spot * size, size), size)
        q, k, v = q_ref[at, :], k_ref[at, :], v_ref[at, :]
        seg = segc_ref[at, :]
        keep = (lower & (seg == segr_ref[spot])).astype(BF)
        before, after = last_ref[c], last_ref[c + 1]
        carried = (seg == before).astype(F32)
        sums = [jnp.zeros((size, width), F32)] * 2
        for h in range(width // HEAD):
            mine = lanes == h
            score = nt(pick(mine, q), k).astype(BF) * keep
            both = jnp.where(mine, v, (lanes == (h ^ 1)).astype(BF))
            sums[h % 2] = sums[h % 2] + nn(score, both)
        num = jnp.where(even, sums[0], sums[1])
        den = swap_heads(jnp.where(even, sums[1], sums[0]))
        num_ref[at, :] = num + carried * nn(q, st_ref[...].astype(BF))
        den_ref[at, :] = den + carried * nn((q.astype(F32) * ks_ref[0:1, :]).astype(BF), ones_block)
        kept = pick(seg == after, k)
        cont = (before == after).astype(F32)
        st_ref[...] = cont * st_ref[...] + pick(block, tn(kept, v))
        ks_ref[...] = cont * ks_ref[...] + jnp.sum(kept.astype(F32), axis=0, keepdims=True)
        return carry

    lax.fori_loop(0, rows // size, step, 0)


def attend(last, spot, q, k, v, segc, segr):
    rows, width = q.shape
    call = kernel(
        forward_body, "attend", (shape(rows, width, F32),) * 2, [smem()] * 2 + [vmem()] * 5, 24,
        scratch=[pltpu.VMEM((width, width), F32), pltpu.VMEM((8, width), F32)],
    )
    return call(last, spot, q, k, v, segc, segr)


def project_body(
    pair, first_ref, num_ref, den_ref, q_ref, pack_ref, segc_ref, valid_ref, w_ref,
    heads_ref, wide_ref, rinv_ref, a_ref, b_ref
):
    width = q_ref.shape[1]
    block = same_head(width)
    state = spread_heads(pack_ref[0:HEAD, :], width, block).astype(BF)
    sums = pack_ref[HEAD : HEAD + 1, :]
    for i, own, at in pair_slices(pair, a_ref.shape[0]):
        q = q_ref[at, :]
        opening = (segc_ref[at, :] == first_ref[0]).astype(F32)
        valid = valid_ref[at, :]
        num = num_ref[at, :] + opening * nn(q, state)
        den = den_ref[at, :] + opening * nn((q.astype(F32) * sums).astype(BF), block.astype(BF))
        rinv = valid / (den + 1e-06 + 1.0 - valid)
        wide = num * rinv
        heads = wide.astype(BF)
        heads_ref[own, :] = heads
        wide_ref[own, :] = wide
        rinv_ref[own, :] = rinv
        (a_ref, b_ref)[i][...] = nn(heads, w_ref[...]).astype(BF)


def project(pair, rows, last, num, den, q, pack, segc, valid, w, tokens):
    width = q.shape[1]
    call = kernel(
        functools.partial(project_body, pair), "project",
        (shape(2 * rows, width, BF), shape(2 * rows, width, F32), shape(2 * rows, width, F32))
        + (shape(rows, D, BF),) * 2,
        [smem()] + [vmem()] * 7, 12, tokens=tokens,
    )
    return call(last, num, den, q, pack, segc, valid, w)


def mlp_body(
    xa_ref, xb_ref, ga_ref, gb_ref, up_ref, down_ref, act_ref, hid_ref, na_ref, nb_ref, ba_ref, bb_ref
):
    root = 0.7978845608028654
    tile = min(512, up_ref.shape[1])
    for i, own, _ in pair_slices(0, xa_ref.shape[0]):
        x, g = (xa_ref, xb_ref)[i][...], (ga_ref, gb_ref)[i][...]
        for j in range(0, up_ref.shape[1], tile):
            cols = slice(j, j + tile)
            h = nn(x, up_ref[:, cols])
            grad = nt(g, down_ref[cols, :])
            square = h * h
            t = jnp.tanh(root * h * (1.0 + 0.044715 * square))
            plus = 0.5 * (1.0 + t)
            slope = plus + 0.5 * h * (1.0 - t * t) * (root + (3.0 * 0.044715 * root) * square)
            act_ref[own, cols] = (h * plus).astype(BF)
            hid_ref[own, cols] = (grad * slope).astype(BF)
        (na_ref, nb_ref)[i][...] = nt(hid_ref[own, :], up_ref[...]).astype(BF)
        (ba_ref, bb_ref)[i][...] = nn(act_ref[own, :], down_ref[...]).astype(BF)


def mlp(xa, xb, ga, gb, up, down):
    rows, hidden = xa.shape[0], up.shape[1]
    call = kernel(
        mlp_body, "mlp", (shape(2 * rows, hidden, BF),) * 2 + (shape(rows, D, BF),) * 4,
        [vmem()] * 6, 32,
    )
    return call(xa, xb, ga, gb, up, down)


def heads_back_body(
    pair, first_ref, ga_ref, gb_ref, w_ref, wide_ref, rinv_ref, q_ref, segc_ref, was_ref, *rest
):
    ng_ref, dg_ref, pack_ref = rest[-3:]
    width = q_ref.shape[1]
    block = same_head(width)
    ones_block = block.astype(BF)
    state, sums = was_ref[0:HEAD, :], was_ref[HEAD:PACK, :]
    for i, own, at in pair_slices(pair, ga_ref.shape[0]):
        hg = nt((ga_ref, gb_ref)[i][...], w_ref[...])
        rinv = rinv_ref[own, :]
        ng = (hg * rinv).astype(BF)
        prod = hg * wide_ref[own, :]
        high = prod.astype(BF)
        low = (prod - high.astype(F32)).astype(BF)
        dg = -(nn(high, ones_block) + nn(low, ones_block)) * rinv
        ng_ref[at, :] = ng
        dg_ref[at, :] = dg
        opened = pick(segc_ref[at, :] == first_ref[0], q_ref[at, :])
        state = state + fold_heads(pick(block, tn(opened, ng)), width)
        sums = sums + jnp.sum(opened.astype(F32) * dg, axis=0, keepdims=True)
    pack_ref[0:HEAD, :] = state
    pack_ref[HEAD:PACK, :] = sums


def heads_back(pair, last, ga, gb, w, wide, rinv, q, segc, was, made):
    whole, width = q.shape
    call = kernel(
        functools.partial(heads_back_body, pair), "heads_back",
        (shape(whole, width, BF), shape(whole, width, F32), shape(PACK, width, F32)),
        [smem()] + [vmem()] * (8 + len(made)), 16,
        aliases={9 + i: i for i in range(len(made))},
    )
    return call(last, ga, gb, w, wide, rinv, q, segc, was, *made)


def backward_body(
    last_ref, spot_ref, q_ref, k_ref, v_ref, ng_ref, dg_ref, segc_ref, segr_ref, pack_ref,
    dq_ref, dk_ref, dv_ref, all_ref, sums_ref, st_ref, ks_ref
):
    rows, width = q_ref.shape
    size = CHUNK
    count = rows // size
    block = same_head(width)
    lanes = lane_head(size, width)
    half = (lax.broadcasted_iota(jnp.int32, (size, width), 1) % HEAD) < HEAD // 2
    lower = causal(size)
    st_ref[...] = spread_heads(pack_ref[0:HEAD, :], width, block)
    ks_ref[...] = jnp.broadcast_to(pack_ref[HEAD : HEAD + 1, :], ks_ref.shape)

    def collect(c, carry):
        at = pl.ds(pl.multiple_of(spot_ref[c] * size, size), size)
        all_ref[c] = st_ref[...].astype(BF)
        sums_ref[c] = ks_ref[...]
        before, after = last_ref[c], last_ref[c + 1]
        kept = pick(segc_ref[at, :] == after, k_ref[at, :])
        cont = (before == after).astype(F32)
        st_ref[...] = cont * st_ref[...] + pick(block, tn(kept, v_ref[at, :]))
        ks_ref[...] = cont * ks_ref[...] + jnp.sum(kept.astype(F32), axis=0, keepdims=True)
        return carry

    lax.fori_loop(0, count, collect, 0)
    st_ref[...] = jnp.zeros_like(st_ref)
    ks_ref[...] = jnp.zeros_like(ks_ref)

    def step(i, carry):
        c = count - 1 - i
        spot = spot_ref[c]
        at = pl.ds(pl.multiple_of(spot * size, size), size)
        q, k, v, ng, dg = q_ref[at, :], k_ref[at, :], v_ref[at, :], ng_ref[at, :], dg_ref[at, :]
        seg = segc_ref[at, :]
        keep = (lower & (seg == segr_ref[spot])).astype(BF)
        before, after = last_ref[c], last_ref[c + 1]
        opened = seg == before
        carried = opened.astype(F32)
        tail = (seg == after).astype(F32)
        grad_state = st_ref[...].astype(BF)
        moved = swap_heads(dg)
        high = moved.astype(BF)
        low = (moved - high.astype(F32)).astype(BF)
        terms = jnp.where(half, high, low) * jnp.asarray(2.0 / HEAD, BF)
        one = jnp.ones((), BF)
        dq = carried * (nt(ng, all_ref[c]) + dg * sums_ref[c][0:1, :])
        dk = tail * (nt(v, grad_state) + ks_ref[0:1, :])
        dv = tail * nn(k, grad_state)
        for h in range(width // HEAD):
            mine = lanes == h
            qh, kh, nh = pick(mine, q), pick(mine, k), pick(mine, ng)
            score = nt(qh, k).astype(BF) * keep
            left = jnp.where(mine, ng, pick(lanes == (h ^ 1), terms))
            back = nt(left, jnp.where(mine, v, one)).astype(BF) * keep
            dq = dq + nn(back, kh)
            dk = dk + tn(back, qh)
            dv = dv + tn(score, nh)
        dq_ref[at, :] = (dq * jnp.minimum(q.astype(F32), 1.0)).astype(BF)
        dk_ref[at, :] = dk
        dv_ref[at, :] = dv
        cont = (before == after).astype(F32)
        st_ref[...] = cont * st_ref[...] + pick(block, tn(pick(opened, q), ng))
        ks_ref[...] = cont * ks_ref[...] + jnp.sum(carried * q.astype(F32) * dg, axis=0, keepdims=True)
        return carry

    lax.fori_loop(0, count, step, 0)


def attend_back(last, spot, q, k, v, ng, dg, segc, segr, pack):
    rows, width = q.shape
    count = rows // CHUNK
    call = kernel(
        backward_body, "attend_back",
        (shape(rows, width, BF), shape(rows, width, F32), shape(rows, width, F32)),
        [smem()] * 2 + [vmem()] * 8, 32,
        scratch=[
            pltpu.VMEM((count, width, width), BF),
            pltpu.VMEM((count, 8, width), F32),
            pltpu.VMEM((width, width), F32),
            pltpu.VMEM((8, width), F32),
        ],
    )
    return call(last, spot, q, k, v, ng, dg, segc, segr, pack)


def mix_body(
    pair, tail_ref, dq_ref, dk_ref, dv_ref, k_ref, v_ref, segc_ref, valid_ref, pack_ref, w_ref,
    mixed_ref, a_ref, b_ref
):
    width = k_ref.shape[1]
    block = same_head(width)
    state = spread_heads(pack_ref[0:HEAD, :], width, block).astype(BF)
    sums = pack_ref[HEAD : HEAD + 1, :]
    for i, own, at in pair_slices(pair, a_ref.shape[0]):
        tail = (segc_ref[at, :] == tail_ref[0]).astype(F32)
        k = k_ref[at, :]
        dk = dk_ref[at, :] + tail * (nt(v_ref[at, :], state) + sums)
        dv = dv_ref[at, :] + tail * nn(k, state)
        dq = dq_ref[at, :]
        dk = (valid_ref[at, :] * dk * jnp.minimum(k.astype(F32), 1.0)).astype(BF)
        dv = dv.astype(BF)
        mixed_ref[own, 0:width] = dq
        mixed_ref[own, width : 2 * width] = dk
        mixed_ref[own, 2 * width : 3 * width] = dv
        out = nt(dq, w_ref[0]) + nt(dk, w_ref[1]) + nt(dv, w_ref[2])
        (a_ref, b_ref)[i][...] = out.astype(BF)


def mix(pair, rows, tail, dq, dk, dv, k, v, segc, valid, pack, w):
    width = k.shape[1]
    call = kernel(
        functools.partial(mix_body, pair), "mix",
        (shape(2 * rows, 3 * width, BF),) + (shape(rows, D, BF),) * 2,
        [smem()] + [vmem()] * 9, 16,
    )
    return call(tail, dq, dk, dv, k, v, segc, valid, pack, w)


def feature(values):
    return jnp.where(values > 0, values + 1.0, jnp.exp(jnp.minimum(values, 0.0)))


def bits_of(count):
    return [1 << b for b in range(count.bit_length() - 1)]


def swap(value, axis, bit):
    return lax.ppermute(value, axis, [(i, i ^ bit) for i in range(lax.axis_size(axis))])


def after(value, *tokens):
    return lax.optimization_barrier((value, *tokens))[0] if tokens else value


def gather_begin(value):
    slots = {0: value}
    for bit in reversed(bits_of(lax.axis_size("feat"))[1:]):
        for s in sorted(slots):
            slots[s | bit] = swap(slots[s], "feat", bit)
    slots[1] = swap(value, "feat", 1)
    return slots


def gather_end(slots, *tokens):
    for s in range(2, lax.axis_size("feat"), 2):
        slots[s + 1] = swap(after(slots[s], *tokens), "feat", 1)
    return [slots[s] for s in range(len(slots))]


def scatter_slots(parts, *tokens):
    parts = {s: [part] for s, part in enumerate(parts)}
    for bit in bits_of(lax.axis_size("feat")):
        for s in sorted(parts, reverse=True):
            if s & bit:
                pieces = parts.pop(s)
                value = pieces[0]
                if len(pieces) > 1:
                    value = functools.reduce(jnp.add, [p.astype(F32) for p in pieces]).astype(BF)
                if bit > 1:
                    value = after(value, *tokens)
                parts[s ^ bit].append(swap(value, "feat", bit))
    return parts[0]


def sum_everywhere(value):
    for axis in ("feat", "rows"):
        for bit in bits_of(lax.axis_size(axis)):
            value = value + swap(value, axis, bit)
    return value


def sum_rows(value, order):
    here = lax.axis_index("rows")
    for bit in order:
        half = value.shape[0] // 2
        upper = (here & bit) != 0
        low, high = value[:half], value[half:]
        got = swap(jnp.where(upper, low, high), "rows", bit)
        value = (jnp.where(upper, high, low).astype(F32) + got.astype(F32)).astype(BF)
    for bit in reversed(order):
        upper = (here & bit) != 0
        got = swap(value, "rows", bit)
        value = jnp.concatenate([jnp.where(upper, got, value), jnp.where(upper, value, got)], axis=0)
    return value


def sum_pieces(value, count, order, turned):
    size = value.shape[0] // count
    return jnp.concatenate(
        [
            sum_rows(value[i * size : (i + 1) * size], turned if i % 2 else order)
            for i in range(count)
        ],
        axis=0,
    )


def shifted(pack, hop, groups, reverse):
    if reverse:
        pairs = [(i, i - hop) for i in range(hop, groups)]
    else:
        pairs = [(i, i + hop) for i in range(groups - hop)]
    return lax.ppermute(pack, "rows", pairs)


def gather_carry(pack, crops_at, here, groups, reach, reverse):
    total = jnp.zeros(pack.shape, F32)
    mine = crops_at[here + 1] if reverse else crops_at[here]
    for hop in range(1, reach + 1):
        got = shifted(pack, hop, groups, reverse).astype(F32)
        other = here + hop if reverse else here - hop
        inside = (other < groups) if reverse else (other >= 0)
        at = jnp.clip(other, 0, groups - 1)
        theirs = crops_at[at] if reverse else crops_at[at + 1]
        total = total + jnp.where(inside & (theirs == mine), got, 0.0)
    return total


def on_device(
    pixels,
    qkv_weight,
    out_weight,
    up_weight,
    down_weight,
    norm1_gain,
    norm1_bias,
    norm2_gain,
    norm2_bias,
    crop_lengths,
    crop_offsets,
    pixel_mask,
    out_grad,
):
    local_rows = pixels.shape[0]
    group_rows = pixel_mask.shape[0]
    width = qkv_weight.shape[2]
    crop_count = crop_offsets.shape[0]
    groups = lax.axis_size("rows")
    members = lax.axis_size("feat")
    pairs = members // 2
    here = lax.axis_index("rows")
    member = lax.axis_index("feat")
    reach = min(groups - 1, -(-(CROP_MAX - 1) // group_rows))
    group_start = here * group_rows
    slot_ids = jnp.arange(members, dtype=jnp.int32) ^ member
    in_group = (slot_ids[:, None] * local_rows + jnp.arange(local_rows, dtype=jnp.int32)[None, :]).reshape(-1)
    places = group_start + in_group
    started = crop_offsets[None, :] <= places[:, None]
    crop_ends = crop_offsets + crop_lengths
    segment = jnp.sum(started.astype(jnp.int32), axis=1) - 1
    inside = jnp.sum((started & (places[:, None] < crop_ends[None, :])).astype(jnp.int32), axis=1)
    mask = jnp.concatenate(
        [
            lax.dynamic_slice_in_dim(pixel_mask, (member ^ s) * local_rows, local_rows)
            for s in range(members)
        ]
    )
    pixel_valid = (mask * inside).astype(F32)
    edges = jnp.arange(groups + 1, dtype=jnp.int32) * group_rows - 1
    crops_at = jnp.sum((crop_offsets[None, :] <= edges[:, None]).astype(jnp.int32), axis=1) - 1
    chunks = group_rows // CHUNK
    per = local_rows // CHUNK
    chunk_edges = group_start - 1 + jnp.arange(chunks + 1, dtype=jnp.int32) * CHUNK
    last = jnp.sum((crop_offsets[None, :] <= chunk_edges[:, None]).astype(jnp.int32), axis=1) - 1
    tail = last[-1:]
    order = jnp.arange(chunks, dtype=jnp.int32)
    spot = ((order // per) ^ member) * per + order % per
    segc = segment[:, None]
    segr = segment.reshape(chunks, 1, CHUNK)
    validc = pixel_valid[:, None]
    gain1, bias1, gain2, bias2 = (
        a[None, :] for a in (norm1_gain, norm1_bias, norm2_gain, norm2_bias)
    )
    no_pack = jnp.zeros((PACK, width), F32)

    normed_slots = gather_begin(norm_one(pixels, gain1, bias1))
    grad_slots = gather_begin(after(out_grad, normed_slots[members // 2]))
    *made, pack = project_qkv(0, tail, normed_slots[0], normed_slots[1], qkv_weight, validc, segc, no_pack, ())
    normed_slots = gather_end(normed_slots, pack)
    for p in range(1, pairs):
        *made, pack = project_qkv(
            p, tail, normed_slots[2 * p], normed_slots[2 * p + 1], qkv_weight, validc, segc, pack, made
        )
    q, k, v = made
    carry = gather_carry(pack.astype(BF), crops_at, here, groups, reach, False)
    num, den = attend(last, spot, q, k, v, segc, segr)
    grad_slots = gather_end(grad_slots, num)
    sent = {
        p: project(
            p, local_rows, last, num, den, q, carry, segc, validc, out_weight, [grad_slots[members // 2]]
        )
        for p in reversed(range(pairs))
    }
    parts = [sent[s // 2][3 + s % 2] for s in range(members)]
    middle, normed_two, attended_square = norm_two(pixels, gain2, bias2, scatter_slots(parts))
    two_slots = gather_begin(normed_two)
    hidden = [mlp(two_slots[0], two_slots[1], grad_slots[0], grad_slots[1], up_weight, down_weight)]
    two_slots = gather_end(two_slots, hidden[0][0])
    for p in range(1, pairs):
        hidden.append(mlp(*two_slots[2 * p : 2 * p + 2], *grad_slots[2 * p : 2 * p + 2], up_weight, down_weight))
    two_parts = scatter_slots([hidden[s // 2][2 + s % 2] for s in range(members)])
    down_grad = tn(
        jnp.concatenate([h[0] for h in hidden], axis=0), jnp.concatenate(grad_slots, axis=0)
    ).astype(BF)
    up_grad = tn(
        jnp.concatenate(two_slots, axis=0), jnp.concatenate([h[1] for h in hidden], axis=0)
    ).astype(BF)
    middle_grad, middle_low, gain2_grad, bias2_grad = norm_two_back(
        out_grad, middle, gain2, two_parts, [down_grad, up_grad]
    )
    middle_slots = gather_begin(middle_low)
    *made, grad_pack = heads_back(
        0, last, middle_slots[0], middle_slots[1], out_weight, sent[0][1], sent[0][2], q, segc, no_pack, ()
    )
    branch_parts = scatter_slots(
        [hidden[s // 2][4 + s % 2] for s in range(members)], middle_slots[members // 2]
    )
    middle_slots = gather_end(middle_slots, grad_pack)
    for p in range(1, pairs):
        *made, grad_pack = heads_back(
            p, last, middle_slots[2 * p], middle_slots[2 * p + 1], out_weight,
            sent[p][1], sent[p][2], q, segc, grad_pack, made
        )
    ng, dg = made
    grad_carry = gather_carry(grad_pack.astype(BF), crops_at, here, groups, reach, True)
    out_weight_grad = tn(
        jnp.concatenate([sent[p][0] for p in range(pairs)], axis=0), jnp.concatenate(middle_slots, axis=0)
    ).astype(BF)
    dq, dk, dv = attend_back(last, spot, q, k, v, ng, dg, segc, segr, carry)
    mixes = {
        p: mix(p, local_rows, tail, dq, dk, dv, k, v, segc, validc, grad_carry, qkv_weight)
        for p in reversed(range(pairs))
    }
    normed_parts = scatter_slots([mixes[s // 2][1 + s % 2] for s in range(members)])
    mixed_grad = jnp.concatenate([mixes[p][0] for p in range(pairs)], axis=0)
    qkv_grad = tn(mixed_grad, jnp.concatenate(normed_slots, axis=0)).astype(BF)
    output, result_square, branch_square = finish(middle, branch_parts, [dq])
    pixels_grad, gain1_grad, bias1_grad = norm_one_back(pixels, middle_grad, gain1, normed_parts)

    bits = bits_of(groups)
    turned = bits[1:] + bits[:1]
    down_grad = lax.psum(down_grad, "rows").astype(F32)
    up_grad = lax.psum(up_grad, "rows").astype(F32)
    out_weight_grad = sum_rows(out_weight_grad, turned).astype(F32)
    qkv_grad = sum_pieces(qkv_grad, 2, bits, turned)
    qkv_grad = jnp.swapaxes(qkv_grad.reshape(3, width, D), 1, 2).astype(F32)

    crop_onehot = (
        segment[:local_rows, None] == jnp.arange(crop_count, dtype=jnp.int32)[None, :]
    ).astype(F32)
    squares = (
        jnp.concatenate(
            [result_square, attended_square, branch_square, jnp.ones((local_rows, 1), F32)], axis=1
        )
        * validc[:local_rows]
    )
    crop_sums = lax.dot_general(
        squares, crop_onehot, (((0,), (0,)), ((), ())), precision=precise, preferred_element_type=F32
    )
    sums = jnp.concatenate(
        [gain1_grad[0], bias1_grad[0], gain2_grad[0], bias2_grad[0], crop_sums.reshape(-1)]
    )
    sums = sum_everywhere(sums)
    gain1_grad, bias1_grad, gain2_grad, bias2_grad = sums[: 4 * D].reshape(4, D)
    crop_sums = sums[4 * D :].reshape(4, crop_count)
    crop_rms = jnp.sqrt(crop_sums[:3] / (D * jnp.maximum(crop_sums[3], 1.0))[None, :])
    return (
        output,
        pixels_grad,
        qkv_grad,
        out_weight_grad,
        up_grad,
        down_grad,
        gain1_grad,
        bias1_grad,
        gain2_grad,
        bias2_grad,
        crop_rms,
    )


def solution(mesh):
    split = P(("rows", "feat"), None)
    qkv, rows_feat, cols_feat = P(None, None, "feat"), P("feat", None), P(None, "feat")
    in_specs = (
        (split, qkv, rows_feat, cols_feat, rows_feat) + (P(),) * 6 + (P("rows"), split)
    )
    out_specs = (split, split, qkv, rows_feat, cols_feat, rows_feat) + (P(),) * 5
    return jax.shard_map(
        on_device, mesh=mesh, in_specs=in_specs, out_specs=out_specs, check_vma=False
    )
```

```python
import functools

import jax
import jax.numpy as jnp
from jax import lax
from jax.experimental import pallas as pl
from jax.experimental.pallas import tpu as pltpu
from jax.sharding import PartitionSpec as P

D = 1024
HEAD = 64
CHUNK = 384
CROP_MAX = 3072
PACK = HEAD + 16

BF = jnp.bfloat16
F32 = jnp.float32
precise = lax.Precision.HIGHEST


def nn(a, b):
    return lax.dot_general(a, b, (((1,), (0,)), ((), ())), preferred_element_type=F32)


def nt(a, b):
    return lax.dot_general(a, b, (((1,), (1,)), ((), ())), preferred_element_type=F32)


def tn(a, b):
    return lax.dot_general(a, b, (((0,), (0,)), ((), ())), preferred_element_type=F32)


def same_head(width):
    row = lax.broadcasted_iota(jnp.int32, (width, width), 0) // HEAD
    col = lax.broadcasted_iota(jnp.int32, (width, width), 1) // HEAD
    return row == col


def lane_head(rows, width):
    return lax.broadcasted_iota(jnp.int32, (rows, width), 1) // HEAD


def causal(rows):
    row = lax.broadcasted_iota(jnp.int32, (rows, rows), 0)
    col = lax.broadcasted_iota(jnp.int32, (rows, rows), 1)
    return row >= col


def fold_heads(full, width):
    out = full[0:HEAD]
    for h in range(1, width // HEAD):
        out = out + full[h * HEAD : (h + 1) * HEAD]
    return out


def spread_heads(part, width, block):
    tall = jnp.concatenate([part] * (width // HEAD), axis=0)
    return jnp.where(block, tall, jnp.zeros_like(tall))


def pick(mask, value):
    return jnp.where(mask, value, jnp.zeros_like(value))


def vmem():
    return pl.BlockSpec(memory_space=pltpu.VMEM)


def smem():
    return pl.BlockSpec(memory_space=pltpu.SMEM)


def shape(rows, cols, kind):
    return jax.ShapeDtypeStruct((rows, cols), kind)


ROW_TILE = 192


def tiles(rows):
    return [slice(i, i + ROW_TILE) for i in range(0, rows, ROW_TILE)]


def kernel(body, name, out_shape, in_specs, megabytes, scratch=(), aliases=None, tokens=()):
    outs = vmem() if not isinstance(out_shape, tuple) else (vmem(),) * len(out_shape)
    count = len(in_specs)

    def run(*refs):
        body(*refs[:count], *refs[count + len(tokens) :])

    call = pl.pallas_call(
        run,
        out_shape=out_shape,
        in_specs=in_specs + [pl.BlockSpec(memory_space=pl.ANY)] * len(tokens),
        out_specs=outs,
        scratch_shapes=list(scratch),
        input_output_aliases=aliases or {},
        compiler_params=pltpu.CompilerParams(vmem_limit_bytes=megabytes << 20),
        name=name,
    )
    return lambda *args: call(*args, *tokens)


def normal(values):
    centre = jnp.mean(values, axis=-1, keepdims=True)
    moved = values - centre
    scale = lax.rsqrt(jnp.mean(moved * moved, axis=-1, keepdims=True) + 1e-05)
    return moved * scale, scale


def normal_back(grad, gain, xhat, scale):
    g = grad * gain
    return scale * (
        g - jnp.mean(g, axis=-1, keepdims=True) - xhat * jnp.mean(g * xhat, axis=-1, keepdims=True)
    )


def total(refs):
    value = refs[0][...].astype(F32)
    for ref in refs[1:]:
        value = value + ref[...].astype(F32)
    return value


def norm_body(x_ref, gain_ref, bias_ref, out_ref):
    for at in tiles(x_ref.shape[0]):
        xhat, _ = normal(x_ref[at, :].astype(F32))
        out_ref[at, :] = (xhat * gain_ref[...] + bias_ref[...]).astype(BF)


def norm_one(x, gain, bias):
    call = kernel(norm_body, "norm_one", shape(x.shape[0], D, BF), [vmem()] * 3, 8)
    return call(x, gain, bias)


def total(refs, at):
    value = refs[0][at, :].astype(F32)
    for ref in refs[1:]:
        value = value + ref[at, :].astype(F32)
    return value


def middle_body(*refs):
    x_ref, gain_ref, bias_ref = refs[:3]
    parts = refs[3:-3]
    middle_ref, out_ref, square_ref = refs[-3:]
    for at in tiles(x_ref.shape[0]):
        attended = total(parts, at)
        middle = x_ref[at, :].astype(F32) + attended
        middle_ref[at, :] = middle
        xhat, _ = normal(middle)
        out_ref[at, :] = (xhat * gain_ref[...] + bias_ref[...]).astype(BF)
        square_ref[at, :] = jnp.sum(attended * attended, axis=-1, keepdims=True)


def norm_two(x, gain, bias, parts):
    rows = x.shape[0]
    call = kernel(
        middle_body, "norm_two", (shape(rows, D, F32), shape(rows, D, BF), shape(rows, 1, F32)),
        [vmem()] * (3 + len(parts)), 12,
    )
    return call(x, gain, bias, *parts)


def middle_back_body(*refs):
    grad_ref, middle_ref, gain_ref = refs[:3]
    parts = refs[3:-4]
    wide_ref, low_ref, gain_grad_ref, bias_grad_ref = refs[-4:]
    gain_grad = bias_grad = jnp.zeros(gain_ref.shape, F32)
    for at in tiles(grad_ref.shape[0]):
        grad = total(parts, at)
        xhat, scale = normal(middle_ref[at, :])
        gain_grad = gain_grad + jnp.sum(grad * xhat, axis=0, keepdims=True)
        bias_grad = bias_grad + jnp.sum(grad, axis=0, keepdims=True)
        out = grad_ref[at, :].astype(F32) + normal_back(grad, gain_ref[...], xhat, scale)
        wide_ref[at, :] = out
        low_ref[at, :] = out.astype(BF)
    gain_grad_ref[...] = gain_grad
    bias_grad_ref[...] = bias_grad


def norm_two_back(grad, middle, gain, parts, tokens):
    rows = grad.shape[0]
    call = kernel(
        middle_back_body, "norm_two_back",
        (shape(rows, D, F32), shape(rows, D, BF), shape(1, D, F32), shape(1, D, F32)),
        [vmem()] * (3 + len(parts)), 16, tokens=tokens,
    )
    return call(grad, middle, gain, *parts)


def pixels_back_body(*refs):
    x_ref, wide_ref, gain_ref = refs[:3]
    parts = refs[3:-3]
    out_ref, gain_grad_ref, bias_grad_ref = refs[-3:]
    gain_grad = bias_grad = jnp.zeros(gain_ref.shape, F32)
    for at in tiles(x_ref.shape[0]):
        grad = total(parts, at)
        xhat, scale = normal(x_ref[at, :].astype(F32))
        gain_grad = gain_grad + jnp.sum(grad * xhat, axis=0, keepdims=True)
        bias_grad = bias_grad + jnp.sum(grad, axis=0, keepdims=True)
        out_ref[at, :] = (wide_ref[at, :] + normal_back(grad, gain_ref[...], xhat, scale)).astype(BF)
    gain_grad_ref[...] = gain_grad
    bias_grad_ref[...] = bias_grad


def norm_one_back(x, wide, gain, parts):
    rows = x.shape[0]
    call = kernel(
        pixels_back_body, "norm_one_back", (shape(rows, D, BF), shape(1, D, F32), shape(1, D, F32)),
        [vmem()] * (3 + len(parts)), 16,
    )
    return call(x, wide, gain, *parts)


def result_body(*refs):
    middle_ref = refs[0]
    parts = refs[1:-3]
    out_ref, result_square_ref, branch_square_ref = refs[-3:]
    for at in tiles(middle_ref.shape[0]):
        branch = total(parts, at)
        result = middle_ref[at, :] + branch
        out_ref[at, :] = result.astype(BF)
        result_square_ref[at, :] = jnp.sum(result * result, axis=-1, keepdims=True)
        branch_square_ref[at, :] = jnp.sum(branch * branch, axis=-1, keepdims=True)


def finish(middle, parts, tokens):
    rows = middle.shape[0]
    call = kernel(
        result_body, "finish", (shape(rows, D, BF), shape(rows, 1, F32), shape(rows, 1, F32)),
        [vmem()] * (1 + len(parts)), 12, tokens=tokens,
    )
    return call(middle, *parts)


def pair_slices(pair, rows):
    for i in range(2):
        yield i, slice(i * rows, (i + 1) * rows), slice((2 * pair + i) * rows, (2 * pair + i + 1) * rows)


def qkv_body(pair, tail_ref, xa_ref, xb_ref, w_ref, valid_ref, seg_ref, was_ref, *rest):
    q_ref, k_ref, v_ref, pack_ref = rest[-4:]
    width = q_ref.shape[1]
    block = same_head(width)
    state, sums = was_ref[0:HEAD, :], was_ref[HEAD:PACK, :]
    for i, _, at in pair_slices(pair, xa_ref.shape[0]):
        x = (xa_ref, xb_ref)[i][...]
        q_ref[at, :] = feature(nn(x, w_ref[0])).astype(BF)
        k = (feature(nn(x, w_ref[1])) * valid_ref[at, :]).astype(BF)
        v = nn(x, w_ref[2]).astype(BF)
        k_ref[at, :] = k
        v_ref[at, :] = v
        kept = pick(seg_ref[at, :] == tail_ref[0], k)
        state = state + fold_heads(pick(block, tn(kept, v)), width)
        sums = sums + jnp.sum(kept.astype(F32), axis=0, keepdims=True)
    pack_ref[0:HEAD, :] = state
    pack_ref[HEAD:PACK, :] = sums


def project_qkv(pair, tail, xa, xb, w, valid, seg, was, made):
    width, whole = w.shape[2], valid.shape[0]
    call = kernel(
        functools.partial(qkv_body, pair), "project_qkv",
        (shape(whole, width, BF),) * 3 + (shape(PACK, width, F32),),
        [smem()] + [vmem()] * (6 + len(made)), 16,
        aliases={7 + i: i for i in range(len(made))},
    )
    return call(tail, xa, xb, w, valid, seg, was, *made)


def swap_heads(x):
    return jnp.concatenate(
        [pltpu.roll(x[:, i : i + 2 * HEAD], HEAD, 1) for i in range(0, x.shape[1], 2 * HEAD)], axis=1
    )


def forward_body(
    last_ref, spot_ref, q_ref, k_ref, v_ref, segc_ref, segr_ref, num_ref, den_ref, st_ref, ks_ref
):
    rows, width = q_ref.shape
    size = CHUNK
    block = same_head(width)
    ones_block = block.astype(BF)
    lanes = lane_head(size, width)
    even = (lanes % 2) == 0
    lower = causal(size)
    st_ref[...] = jnp.zeros_like(st_ref)
    ks_ref[...] = jnp.zeros_like(ks_ref)

    def step(c, carry):
        spot = spot_ref[c]
        at = pl.ds(pl.multiple_of(spot * size, size), size)
        q, k, v = q_ref[at, :], k_ref[at, :], v_ref[at, :]
        seg = segc_ref[at, :]
        keep = (lower & (seg == segr_ref[spot])).astype(BF)
        before, after = last_ref[c], last_ref[c + 1]
        carried = (seg == before).astype(F32)
        sums = [jnp.zeros((size, width), F32)] * 2
        for h in range(width // HEAD):
            mine = lanes == h
            score = nt(pick(mine, q), k).astype(BF) * keep
            both = jnp.where(mine, v, (lanes == (h ^ 1)).astype(BF))
            sums[h % 2] = sums[h % 2] + nn(score, both)
        num = jnp.where(even, sums[0], sums[1])
        den = swap_heads(jnp.where(even, sums[1], sums[0]))
        num_ref[at, :] = num + carried * nn(q, st_ref[...].astype(BF))
        den_ref[at, :] = den + carried * nn((q.astype(F32) * ks_ref[0:1, :]).astype(BF), ones_block)
        kept = pick(seg == after, k)
        cont = (before == after).astype(F32)
        st_ref[...] = cont * st_ref[...] + pick(block, tn(kept, v))
        ks_ref[...] = cont * ks_ref[...] + jnp.sum(kept.astype(F32), axis=0, keepdims=True)
        return carry

    lax.fori_loop(0, rows // size, step, 0)


def attend(last, spot, q, k, v, segc, segr):
    rows, width = q.shape
    call = kernel(
        forward_body, "attend", (shape(rows, width, F32),) * 2, [smem()] * 2 + [vmem()] * 5, 24,
        scratch=[pltpu.VMEM((width, width), F32), pltpu.VMEM((8, width), F32)],
    )
    return call(last, spot, q, k, v, segc, segr)


def project_body(
    pair, first_ref, num_ref, den_ref, q_ref, pack_ref, segc_ref, valid_ref, w_ref,
    heads_ref, wide_ref, rinv_ref, a_ref, b_ref
):
    width = q_ref.shape[1]
    block = same_head(width)
    state = spread_heads(pack_ref[0:HEAD, :], width, block).astype(BF)
    sums = pack_ref[HEAD : HEAD + 1, :]
    for i, own, at in pair_slices(pair, a_ref.shape[0]):
        q = q_ref[at, :]
        opening = (segc_ref[at, :] == first_ref[0]).astype(F32)
        valid = valid_ref[at, :]
        num = num_ref[at, :] + opening * nn(q, state)
        den = den_ref[at, :] + opening * nn((q.astype(F32) * sums).astype(BF), block.astype(BF))
        rinv = valid / (den + 1e-06 + 1.0 - valid)
        wide = num * rinv
        heads = wide.astype(BF)
        heads_ref[own, :] = heads
        wide_ref[own, :] = wide
        rinv_ref[own, :] = rinv
        (a_ref, b_ref)[i][...] = nn(heads, w_ref[...]).astype(BF)


def project(pair, rows, last, num, den, q, pack, segc, valid, w, tokens):
    width = q.shape[1]
    call = kernel(
        functools.partial(project_body, pair), "project",
        (shape(2 * rows, width, BF), shape(2 * rows, width, F32), shape(2 * rows, width, F32))
        + (shape(rows, D, BF),) * 2,
        [smem()] + [vmem()] * 7, 12, tokens=tokens,
    )
    return call(last, num, den, q, pack, segc, valid, w)


def mlp_body(
    xa_ref, xb_ref, ga_ref, gb_ref, up_ref, down_ref, act_ref, hid_ref, na_ref, nb_ref, ba_ref, bb_ref
):
    root = 0.7978845608028654
    tile = min(512, up_ref.shape[1])
    for i, own, _ in pair_slices(0, xa_ref.shape[0]):
        x, g = (xa_ref, xb_ref)[i][...], (ga_ref, gb_ref)[i][...]
        for j in range(0, up_ref.shape[1], tile):
            cols = slice(j, j + tile)
            h = nn(x, up_ref[:, cols])
            grad = nt(g, down_ref[cols, :])
            square = h * h
            t = jnp.tanh(root * h * (1.0 + 0.044715 * square))
            plus = 0.5 * (1.0 + t)
            slope = plus + 0.5 * h * (1.0 - t * t) * (root + (3.0 * 0.044715 * root) * square)
            act_ref[own, cols] = (h * plus).astype(BF)
            hid_ref[own, cols] = (grad * slope).astype(BF)
        (na_ref, nb_ref)[i][...] = nt(hid_ref[own, :], up_ref[...]).astype(BF)
        (ba_ref, bb_ref)[i][...] = nn(act_ref[own, :], down_ref[...]).astype(BF)


def mlp(xa, xb, ga, gb, up, down):
    rows, hidden = xa.shape[0], up.shape[1]
    call = kernel(
        mlp_body, "mlp", (shape(2 * rows, hidden, BF),) * 2 + (shape(rows, D, BF),) * 4,
        [vmem()] * 6, 32,
    )
    return call(xa, xb, ga, gb, up, down)


def heads_back_body(
    pair, first_ref, ga_ref, gb_ref, w_ref, wide_ref, rinv_ref, q_ref, segc_ref, was_ref, *rest
):
    ng_ref, dg_ref, pack_ref = rest[-3:]
    width = q_ref.shape[1]
    block = same_head(width)
    ones_block = block.astype(BF)
    state, sums = was_ref[0:HEAD, :], was_ref[HEAD:PACK, :]
    for i, own, at in pair_slices(pair, ga_ref.shape[0]):
        hg = nt((ga_ref, gb_ref)[i][...], w_ref[...])
        rinv = rinv_ref[own, :]
        ng = (hg * rinv).astype(BF)
        prod = hg * wide_ref[own, :]
        high = prod.astype(BF)
        low = (prod - high.astype(F32)).astype(BF)
        dg = -(nn(high, ones_block) + nn(low, ones_block)) * rinv
        ng_ref[at, :] = ng
        dg_ref[at, :] = dg
        opened = pick(segc_ref[at, :] == first_ref[0], q_ref[at, :])
        state = state + fold_heads(pick(block, tn(opened, ng)), width)
        sums = sums + jnp.sum(opened.astype(F32) * dg, axis=0, keepdims=True)
    pack_ref[0:HEAD, :] = state
    pack_ref[HEAD:PACK, :] = sums


def heads_back(pair, last, ga, gb, w, wide, rinv, q, segc, was, made, tokens=()):
    whole, width = q.shape
    call = kernel(
        functools.partial(heads_back_body, pair), "heads_back",
        (shape(whole, width, BF), shape(whole, width, F32), shape(PACK, width, F32)),
        [smem()] + [vmem()] * (8 + len(made)), 16,
        aliases={9 + i: i for i in range(len(made))}, tokens=tokens,
    )
    return call(last, ga, gb, w, wide, rinv, q, segc, was, *made)


def backward_body(
    last_ref, spot_ref, q_ref, k_ref, v_ref, ng_ref, dg_ref, segc_ref, segr_ref, pack_ref,
    dq_ref, dk_ref, dv_ref, all_ref, sums_ref, st_ref, ks_ref
):
    rows, width = q_ref.shape
    size = CHUNK
    count = rows // size
    block = same_head(width)
    lanes = lane_head(size, width)
    half = (lax.broadcasted_iota(jnp.int32, (size, width), 1) % HEAD) < HEAD // 2
    lower = causal(size)
    st_ref[...] = spread_heads(pack_ref[0:HEAD, :], width, block)
    ks_ref[...] = jnp.broadcast_to(pack_ref[HEAD : HEAD + 1, :], ks_ref.shape)

    def collect(c, carry):
        at = pl.ds(pl.multiple_of(spot_ref[c] * size, size), size)
        all_ref[c] = st_ref[...].astype(BF)
        sums_ref[c] = ks_ref[...]
        before, after = last_ref[c], last_ref[c + 1]
        kept = pick(segc_ref[at, :] == after, k_ref[at, :])
        cont = (before == after).astype(F32)
        st_ref[...] = cont * st_ref[...] + pick(block, tn(kept, v_ref[at, :]))
        ks_ref[...] = cont * ks_ref[...] + jnp.sum(kept.astype(F32), axis=0, keepdims=True)
        return carry

    lax.fori_loop(0, count, collect, 0)
    st_ref[...] = jnp.zeros_like(st_ref)
    ks_ref[...] = jnp.zeros_like(ks_ref)

    def step(i, carry):
        c = count - 1 - i
        spot = spot_ref[c]
        at = pl.ds(pl.multiple_of(spot * size, size), size)
        q, k, v, ng, dg = q_ref[at, :], k_ref[at, :], v_ref[at, :], ng_ref[at, :], dg_ref[at, :]
        seg = segc_ref[at, :]
        keep = (lower & (seg == segr_ref[spot])).astype(BF)
        before, after = last_ref[c], last_ref[c + 1]
        opened = seg == before
        carried = opened.astype(F32)
        tail = (seg == after).astype(F32)
        grad_state = st_ref[...].astype(BF)
        moved = swap_heads(dg)
        high = moved.astype(BF)
        low = (moved - high.astype(F32)).astype(BF)
        terms = jnp.where(half, high, low) * jnp.asarray(2.0 / HEAD, BF)
        one = jnp.ones((), BF)
        dq = carried * (nt(ng, all_ref[c]) + dg * sums_ref[c][0:1, :])
        dk = tail * (nt(v, grad_state) + ks_ref[0:1, :])
        dv = tail * nn(k, grad_state)
        for h in range(width // HEAD):
            mine = lanes == h
            qh, kh, nh = pick(mine, q), pick(mine, k), pick(mine, ng)
            score = nt(qh, k).astype(BF) * keep
            left = jnp.where(mine, ng, pick(lanes == (h ^ 1), terms))
            back = nt(left, jnp.where(mine, v, one)).astype(BF) * keep
            dq = dq + nn(back, kh)
            dk = dk + tn(back, qh)
            dv = dv + tn(score, nh)
        dq_ref[at, :] = (dq * jnp.minimum(q.astype(F32), 1.0)).astype(BF)
        dk_ref[at, :] = dk
        dv_ref[at, :] = dv
        cont = (before == after).astype(F32)
        st_ref[...] = cont * st_ref[...] + pick(block, tn(pick(opened, q), ng))
        ks_ref[...] = cont * ks_ref[...] + jnp.sum(carried * q.astype(F32) * dg, axis=0, keepdims=True)
        return carry

    lax.fori_loop(0, count, step, 0)


def attend_back(last, spot, q, k, v, ng, dg, segc, segr, pack, tokens):
    rows, width = q.shape
    count = rows // CHUNK
    call = kernel(
        backward_body, "attend_back",
        (shape(rows, width, BF), shape(rows, width, F32), shape(rows, width, F32)),
        [smem()] * 2 + [vmem()] * 8, 32,
        scratch=[
            pltpu.VMEM((count, width, width), BF),
            pltpu.VMEM((count, 8, width), F32),
            pltpu.VMEM((width, width), F32),
            pltpu.VMEM((8, width), F32),
        ],
        tokens=tokens,
    )
    return call(last, spot, q, k, v, ng, dg, segc, segr, pack)


def mix_body(
    pair, tail_ref, dq_ref, dk_ref, dv_ref, k_ref, v_ref, segc_ref, valid_ref, pack_ref, w_ref,
    mixed_ref, a_ref, b_ref
):
    width = k_ref.shape[1]
    block = same_head(width)
    state = spread_heads(pack_ref[0:HEAD, :], width, block).astype(BF)
    sums = pack_ref[HEAD : HEAD + 1, :]
    for i, own, at in pair_slices(pair, a_ref.shape[0]):
        tail = (segc_ref[at, :] == tail_ref[0]).astype(F32)
        k = k_ref[at, :]
        dk = dk_ref[at, :] + tail * (nt(v_ref[at, :], state) + sums)
        dv = dv_ref[at, :] + tail * nn(k, state)
        dq = dq_ref[at, :]
        dk = (valid_ref[at, :] * dk * jnp.minimum(k.astype(F32), 1.0)).astype(BF)
        dv = dv.astype(BF)
        mixed_ref[own, 0:width] = dq
        mixed_ref[own, width : 2 * width] = dk
        mixed_ref[own, 2 * width : 3 * width] = dv
        out = nt(dq, w_ref[0]) + nt(dk, w_ref[1]) + nt(dv, w_ref[2])
        (a_ref, b_ref)[i][...] = out.astype(BF)


def mix(pair, rows, tail, dq, dk, dv, k, v, segc, valid, pack, w, tokens):
    width = k.shape[1]
    call = kernel(
        functools.partial(mix_body, pair), "mix",
        (shape(2 * rows, 3 * width, BF),) + (shape(rows, D, BF),) * 2,
        [smem()] + [vmem()] * 9, 16, tokens=tokens,
    )
    return call(tail, dq, dk, dv, k, v, segc, valid, pack, w)


def feature(values):
    return jnp.where(values > 0, values + 1.0, jnp.exp(jnp.minimum(values, 0.0)))


def bits_of(count):
    return [1 << b for b in range(count.bit_length() - 1)]


def swap(value, axis, bit):
    return lax.ppermute(value, axis, [(i, i ^ bit) for i in range(lax.axis_size(axis))])


def after(value, *tokens):
    return lax.optimization_barrier((value, *tokens))[0] if tokens else value


def gather_begin(value):
    slots = {0: value}
    for bit in reversed(bits_of(lax.axis_size("feat"))[1:]):
        for s in sorted(slots):
            slots[s | bit] = swap(slots[s], "feat", bit)
    slots[1] = swap(value, "feat", 1)
    return slots


def gather_end(slots, *tokens):
    for s in range(2, lax.axis_size("feat"), 2):
        slots[s + 1] = swap(after(slots[s], *tokens), "feat", 1)
    return [slots[s] for s in range(len(slots))]


def scatter_begin(parts):
    sums = {}
    for s in range(len(parts) - 2, -1, -2):
        got = swap(parts[s + 1], "feat", 1)
        sums[s] = (parts[s].astype(F32) + got.astype(F32)).astype(BF) if s else [parts[0], got]
    return sums


def scatter_end(sums, *tokens):
    sums = {s: part if s == 0 else [after(part, *tokens)] for s, part in sums.items()}
    for bit in bits_of(lax.axis_size("feat"))[1:]:
        for s in sorted(sums, reverse=True):
            if s & bit:
                pieces = sums.pop(s)
                value = pieces[0]
                if len(pieces) > 1:
                    value = functools.reduce(jnp.add, [p.astype(F32) for p in pieces]).astype(BF)
                sums[s ^ bit].append(swap(value, "feat", bit))
    return sums[0]


def sum_everywhere(value):
    for axis in ("feat", "rows"):
        for bit in bits_of(lax.axis_size(axis)):
            value = value + swap(value, axis, bit)
    return value


class RowSum:
    def __init__(self, value, order, *tokens):
        self.order, self.step = order, 0
        self.value = after(value, *tokens)
        self.launch()

    def launch(self):
        count = len(self.order)
        halving = self.step < count
        bit = self.order[self.step] if halving else self.order[2 * count - 1 - self.step]
        self.upper = (lax.axis_index("rows") & bit) != 0
        self.sent = self.kept = self.value
        if halving:
            half = self.value.shape[0] // 2
            low, high = self.value[:half], self.value[half:]
            self.sent = jnp.where(self.upper, low, high)
            self.kept = jnp.where(self.upper, high, low)
        self.got = swap(self.sent, "rows", bit)

    def next(self, *tokens):
        got = after(self.got, *tokens)
        if self.step < len(self.order):
            self.value = (self.kept.astype(F32) + got.astype(F32)).astype(BF)
        else:
            first = jnp.where(self.upper, got, self.kept)
            self.value = jnp.concatenate([first, jnp.where(self.upper, self.kept, got)], axis=0)
        self.step += 1
        if self.step < 2 * len(self.order):
            self.launch()
            return self.sent
        return self.value

    def finish(self, *tokens):
        while self.step < 2 * len(self.order):
            self.next(*tokens)
        return self.value


def shifted(pack, hop, groups, reverse):
    if reverse:
        pairs = [(i, i - hop) for i in range(hop, groups)]
    else:
        pairs = [(i, i + hop) for i in range(groups - hop)]
    return lax.ppermute(pack, "rows", pairs)


def gather_carry(pack, crops_at, here, groups, reach, reverse):
    total = jnp.zeros(pack.shape, F32)
    mine = crops_at[here + 1] if reverse else crops_at[here]
    for hop in range(1, reach + 1):
        got = shifted(pack, hop, groups, reverse).astype(F32)
        other = here + hop if reverse else here - hop
        inside = (other < groups) if reverse else (other >= 0)
        at = jnp.clip(other, 0, groups - 1)
        theirs = crops_at[at] if reverse else crops_at[at + 1]
        total = total + jnp.where(inside & (theirs == mine), got, 0.0)
    return total


def on_device(
    pixels,
    qkv_weight,
    out_weight,
    up_weight,
    down_weight,
    norm1_gain,
    norm1_bias,
    norm2_gain,
    norm2_bias,
    crop_lengths,
    crop_offsets,
    pixel_mask,
    out_grad,
):
    local_rows = pixels.shape[0]
    group_rows = pixel_mask.shape[0]
    width = qkv_weight.shape[2]
    crop_count = crop_offsets.shape[0]
    groups = lax.axis_size("rows")
    members = lax.axis_size("feat")
    pairs = members // 2
    here = lax.axis_index("rows")
    member = lax.axis_index("feat")
    reach = min(groups - 1, -(-(CROP_MAX - 1) // group_rows))
    group_start = here * group_rows
    slot_ids = jnp.arange(members, dtype=jnp.int32) ^ member
    in_group = (slot_ids[:, None] * local_rows + jnp.arange(local_rows, dtype=jnp.int32)[None, :]).reshape(-1)
    places = group_start + in_group
    started = crop_offsets[None, :] <= places[:, None]
    crop_ends = crop_offsets + crop_lengths
    segment = jnp.sum(started.astype(jnp.int32), axis=1) - 1
    inside = jnp.sum((started & (places[:, None] < crop_ends[None, :])).astype(jnp.int32), axis=1)
    mask = jnp.concatenate(
        [
            lax.dynamic_slice_in_dim(pixel_mask, (member ^ s) * local_rows, local_rows)
            for s in range(members)
        ]
    )
    pixel_valid = (mask * inside).astype(F32)
    edges = jnp.arange(groups + 1, dtype=jnp.int32) * group_rows - 1
    crops_at = jnp.sum((crop_offsets[None, :] <= edges[:, None]).astype(jnp.int32), axis=1) - 1
    chunks = group_rows // CHUNK
    per = local_rows // CHUNK
    chunk_edges = group_start - 1 + jnp.arange(chunks + 1, dtype=jnp.int32) * CHUNK
    last = jnp.sum((crop_offsets[None, :] <= chunk_edges[:, None]).astype(jnp.int32), axis=1) - 1
    tail = last[-1:]
    order = jnp.arange(chunks, dtype=jnp.int32)
    spot = ((order // per) ^ member) * per + order % per
    segc = segment[:, None]
    segr = segment.reshape(chunks, 1, CHUNK)
    validc = pixel_valid[:, None]
    gain1, bias1, gain2, bias2 = (
        a[None, :] for a in (norm1_gain, norm1_bias, norm2_gain, norm2_bias)
    )
    no_pack = jnp.zeros((PACK, width), F32)

    normed_slots = gather_begin(norm_one(pixels, gain1, bias1))
    grad_slots = gather_begin(after(out_grad, normed_slots[members // 2]))
    *made, pack = project_qkv(0, tail, normed_slots[0], normed_slots[1], qkv_weight, validc, segc, no_pack, ())
    normed_slots = gather_end(normed_slots, pack)
    for p in range(1, pairs):
        *made, pack = project_qkv(
            p, tail, normed_slots[2 * p], normed_slots[2 * p + 1], qkv_weight, validc, segc, pack, made
        )
    q, k, v = made
    carry = gather_carry(pack.astype(BF), crops_at, here, groups, reach, False)
    num, den = attend(last, spot, q, k, v, segc, segr)
    grad_slots = gather_end(grad_slots, num)
    sent = {
        p: project(
            p, local_rows, last, num, den, q, carry, segc, validc, out_weight, [grad_slots[members // 2]]
        )
        for p in reversed(range(pairs))
    }
    parts = scatter_end(scatter_begin([sent[s // 2][3 + s % 2] for s in range(members)]))
    middle, normed_two, attended_square = norm_two(pixels, gain2, bias2, parts)
    two_slots = gather_begin(normed_two)
    hidden = [mlp(two_slots[0], two_slots[1], grad_slots[0], grad_slots[1], up_weight, down_weight)]
    two_slots = gather_end(two_slots, hidden[0][0])
    for p in range(1, pairs):
        hidden.append(mlp(*two_slots[2 * p : 2 * p + 2], *grad_slots[2 * p : 2 * p + 2], up_weight, down_weight))
    two_parts = scatter_end(scatter_begin([hidden[s // 2][2 + s % 2] for s in range(members)]))
    branch_sums = scatter_begin([hidden[s // 2][4 + s % 2] for s in range(members)])
    down_grad = tn(
        jnp.concatenate([h[0] for h in hidden], axis=0), jnp.concatenate(grad_slots, axis=0)
    ).astype(BF)
    up_grad = tn(
        jnp.concatenate(two_slots, axis=0), jnp.concatenate([h[1] for h in hidden], axis=0)
    ).astype(BF)
    bits = bits_of(groups)
    turned = bits[1:] + bits[:1]
    down_sum = RowSum(down_grad, bits, two_parts[-1])
    up_sum = RowSum(up_grad, turned, two_parts[-1])
    middle_grad, middle_low, gain2_grad, bias2_grad = norm_two_back(
        out_grad, middle, gain2, two_parts,
        [down_sum.sent, up_sum.sent, branch_sums[0][1], branch_sums[members - 2]],
    )
    middle_slots = gather_begin(middle_low)
    *made, grad_pack = heads_back(
        0, last, middle_slots[0], middle_slots[1], out_weight, sent[0][1], sent[0][2], q, segc, no_pack, ()
    )
    branch_parts = scatter_end(branch_sums, middle_slots[members // 2])
    tokens = [x.next(middle_slots[members // 2]) for x in (down_sum, up_sum)]
    middle_slots = gather_end(middle_slots, grad_pack)
    for p in range(1, pairs):
        *made, grad_pack = heads_back(
            p, last, middle_slots[2 * p], middle_slots[2 * p + 1], out_weight,
            sent[p][1], sent[p][2], q, segc, grad_pack, made, tokens
        )
    ng, dg = made
    grad_carry = gather_carry(grad_pack.astype(BF), crops_at, here, groups, reach, True)
    out_weight_grad = tn(
        jnp.concatenate([sent[p][0] for p in range(pairs)], axis=0), jnp.concatenate(middle_slots, axis=0)
    ).astype(BF)
    tokens = [out_weight_grad]
    dq, dk, dv = attend_back(last, spot, q, k, v, ng, dg, segc, segr, carry, tokens)
    out_sum = RowSum(out_weight_grad, turned, dq)
    tokens = [down_sum.next(dq), up_sum.next(dq), out_sum.sent]
    mixes = {
        p: mix(p, local_rows, tail, dq, dk, dv, k, v, segc, validc, grad_carry, qkv_weight, tokens)
        for p in reversed(range(pairs))
    }
    normed_sums = scatter_begin([mixes[s // 2][1 + s % 2] for s in range(members)])
    normed_parts = scatter_end(normed_sums)
    mixed_grad = jnp.concatenate([mixes[p][0] for p in range(pairs)], axis=0)
    qkv_grad = tn(mixed_grad, jnp.concatenate(normed_slots, axis=0)).astype(BF)
    output, result_square, branch_square = finish(middle, branch_parts, [dq])
    pixels_grad, gain1_grad, bias1_grad = norm_one_back(pixels, middle_grad, gain1, normed_parts)

    tokens = [down_sum.next(mixed_grad), up_sum.next(mixed_grad), out_sum.next(mixed_grad)]
    cut = 3 * width // 2
    low_sum = RowSum(qkv_grad[:cut], bits, *tokens)
    high_sum = RowSum(qkv_grad[cut:], turned, *tokens)
    normed_sent = normed_sums[members - 2]
    tokens = [low_sum.next(normed_sent), high_sum.next(normed_sent)]
    tokens = [down_sum.next(*tokens), up_sum.next(*tokens), out_sum.next(*tokens)]
    tokens = [low_sum.next(*tokens), high_sum.next(*tokens)]
    out_weight_grad = out_sum.finish(*tokens).astype(F32)
    tokens = [low_sum.next(), high_sum.next()]
    down_grad = down_sum.finish(*tokens).astype(F32)
    up_grad = up_sum.finish(*tokens).astype(F32)
    qkv_grad = jnp.concatenate([low_sum.finish(), high_sum.finish()], axis=0)
    qkv_grad = jnp.swapaxes(qkv_grad.reshape(3, width, D), 1, 2).astype(F32)

    crop_onehot = (
        segment[:local_rows, None] == jnp.arange(crop_count, dtype=jnp.int32)[None, :]
    ).astype(F32)
    squares = (
        jnp.concatenate(
            [result_square, attended_square, branch_square, jnp.ones((local_rows, 1), F32)], axis=1
        )
        * validc[:local_rows]
    )
    crop_sums = lax.dot_general(
        squares, crop_onehot, (((0,), (0,)), ((), ())), precision=precise, preferred_element_type=F32
    )
    sums = jnp.concatenate(
        [gain1_grad[0], bias1_grad[0], gain2_grad[0], bias2_grad[0], crop_sums.reshape(-1)]
    )
    sums = sum_everywhere(sums)
    gain1_grad, bias1_grad, gain2_grad, bias2_grad = sums[: 4 * D].reshape(4, D)
    crop_sums = sums[4 * D :].reshape(4, crop_count)
    crop_rms = jnp.sqrt(crop_sums[:3] / (D * jnp.maximum(crop_sums[3], 1.0))[None, :])
    return (
        output,
        pixels_grad,
        qkv_grad,
        out_weight_grad,
        up_grad,
        down_grad,
        gain1_grad,
        bias1_grad,
        gain2_grad,
        bias2_grad,
        crop_rms,
    )


def solution(mesh):
    split = P(("rows", "feat"), None)
    qkv, rows_feat, cols_feat = P(None, None, "feat"), P("feat", None), P(None, "feat")
    in_specs = (
        (split, qkv, rows_feat, cols_feat, rows_feat) + (P(),) * 6 + (P("rows"), split)
    )
    out_specs = (split, split, qkv, rows_feat, cols_feat, rows_feat) + (P(),) * 5
    return jax.shard_map(
        on_device, mesh=mesh, in_specs=in_specs, out_specs=out_specs, check_vma=False
    )
```

```python
import functools

import jax
import jax.numpy as jnp
from jax import lax
from jax.experimental import pallas as pl
from jax.experimental.pallas import tpu as pltpu
from jax.sharding import PartitionSpec as P

D = 1024
HEAD = 64
CHUNK = 384
CROP_MAX = 3072
PACK = HEAD + 16

BF = jnp.bfloat16
F32 = jnp.float32
precise = lax.Precision.HIGHEST


def nn(a, b):
    return lax.dot_general(a, b, (((1,), (0,)), ((), ())), preferred_element_type=F32)


def nt(a, b):
    return lax.dot_general(a, b, (((1,), (1,)), ((), ())), preferred_element_type=F32)


def tn(a, b):
    return lax.dot_general(a, b, (((0,), (0,)), ((), ())), preferred_element_type=F32)


def same_head(width):
    row = lax.broadcasted_iota(jnp.int32, (width, width), 0) // HEAD
    col = lax.broadcasted_iota(jnp.int32, (width, width), 1) // HEAD
    return row == col


def lane_head(rows, width):
    return lax.broadcasted_iota(jnp.int32, (rows, width), 1) // HEAD


def causal(rows):
    row = lax.broadcasted_iota(jnp.int32, (rows, rows), 0)
    col = lax.broadcasted_iota(jnp.int32, (rows, rows), 1)
    return row >= col


def fold_heads(full, width):
    out = full[0:HEAD]
    for h in range(1, width // HEAD):
        out = out + full[h * HEAD : (h + 1) * HEAD]
    return out


def spread_heads(part, width, block):
    tall = jnp.concatenate([part] * (width // HEAD), axis=0)
    return jnp.where(block, tall, jnp.zeros_like(tall))


def pick(mask, value):
    return jnp.where(mask, value, jnp.zeros_like(value))


def vmem():
    return pl.BlockSpec(memory_space=pltpu.VMEM)


def smem():
    return pl.BlockSpec(memory_space=pltpu.SMEM)


def shape(rows, cols, kind):
    return jax.ShapeDtypeStruct((rows, cols), kind)


ROW_TILE = 192


def tiles(rows):
    return [slice(i, i + ROW_TILE) for i in range(0, rows, ROW_TILE)]


def kernel(body, name, out_shape, in_specs, megabytes, scratch=(), aliases=None, tokens=()):
    outs = vmem() if not isinstance(out_shape, tuple) else (vmem(),) * len(out_shape)
    count = len(in_specs)

    def run(*refs):
        body(*refs[:count], *refs[count + len(tokens) :])

    call = pl.pallas_call(
        run,
        out_shape=out_shape,
        in_specs=in_specs + [pl.BlockSpec(memory_space=pl.ANY)] * len(tokens),
        out_specs=outs,
        scratch_shapes=list(scratch),
        input_output_aliases=aliases or {},
        compiler_params=pltpu.CompilerParams(vmem_limit_bytes=megabytes << 20),
        name=name,
    )
    return lambda *args: call(*args, *tokens)


def normal(values):
    centre = jnp.mean(values, axis=-1, keepdims=True)
    moved = values - centre
    scale = lax.rsqrt(jnp.mean(moved * moved, axis=-1, keepdims=True) + 1e-05)
    return moved * scale, scale


def normal_back(grad, gain, xhat, scale):
    g = grad * gain
    return scale * (
        g - jnp.mean(g, axis=-1, keepdims=True) - xhat * jnp.mean(g * xhat, axis=-1, keepdims=True)
    )


def total(refs):
    value = refs[0][...].astype(F32)
    for ref in refs[1:]:
        value = value + ref[...].astype(F32)
    return value


def norm_body(x_ref, gain_ref, bias_ref, out_ref):
    for at in tiles(x_ref.shape[0]):
        xhat, _ = normal(x_ref[at, :].astype(F32))
        out_ref[at, :] = (xhat * gain_ref[...] + bias_ref[...]).astype(BF)


def norm_one(x, gain, bias):
    call = kernel(norm_body, "norm_one", shape(x.shape[0], D, BF), [vmem()] * 3, 4)
    return call(x, gain, bias)


def total(refs, at):
    value = refs[0][at, :].astype(F32)
    for ref in refs[1:]:
        value = value + ref[at, :].astype(F32)
    return value


def middle_body(*refs):
    x_ref, gain_ref, bias_ref = refs[:3]
    parts = refs[3:-3]
    middle_ref, out_ref, square_ref = refs[-3:]
    for at in tiles(x_ref.shape[0]):
        attended = total(parts, at)
        middle = x_ref[at, :].astype(F32) + attended
        middle_ref[at, :] = middle.astype(BF)
        xhat, _ = normal(middle)
        out_ref[at, :] = (xhat * gain_ref[...] + bias_ref[...]).astype(BF)
        square_ref[at, :] = jnp.sum(attended * attended, axis=-1, keepdims=True)


def norm_two(x, gain, bias, parts):
    rows = x.shape[0]
    call = kernel(
        middle_body, "norm_two", (shape(rows, D, BF), shape(rows, D, BF), shape(rows, 1, F32)),
        [vmem()] * (3 + len(parts)), 4,
    )
    return call(x, gain, bias, *parts)


def middle_back_body(*refs):
    grad_ref, middle_ref, gain_ref = refs[:3]
    parts = refs[3:-3]
    low_ref, gain_grad_ref, bias_grad_ref = refs[-3:]
    gain_grad = bias_grad = jnp.zeros(gain_ref.shape, F32)
    for at in tiles(grad_ref.shape[0]):
        grad = total(parts, at)
        xhat, scale = normal(middle_ref[at, :].astype(F32))
        gain_grad = gain_grad + jnp.sum(grad * xhat, axis=0, keepdims=True)
        bias_grad = bias_grad + jnp.sum(grad, axis=0, keepdims=True)
        out = grad_ref[at, :].astype(F32) + normal_back(grad, gain_ref[...], xhat, scale)
        low_ref[at, :] = out.astype(BF)
    gain_grad_ref[...] = gain_grad
    bias_grad_ref[...] = bias_grad


def norm_two_back(grad, middle, gain, parts, tokens):
    rows = grad.shape[0]
    call = kernel(
        middle_back_body, "norm_two_back",
        (shape(rows, D, BF), shape(1, D, F32), shape(1, D, F32)),
        [vmem()] * (3 + len(parts)), 9, tokens=tokens,
    )
    return call(grad, middle, gain, *parts)


def pixels_back_body(*refs):
    x_ref, wide_ref, gain_ref = refs[:3]
    parts = refs[3:-3]
    out_ref, gain_grad_ref, bias_grad_ref = refs[-3:]
    gain_grad = bias_grad = jnp.zeros(gain_ref.shape, F32)
    for at in tiles(x_ref.shape[0]):
        grad = total(parts, at)
        xhat, scale = normal(x_ref[at, :].astype(F32))
        gain_grad = gain_grad + jnp.sum(grad * xhat, axis=0, keepdims=True)
        bias_grad = bias_grad + jnp.sum(grad, axis=0, keepdims=True)
        out_ref[at, :] = (wide_ref[at, :].astype(F32) + normal_back(grad, gain_ref[...], xhat, scale)).astype(BF)
    gain_grad_ref[...] = gain_grad
    bias_grad_ref[...] = bias_grad


def norm_one_back(x, wide, gain, parts):
    rows = x.shape[0]
    call = kernel(
        pixels_back_body, "norm_one_back", (shape(rows, D, BF), shape(1, D, F32), shape(1, D, F32)),
        [vmem()] * (3 + len(parts)), 9,
    )
    return call(x, wide, gain, *parts)


def result_body(*refs):
    middle_ref = refs[0]
    parts = refs[1:-3]
    out_ref, result_square_ref, branch_square_ref = refs[-3:]
    for at in tiles(middle_ref.shape[0]):
        branch = total(parts, at)
        result = middle_ref[at, :].astype(F32) + branch
        out_ref[at, :] = result.astype(BF)
        result_square_ref[at, :] = jnp.sum(result * result, axis=-1, keepdims=True)
        branch_square_ref[at, :] = jnp.sum(branch * branch, axis=-1, keepdims=True)


def finish(middle, parts, tokens):
    rows = middle.shape[0]
    call = kernel(
        result_body, "finish", (shape(rows, D, BF), shape(rows, 1, F32), shape(rows, 1, F32)),
        [vmem()] * (1 + len(parts)), 4, tokens=tokens,
    )
    return call(middle, *parts)


def decode(code):
    return code >> 1, (code & 1).astype(F32)


def pair_slices(pair, rows):
    for i in range(2):
        yield i, slice(i * rows, (i + 1) * rows), slice((2 * pair + i) * rows, (2 * pair + i + 1) * rows)


def qkv_body(pair, tail_ref, xa_ref, xb_ref, w_ref, code_ref, was_ref, *rest):
    q_ref, k_ref, v_ref, pack_ref = rest[-4:]
    width = q_ref.shape[1]
    block = same_head(width)
    state, sums = was_ref[0:HEAD, :], was_ref[HEAD:PACK, :]
    for i, _, at in pair_slices(pair, xa_ref.shape[0]):
        x = (xa_ref, xb_ref)[i][...]
        q_ref[at, :] = feature(nn(x, w_ref[0])).astype(BF)
        segment, valid = decode(code_ref[at, :])
        k = (feature(nn(x, w_ref[1])) * valid).astype(BF)
        v = nn(x, w_ref[2]).astype(BF)
        k_ref[at, :] = k
        v_ref[at, :] = v
        kept = pick(segment == tail_ref[0], k)
        state = state + fold_heads(pick(block, tn(kept, v)), width)
        sums = sums + jnp.sum(kept.astype(F32), axis=0, keepdims=True)
    pack_ref[0:HEAD, :] = state
    pack_ref[HEAD:PACK, :] = sums


def project_qkv(pair, tail, xa, xb, w, code, was, made):
    width, whole = w.shape[2], code.shape[0]
    call = kernel(
        functools.partial(qkv_body, pair), "project_qkv",
        (shape(whole, width, BF),) * 3 + (shape(PACK, width, F32),),
        [smem()] + [vmem()] * (5 + len(made)), 8,
        aliases={6 + i: i for i in range(len(made))},
    )
    return call(tail, xa, xb, w, code, was, *made)


def swap_heads(x):
    return jnp.concatenate(
        [pltpu.roll(x[:, i : i + 2 * HEAD], HEAD, 1) for i in range(0, x.shape[1], 2 * HEAD)], axis=1
    )


def forward_body(
    last_ref, spot_ref, q_ref, k_ref, v_ref, code_ref, segr_ref, num_ref, den_ref, st_ref, ks_ref
):
    rows, width = q_ref.shape
    size = CHUNK
    block = same_head(width)
    ones_block = block.astype(BF)
    lanes = lane_head(size, width)
    even = (lanes % 2) == 0
    lower = causal(size)
    st_ref[...] = jnp.zeros_like(st_ref)
    ks_ref[...] = jnp.zeros_like(ks_ref)

    def step(c, carry):
        spot = spot_ref[c]
        at = pl.ds(pl.multiple_of(spot * size, size), size)
        q, k, v = q_ref[at, :], k_ref[at, :], v_ref[at, :]
        seg = decode(code_ref[at, :])[0]
        keep = (lower & (seg == segr_ref[spot])).astype(BF)
        before, after = last_ref[c], last_ref[c + 1]
        carried = (seg == before).astype(F32)
        sums = [jnp.zeros((size, width), F32)] * 2
        for h in range(width // HEAD):
            mine = lanes == h
            score = nt(pick(mine, q), k).astype(BF) * keep
            both = jnp.where(mine, v, (lanes == (h ^ 1)).astype(BF))
            sums[h % 2] = sums[h % 2] + nn(score, both)
        num = jnp.where(even, sums[0], sums[1])
        den = swap_heads(jnp.where(even, sums[1], sums[0]))
        num_ref[at, :] = num + carried * nn(q, st_ref[...].astype(BF))
        den_ref[at, :] = den + carried * nn((q.astype(F32) * ks_ref[0:1, :]).astype(BF), ones_block)
        kept = pick(seg == after, k)
        cont = (before == after).astype(F32)
        st_ref[...] = cont * st_ref[...] + pick(block, tn(kept, v))
        ks_ref[...] = cont * ks_ref[...] + jnp.sum(kept.astype(F32), axis=0, keepdims=True)
        return carry

    lax.fori_loop(0, rows // size, step, 0)


def attend(last, spot, q, k, v, code, segr):
    rows, width = q.shape
    call = kernel(
        forward_body, "attend", (shape(rows, width, F32),) * 2, [smem()] * 2 + [vmem()] * 5, 8,
        scratch=[pltpu.VMEM((width, width), F32), pltpu.VMEM((8, width), F32)],
    )
    return call(last, spot, q, k, v, code, segr)


def project_body(
    pair, first_ref, num_ref, den_ref, q_ref, pack_ref, code_ref, w_ref,
    heads_ref, rinv_ref, a_ref, b_ref
):
    width = q_ref.shape[1]
    block = same_head(width)
    state = spread_heads(pack_ref[0:HEAD, :], width, block).astype(BF)
    sums = pack_ref[HEAD : HEAD + 1, :]
    for i, own, at in pair_slices(pair, a_ref.shape[0]):
        q = q_ref[at, :]
        segment, valid = decode(code_ref[at, :])
        opening = (segment == first_ref[0]).astype(F32)
        num = num_ref[at, :] + opening * nn(q, state)
        den = den_ref[at, :] + opening * nn((q.astype(F32) * sums).astype(BF), block.astype(BF))
        rinv = valid / (den + 1e-06 + 1.0 - valid)
        heads = (num * rinv).astype(BF)
        heads_ref[own, :] = heads
        rinv_ref[own, :] = rinv.astype(BF)
        (a_ref, b_ref)[i][...] = nn(heads, w_ref[...]).astype(BF)


def project(pair, rows, last, num, den, q, pack, code, w, tokens):
    width = q.shape[1]
    call = kernel(
        functools.partial(project_body, pair), "project",
        (shape(2 * rows, width, BF),) * 2 + (shape(rows, D, BF),) * 2,
        [smem()] + [vmem()] * 6, 8, tokens=tokens,
    )
    return call(last, num, den, q, pack, code, w)


def mlp_body(
    xa_ref, xb_ref, ga_ref, gb_ref, up_ref, down_ref, act_ref, hid_ref, na_ref, nb_ref, ba_ref, bb_ref
):
    root = 0.7978845608028654
    tile = min(512, up_ref.shape[1])
    for i, own, _ in pair_slices(0, xa_ref.shape[0]):
        x, g = (xa_ref, xb_ref)[i][...], (ga_ref, gb_ref)[i][...]
        for j in range(0, up_ref.shape[1], tile):
            cols = slice(j, j + tile)
            h = nn(x, up_ref[:, cols])
            grad = nt(g, down_ref[cols, :])
            square = h * h
            t = jnp.tanh(root * h * (1.0 + 0.044715 * square))
            plus = 0.5 * (1.0 + t)
            slope = plus + 0.5 * h * (1.0 - t * t) * (root + (3.0 * 0.044715 * root) * square)
            act_ref[own, cols] = (h * plus).astype(BF)
            hid_ref[own, cols] = (grad * slope).astype(BF)
        (na_ref, nb_ref)[i][...] = nt(hid_ref[own, :], up_ref[...]).astype(BF)
        (ba_ref, bb_ref)[i][...] = nn(act_ref[own, :], down_ref[...]).astype(BF)


def mlp(xa, xb, ga, gb, up, down):
    rows, hidden = xa.shape[0], up.shape[1]
    call = kernel(
        mlp_body, "mlp", (shape(2 * rows, hidden, BF),) * 2 + (shape(rows, D, BF),) * 4,
        [vmem()] * 6, 9,
    )
    return call(xa, xb, ga, gb, up, down)


def heads_back_body(
    pair, first_ref, ga_ref, gb_ref, w_ref, heads_ref, rinv_ref, q_ref, code_ref, was_ref, *rest
):
    ng_ref, dg_ref, pack_ref = rest[-3:]
    width = q_ref.shape[1]
    block = same_head(width)
    ones_block = block.astype(BF)
    state, sums = was_ref[0:HEAD, :], was_ref[HEAD:PACK, :]
    for i, own, at in pair_slices(pair, ga_ref.shape[0]):
        hg = nt((ga_ref, gb_ref)[i][...], w_ref[...])
        rinv = rinv_ref[own, :].astype(F32)
        ng = (hg * rinv).astype(BF)
        prod = hg * heads_ref[own, :].astype(F32)
        high = prod.astype(BF)
        low = (prod - high.astype(F32)).astype(BF)
        dg = -(nn(high, ones_block) + nn(low, ones_block)) * rinv
        ng_ref[at, :] = ng
        dg_ref[at, :] = dg
        opened = pick(decode(code_ref[at, :])[0] == first_ref[0], q_ref[at, :])
        state = state + fold_heads(pick(block, tn(opened, ng)), width)
        sums = sums + jnp.sum(opened.astype(F32) * dg, axis=0, keepdims=True)
    pack_ref[0:HEAD, :] = state
    pack_ref[HEAD:PACK, :] = sums


def heads_back(pair, last, ga, gb, w, heads, rinv, q, code, was, made, tokens=()):
    whole, width = q.shape
    call = kernel(
        functools.partial(heads_back_body, pair), "heads_back",
        (shape(whole, width, BF), shape(whole, width, F32), shape(PACK, width, F32)),
        [smem()] + [vmem()] * (8 + len(made)), 5,
        aliases={9 + i: i for i in range(len(made))}, tokens=tokens,
    )
    return call(last, ga, gb, w, heads, rinv, q, code, was, *made)


def backward_body(
    last_ref, spot_ref, q_ref, k_ref, v_ref, ng_ref, dg_ref, code_ref, segr_ref, pack_ref,
    dq_ref, dk_ref, dv_ref, all_ref, sums_ref, st_ref, ks_ref
):
    rows, width = q_ref.shape
    size = CHUNK
    count = rows // size
    block = same_head(width)
    lanes = lane_head(size, width)
    half = (lax.broadcasted_iota(jnp.int32, (size, width), 1) % HEAD) < HEAD // 2
    lower = causal(size)
    st_ref[...] = spread_heads(pack_ref[0:HEAD, :], width, block)
    ks_ref[...] = jnp.broadcast_to(pack_ref[HEAD : HEAD + 1, :], ks_ref.shape)

    def collect(c, carry):
        at = pl.ds(pl.multiple_of(spot_ref[c] * size, size), size)
        all_ref[c] = st_ref[...].astype(BF)
        sums_ref[c] = ks_ref[...]
        before, after = last_ref[c], last_ref[c + 1]
        kept = pick(decode(code_ref[at, :])[0] == after, k_ref[at, :])
        cont = (before == after).astype(F32)
        st_ref[...] = cont * st_ref[...] + pick(block, tn(kept, v_ref[at, :]))
        ks_ref[...] = cont * ks_ref[...] + jnp.sum(kept.astype(F32), axis=0, keepdims=True)
        return carry

    lax.fori_loop(0, count, collect, 0)
    st_ref[...] = jnp.zeros_like(st_ref)
    ks_ref[...] = jnp.zeros_like(ks_ref)

    def step(i, carry):
        c = count - 1 - i
        spot = spot_ref[c]
        at = pl.ds(pl.multiple_of(spot * size, size), size)
        q, k, v, ng, dg = q_ref[at, :], k_ref[at, :], v_ref[at, :], ng_ref[at, :], dg_ref[at, :]
        seg = decode(code_ref[at, :])[0]
        keep = (lower & (seg == segr_ref[spot])).astype(BF)
        before, after = last_ref[c], last_ref[c + 1]
        opened = seg == before
        carried = opened.astype(F32)
        tail = (seg == after).astype(F32)
        grad_state = st_ref[...].astype(BF)
        moved = swap_heads(dg)
        high = moved.astype(BF)
        low = (moved - high.astype(F32)).astype(BF)
        terms = jnp.where(half, high, low) * jnp.asarray(2.0 / HEAD, BF)
        one = jnp.ones((), BF)
        dq = carried * (nt(ng, all_ref[c]) + dg * sums_ref[c][0:1, :])
        dk = tail * (nt(v, grad_state) + ks_ref[0:1, :])
        dv = tail * nn(k, grad_state)
        for h in range(width // HEAD):
            mine = lanes == h
            qh, kh, nh = pick(mine, q), pick(mine, k), pick(mine, ng)
            score = nt(qh, k).astype(BF) * keep
            left = jnp.where(mine, ng, pick(lanes == (h ^ 1), terms))
            back = nt(left, jnp.where(mine, v, one)).astype(BF) * keep
            dq = dq + nn(back, kh)
            dk = dk + tn(back, qh)
            dv = dv + tn(score, nh)
        dq_ref[at, :] = (dq * jnp.minimum(q.astype(F32), 1.0)).astype(BF)
        dk_ref[at, :] = dk.astype(BF)
        dv_ref[at, :] = dv.astype(BF)
        cont = (before == after).astype(F32)
        st_ref[...] = cont * st_ref[...] + pick(block, tn(pick(opened, q), ng))
        ks_ref[...] = cont * ks_ref[...] + jnp.sum(carried * q.astype(F32) * dg, axis=0, keepdims=True)
        return carry

    lax.fori_loop(0, count, step, 0)


def attend_back(last, spot, q, k, v, ng, dg, code, segr, pack, tokens):
    rows, width = q.shape
    count = rows // CHUNK
    call = kernel(
        backward_body, "attend_back",
        (shape(rows, width, BF),) * 3,
        [smem()] * 2 + [vmem()] * 8, 12,
        scratch=[
            pltpu.VMEM((count, width, width), BF),
            pltpu.VMEM((count, 8, width), F32),
            pltpu.VMEM((width, width), F32),
            pltpu.VMEM((8, width), F32),
        ],
        tokens=tokens,
    )
    return call(last, spot, q, k, v, ng, dg, code, segr, pack)


def mix_body(
    pair, tail_ref, dq_ref, dk_ref, dv_ref, k_ref, v_ref, code_ref, pack_ref, w_ref,
    mixed_ref, a_ref, b_ref
):
    width = k_ref.shape[1]
    block = same_head(width)
    state = spread_heads(pack_ref[0:HEAD, :], width, block).astype(BF)
    sums = pack_ref[HEAD : HEAD + 1, :]
    for i, own, at in pair_slices(pair, a_ref.shape[0]):
        tail = (decode(code_ref[at, :])[0] == tail_ref[0]).astype(F32)
        k = k_ref[at, :]
        dk = dk_ref[at, :].astype(F32) + tail * (nt(v_ref[at, :], state) + sums)
        dv = dv_ref[at, :].astype(F32) + tail * nn(k, state)
        dq = dq_ref[at, :]
        dk = (dk * jnp.minimum(k.astype(F32), 1.0)).astype(BF)
        dv = dv.astype(BF)
        mixed_ref[own, 0:width] = dq
        mixed_ref[own, width : 2 * width] = dk
        mixed_ref[own, 2 * width : 3 * width] = dv
        out = nt(dq, w_ref[0]) + nt(dk, w_ref[1]) + nt(dv, w_ref[2])
        (a_ref, b_ref)[i][...] = out.astype(BF)


def mix(pair, rows, tail, dq, dk, dv, k, v, code, pack, w, tokens):
    width = k.shape[1]
    call = kernel(
        functools.partial(mix_body, pair), "mix",
        (shape(2 * rows, 3 * width, BF),) + (shape(rows, D, BF),) * 2,
        [smem()] + [vmem()] * 8, 8, tokens=tokens,
    )
    return call(tail, dq, dk, dv, k, v, code, pack, w)


def feature(values):
    return jnp.where(values > 0, values + 1.0, jnp.exp(jnp.minimum(values, 0.0)))


def bits_of(count):
    return [1 << b for b in range(count.bit_length() - 1)]


def swap(value, axis, bit):
    return lax.ppermute(value, axis, [(i, i ^ bit) for i in range(lax.axis_size(axis))])


def after(value, *tokens):
    return lax.optimization_barrier((value, *tokens))[0] if tokens else value


def gather_begin(value):
    slots = {0: value}
    for bit in reversed(bits_of(lax.axis_size("feat"))[1:]):
        for s in sorted(slots):
            slots[s | bit] = swap(slots[s], "feat", bit)
    slots[1] = swap(value, "feat", 1)
    return slots


def gather_end(slots, *tokens):
    for s in range(2, lax.axis_size("feat"), 2):
        slots[s + 1] = swap(after(slots[s], *tokens), "feat", 1)
    return [slots[s] for s in range(len(slots))]


def scatter_begin(parts):
    sums = {}
    for s in range(len(parts) - 2, -1, -2):
        got = swap(parts[s + 1], "feat", 1)
        sums[s] = (parts[s].astype(F32) + got.astype(F32)).astype(BF) if s else [parts[0], got]
    return sums


def scatter_end(sums, *tokens):
    sums = {s: part if s == 0 else [after(part, *tokens)] for s, part in sums.items()}
    for bit in bits_of(lax.axis_size("feat"))[1:]:
        for s in sorted(sums, reverse=True):
            if s & bit:
                pieces = sums.pop(s)
                value = pieces[0]
                if len(pieces) > 1:
                    value = functools.reduce(jnp.add, [p.astype(F32) for p in pieces]).astype(BF)
                sums[s ^ bit].append(swap(value, "feat", bit))
    return sums[0]


def sum_everywhere(value):
    for axis in ("feat", "rows"):
        for bit in bits_of(lax.axis_size(axis)):
            value = value + swap(value, axis, bit)
    return value


class RowSum:
    def __init__(self, value, order, *tokens):
        self.order, self.step = order, 0
        self.value = after(value, *tokens)
        self.launch()

    def launch(self):
        count = len(self.order)
        halving = self.step < count
        bit = self.order[self.step] if halving else self.order[2 * count - 1 - self.step]
        self.upper = (lax.axis_index("rows") & bit) != 0
        self.sent = self.kept = self.value
        if halving:
            half = self.value.shape[0] // 2
            low, high = self.value[:half], self.value[half:]
            self.sent = jnp.where(self.upper, low, high)
            self.kept = jnp.where(self.upper, high, low)
        self.got = swap(self.sent, "rows", bit)

    def next(self, *tokens):
        got = after(self.got, *tokens)
        if self.step < len(self.order):
            self.value = (self.kept.astype(F32) + got.astype(F32)).astype(BF)
        else:
            first = jnp.where(self.upper, got, self.kept)
            self.value = jnp.concatenate([first, jnp.where(self.upper, self.kept, got)], axis=0)
        self.step += 1
        if self.step < 2 * len(self.order):
            self.launch()
            return self.sent
        return self.value

    def finish(self, *tokens):
        while self.step < 2 * len(self.order):
            self.next(*tokens)
        return self.value


def shifted(pack, hop, groups, reverse):
    if reverse:
        pairs = [(i, i - hop) for i in range(hop, groups)]
    else:
        pairs = [(i, i + hop) for i in range(groups - hop)]
    return lax.ppermute(pack, "rows", pairs)


def gather_carry(pack, crops_at, here, groups, reach, reverse):
    total = jnp.zeros(pack.shape, F32)
    mine = crops_at[here + 1] if reverse else crops_at[here]
    for hop in range(1, reach + 1):
        got = shifted(pack, hop, groups, reverse).astype(F32)
        other = here + hop if reverse else here - hop
        inside = (other < groups) if reverse else (other >= 0)
        at = jnp.clip(other, 0, groups - 1)
        theirs = crops_at[at] if reverse else crops_at[at + 1]
        total = total + jnp.where(inside & (theirs == mine), got, 0.0)
    return total


def on_device(
    pixels,
    qkv_weight,
    out_weight,
    up_weight,
    down_weight,
    norm1_gain,
    norm1_bias,
    norm2_gain,
    norm2_bias,
    crop_lengths,
    crop_offsets,
    pixel_mask,
    out_grad,
):
    local_rows = pixels.shape[0]
    group_rows = pixel_mask.shape[0]
    width = qkv_weight.shape[2]
    crop_count = crop_offsets.shape[0]
    groups = lax.axis_size("rows")
    members = lax.axis_size("feat")
    pairs = members // 2
    here = lax.axis_index("rows")
    member = lax.axis_index("feat")
    reach = min(groups - 1, -(-(CROP_MAX - 1) // group_rows))
    group_start = here * group_rows
    slot_ids = jnp.arange(members, dtype=jnp.int32) ^ member
    in_group = (slot_ids[:, None] * local_rows + jnp.arange(local_rows, dtype=jnp.int32)[None, :]).reshape(-1)
    places = group_start + in_group
    started = crop_offsets[None, :] <= places[:, None]
    crop_ends = crop_offsets + crop_lengths
    segment = jnp.sum(started.astype(jnp.int32), axis=1) - 1
    inside = jnp.sum((started & (places[:, None] < crop_ends[None, :])).astype(jnp.int32), axis=1)
    mask = jnp.concatenate(
        [
            lax.dynamic_slice_in_dim(pixel_mask, (member ^ s) * local_rows, local_rows)
            for s in range(members)
        ]
    )
    pixel_valid = (mask * inside).astype(F32)
    edges = jnp.arange(groups + 1, dtype=jnp.int32) * group_rows - 1
    crops_at = jnp.sum((crop_offsets[None, :] <= edges[:, None]).astype(jnp.int32), axis=1) - 1
    chunks = group_rows // CHUNK
    per = local_rows // CHUNK
    chunk_edges = group_start - 1 + jnp.arange(chunks + 1, dtype=jnp.int32) * CHUNK
    last = jnp.sum((crop_offsets[None, :] <= chunk_edges[:, None]).astype(jnp.int32), axis=1) - 1
    tail = last[-1:]
    order = jnp.arange(chunks, dtype=jnp.int32)
    spot = ((order // per) ^ member) * per + order % per
    code = (segment * 2 + mask * inside)[:, None]
    segr = segment.reshape(chunks, 1, CHUNK)
    validc = pixel_valid[:, None]
    gain1, bias1, gain2, bias2 = (
        a[None, :] for a in (norm1_gain, norm1_bias, norm2_gain, norm2_bias)
    )
    no_pack = jnp.zeros((PACK, width), F32)

    normed_slots = gather_begin(norm_one(pixels, gain1, bias1))
    grad_slots = gather_begin(after(out_grad, normed_slots[members // 2]))
    *made, pack = project_qkv(0, tail, normed_slots[0], normed_slots[1], qkv_weight, code, no_pack, ())
    normed_slots = gather_end(normed_slots, pack)
    for p in range(1, pairs):
        *made, pack = project_qkv(
            p, tail, normed_slots[2 * p], normed_slots[2 * p + 1], qkv_weight, code, pack, made
        )
    q, k, v = made
    carry = gather_carry(pack.astype(BF), crops_at, here, groups, reach, False)
    num, den = attend(last, spot, q, k, v, code, segr)
    grad_slots = gather_end(grad_slots, num)
    sent = {
        p: project(
            p, local_rows, last, num, den, q, carry, code, out_weight, [grad_slots[members // 2]]
        )
        for p in reversed(range(pairs))
    }
    parts = scatter_end(scatter_begin([sent[s // 2][2 + s % 2] for s in range(members)]))
    middle, normed_two, attended_square = norm_two(pixels, gain2, bias2, parts)
    two_slots = gather_begin(normed_two)
    hidden = [mlp(two_slots[0], two_slots[1], grad_slots[0], grad_slots[1], up_weight, down_weight)]
    two_slots = gather_end(two_slots, hidden[0][0])
    for p in range(1, pairs):
        hidden.append(mlp(*two_slots[2 * p : 2 * p + 2], *grad_slots[2 * p : 2 * p + 2], up_weight, down_weight))
    two_sums = scatter_begin([hidden[s // 2][2 + s % 2] for s in range(members)])
    two_parts = scatter_end(two_sums)
    branch_sums = scatter_begin([hidden[s // 2][4 + s % 2] for s in range(members)])
    acts, hids, twos = after(
        ([h[0] for h in hidden], [h[1] for h in hidden], two_slots), two_sums[members - 2]
    )
    down_grad = tn(jnp.concatenate(acts, axis=0), jnp.concatenate(grad_slots, axis=0)).astype(BF)
    up_grad = tn(jnp.concatenate(twos, axis=0), jnp.concatenate(hids, axis=0)).astype(BF)
    bits = bits_of(groups)
    turned = bits[1:] + bits[:1]
    both = jnp.concatenate([down_grad, up_grad.reshape(-1, D)], axis=0)
    both = lax.psum_scatter(after(both, two_parts[-1]), "rows", scatter_dimension=0, tiled=True)
    middle_low, gain2_grad, bias2_grad = norm_two_back(
        out_grad, middle, gain2, two_parts,
        [down_grad, up_grad, branch_sums[0][1], branch_sums[members - 2]],
    )
    middle_slots = gather_begin(middle_low)
    *made, grad_pack = heads_back(
        0, last, middle_slots[0], middle_slots[1], out_weight, sent[0][0], sent[0][1], q, code, no_pack, ()
    )
    branch_parts = scatter_end(branch_sums, middle_slots[members // 2], grad_pack)
    middle_slots = gather_end(middle_slots, grad_pack)
    for p in range(1, pairs):
        *made, grad_pack = heads_back(
            p, last, middle_slots[2 * p], middle_slots[2 * p + 1], out_weight,
            sent[p][0], sent[p][1], q, code, grad_pack, made
        )
    ng, dg = made
    grad_carry = gather_carry(grad_pack.astype(BF), crops_at, here, groups, reach, True)
    dq, dk, dv = attend_back(last, spot, q, k, v, ng, dg, code, segr, carry, [])
    mixes = {
        p: mix(p, local_rows, tail, dq, dk, dv, k, v, code, grad_carry, qkv_weight, [])
        for p in reversed(range(pairs))
    }
    normed_sums = scatter_begin([mixes[s // 2][1 + s % 2] for s in range(members)])
    normed_parts = scatter_end(normed_sums)
    mixed_grad = jnp.concatenate([mixes[p][0] for p in range(pairs)], axis=0)
    qkv_grad = tn(mixed_grad, jnp.concatenate(normed_slots, axis=0)).astype(BF)
    both = lax.all_gather(after(both, dq), "rows", axis=0, tiled=True)
    down_grad = both[: down_grad.shape[0]].astype(F32)
    up_grad = both[down_grad.shape[0] :].reshape(up_grad.shape).astype(F32)
    cut = 3 * width // 2
    low_sum = RowSum(qkv_grad[:cut], bits)
    high_sum = RowSum(qkv_grad[cut:], turned)
    normed_sent = normed_sums[members - 2]
    heads_all = jnp.concatenate([sent[p][0] for p in range(pairs)], axis=0)
    out_weight_grad = tn(after(heads_all, low_sum.sent, normed_sent), jnp.concatenate(middle_slots, axis=0))
    out_sum = RowSum(out_weight_grad.astype(BF), turned)
    tokens = [low_sum.next(normed_sent), high_sum.next(normed_sent)]
    output, result_square, branch_square = finish(middle, branch_parts, tokens)
    pixels_grad, gain1_grad, bias1_grad = norm_one_back(pixels, middle_low, gain1, normed_parts)
    tokens = [out_sum.next(*tokens)]
    tokens = [low_sum.next(*tokens), high_sum.next(*tokens)]
    out_weight_grad = out_sum.finish(*tokens).astype(F32)
    qkv_grad = jnp.concatenate([low_sum.finish(), high_sum.finish()], axis=0)
    qkv_grad = jnp.swapaxes(qkv_grad.reshape(3, width, D), 1, 2).astype(F32)

    crop_onehot = (
        segment[:local_rows, None] == jnp.arange(crop_count, dtype=jnp.int32)[None, :]
    ).astype(F32)
    squares = (
        jnp.concatenate(
            [result_square, attended_square, branch_square, jnp.ones((local_rows, 1), F32)], axis=1
        )
        * validc[:local_rows]
    )
    crop_sums = lax.dot_general(
        squares, crop_onehot, (((0,), (0,)), ((), ())), precision=precise, preferred_element_type=F32
    )
    sums = jnp.concatenate(
        [gain1_grad[0], bias1_grad[0], gain2_grad[0], bias2_grad[0], crop_sums.reshape(-1)]
    )
    sums = sum_everywhere(sums)
    gain1_grad, bias1_grad, gain2_grad, bias2_grad = sums[: 4 * D].reshape(4, D)
    crop_sums = sums[4 * D :].reshape(4, crop_count)
    crop_rms = jnp.sqrt(crop_sums[:3] / (D * jnp.maximum(crop_sums[3], 1.0))[None, :])
    return (
        output,
        pixels_grad,
        qkv_grad,
        out_weight_grad,
        up_grad,
        down_grad,
        gain1_grad,
        bias1_grad,
        gain2_grad,
        bias2_grad,
        crop_rms,
    )


def solution(mesh):
    split = P(("rows", "feat"), None)
    qkv, rows_feat, cols_feat = P(None, None, "feat"), P("feat", None), P(None, "feat")
    in_specs = (
        (split, qkv, rows_feat, cols_feat, rows_feat) + (P(),) * 6 + (P("rows"), split)
    )
    out_specs = (split, split, qkv, rows_feat, cols_feat, rows_feat) + (P(),) * 5
    return jax.shard_map(
        on_device, mesh=mesh, in_specs=in_specs, out_specs=out_specs, check_vma=False
    )
```

```python
import functools

import jax
import jax.numpy as jnp
from jax import lax
from jax.experimental import pallas as pl
from jax.experimental.pallas import tpu as pltpu
from jax.sharding import PartitionSpec as P

D = 1024
HEAD = 64
CROP_MAX = 3072
PACK = HEAD + 16

BF = jnp.bfloat16
F32 = jnp.float32
precise = lax.Precision.HIGHEST


def nn(a, b):
    return lax.dot_general(a, b, (((1,), (0,)), ((), ())), preferred_element_type=F32)


def nt(a, b):
    return lax.dot_general(a, b, (((1,), (1,)), ((), ())), preferred_element_type=F32)


def tn(a, b):
    return lax.dot_general(a, b, (((0,), (0,)), ((), ())), preferred_element_type=F32)


def same_head(width):
    row = lax.broadcasted_iota(jnp.int32, (width, width), 0) // HEAD
    col = lax.broadcasted_iota(jnp.int32, (width, width), 1) // HEAD
    return row == col


def lane_head(rows, width):
    return lax.broadcasted_iota(jnp.int32, (rows, width), 1) // HEAD


def causal(rows):
    row = lax.broadcasted_iota(jnp.int32, (rows, rows), 0)
    col = lax.broadcasted_iota(jnp.int32, (rows, rows), 1)
    return row >= col


def fold_heads(full, width):
    out = full[0:HEAD]
    for h in range(1, width // HEAD):
        out = out + full[h * HEAD : (h + 1) * HEAD]
    return out


def spread_heads(part, width, block):
    tall = jnp.concatenate([part] * (width // HEAD), axis=0)
    return jnp.where(block, tall, jnp.zeros_like(tall))


def pick(mask, value):
    return jnp.where(mask, value, jnp.zeros_like(value))


def vmem():
    return pl.BlockSpec(memory_space=pltpu.VMEM)


def smem():
    return pl.BlockSpec(memory_space=pltpu.SMEM)


def shape(rows, cols, kind):
    return jax.ShapeDtypeStruct((rows, cols), kind)


ROW_TILE = 192


def tiles(rows):
    return [slice(i, i + ROW_TILE) for i in range(0, rows, ROW_TILE)]


class Incoming:
    def __init__(self, buffer, copy):
        self.buffer, self.copy, self.shape = buffer, copy, buffer.shape
        copy.start()

    def here(self):
        if self.copy is not None:
            self.copy.wait()
            self.copy = None
        return self.buffer

    def __getitem__(self, index):
        return self.here()[index]


def kernel(body, name, out_shape, in_specs, megabytes, scratch=(), aliases=None, tokens=(), far=()):
    outs = vmem() if not isinstance(out_shape, tuple) else (vmem(),) * len(out_shape)
    made = 1 if not isinstance(out_shape, tuple) else len(out_shape)
    count = len(in_specs)
    specs = [pl.BlockSpec(memory_space=pl.ANY) if i in far else spec for i, spec in enumerate(in_specs)]
    skip = pl.BlockSpec(memory_space=pl.ANY)

    def call(*args):
        buffers = [pltpu.VMEM(args[i].shape, args[i].dtype) for i in far]

        def run(*refs):
            given = list(refs[:count])
            rest = refs[count + len(tokens) :]
            results, own, copied = rest[:made], rest[made : made + len(scratch)], rest[made + len(scratch) :]
            arriving = []
            for n, i in enumerate(far):
                given[i] = Incoming(copied[n], pltpu.make_async_copy(given[i], copied[n], copied[-1].at[n]))
                arriving.append(given[i])
            body(*given, *results, *own)
            for value in arriving:
                value.here()

        sems = [pltpu.SemaphoreType.DMA((len(far),))] if far else []
        return pl.pallas_call(
            run,
            out_shape=out_shape,
            in_specs=specs + [skip] * len(tokens),
            out_specs=outs,
            scratch_shapes=list(scratch) + buffers + sems,
            input_output_aliases=aliases or {},
            compiler_params=pltpu.CompilerParams(vmem_limit_bytes=(60 if far else megabytes) << 20),
            name=name,
        )(*args, *tokens)

    return call


def normal(values):
    centre = jnp.mean(values, axis=-1, keepdims=True)
    moved = values - centre
    scale = lax.rsqrt(jnp.mean(moved * moved, axis=-1, keepdims=True) + 1e-05)
    return moved * scale, scale


def normal_back(grad, gain, xhat, scale):
    g = grad * gain
    return scale * (
        g - jnp.mean(g, axis=-1, keepdims=True) - xhat * jnp.mean(g * xhat, axis=-1, keepdims=True)
    )


def total(refs):
    value = refs[0][...].astype(F32)
    for ref in refs[1:]:
        value = value + ref[...].astype(F32)
    return value


def norm_body(x_ref, gain_ref, bias_ref, out_ref):
    for at in tiles(x_ref.shape[0]):
        xhat, _ = normal(x_ref[at, :].astype(F32))
        out_ref[at, :] = (xhat * gain_ref[...] + bias_ref[...]).astype(BF)


def norm_one(x, gain, bias):
    call = kernel(norm_body, "norm_one", shape(x.shape[0], D, BF), [vmem()] * 3, 4)
    return call(x, gain, bias)


def total(refs, at):
    value = refs[0][at, :].astype(F32)
    for ref in refs[1:]:
        value = value + ref[at, :].astype(F32)
    return value


def middle_body(*refs):
    x_ref, gain_ref, bias_ref = refs[:3]
    parts = refs[3:-3]
    middle_ref, out_ref, square_ref = refs[-3:]
    for at in tiles(x_ref.shape[0]):
        attended = total(parts, at)
        middle = x_ref[at, :].astype(F32) + attended
        middle_ref[at, :] = middle.astype(BF)
        xhat, _ = normal(middle)
        out_ref[at, :] = (xhat * gain_ref[...] + bias_ref[...]).astype(BF)
        square_ref[at, :] = jnp.sum(attended * attended, axis=-1, keepdims=True)


def norm_two(x, gain, bias, parts):
    rows = x.shape[0]
    call = kernel(
        middle_body, "norm_two", (shape(rows, D, BF), shape(rows, D, BF), shape(rows, 1, F32)),
        [vmem()] * (3 + len(parts)), 4,
    )
    return call(x, gain, bias, *parts)


def middle_back_body(*refs):
    grad_ref, middle_ref, gain_ref = refs[:3]
    parts = refs[3:-3]
    low_ref, gain_grad_ref, bias_grad_ref = refs[-3:]
    gain_grad = bias_grad = jnp.zeros(gain_ref.shape, F32)
    for at in tiles(grad_ref.shape[0]):
        grad = total(parts, at)
        xhat, scale = normal(middle_ref[at, :].astype(F32))
        gain_grad = gain_grad + jnp.sum(grad * xhat, axis=0, keepdims=True)
        bias_grad = bias_grad + jnp.sum(grad, axis=0, keepdims=True)
        out = grad_ref[at, :].astype(F32) + normal_back(grad, gain_ref[...], xhat, scale)
        low_ref[at, :] = out.astype(BF)
    gain_grad_ref[...] = gain_grad
    bias_grad_ref[...] = bias_grad


def norm_two_back(grad, middle, gain, parts, tokens):
    rows = grad.shape[0]
    call = kernel(
        middle_back_body, "norm_two_back",
        (shape(rows, D, BF), shape(1, D, F32), shape(1, D, F32)),
        [vmem()] * (3 + len(parts)), 9, tokens=tokens, far=(0, 1) + tuple(range(3, 3 + len(parts))),
    )
    return call(grad, middle, gain, *parts)


def pixels_back_body(*refs):
    x_ref, wide_ref, gain_ref = refs[:3]
    parts = refs[3:-3]
    out_ref, gain_grad_ref, bias_grad_ref = refs[-3:]
    gain_grad = bias_grad = jnp.zeros(gain_ref.shape, F32)
    for at in tiles(x_ref.shape[0]):
        grad = total(parts, at)
        xhat, scale = normal(x_ref[at, :].astype(F32))
        gain_grad = gain_grad + jnp.sum(grad * xhat, axis=0, keepdims=True)
        bias_grad = bias_grad + jnp.sum(grad, axis=0, keepdims=True)
        out_ref[at, :] = (wide_ref[at, :].astype(F32) + normal_back(grad, gain_ref[...], xhat, scale)).astype(BF)
    gain_grad_ref[...] = gain_grad
    bias_grad_ref[...] = bias_grad


def norm_one_back(x, wide, gain, parts):
    rows = x.shape[0]
    call = kernel(
        pixels_back_body, "norm_one_back", (shape(rows, D, BF), shape(1, D, F32), shape(1, D, F32)),
        [vmem()] * (3 + len(parts)), 9,
    )
    return call(x, wide, gain, *parts)


def result_body(*refs):
    middle_ref = refs[0]
    parts = refs[1:-3]
    out_ref, result_square_ref, branch_square_ref = refs[-3:]
    for at in tiles(middle_ref.shape[0]):
        branch = total(parts, at)
        result = middle_ref[at, :].astype(F32) + branch
        out_ref[at, :] = result.astype(BF)
        result_square_ref[at, :] = jnp.sum(result * result, axis=-1, keepdims=True)
        branch_square_ref[at, :] = jnp.sum(branch * branch, axis=-1, keepdims=True)


def finish(middle, parts, tokens):
    rows = middle.shape[0]
    call = kernel(
        result_body, "finish", (shape(rows, D, BF), shape(rows, 1, F32), shape(rows, 1, F32)),
        [vmem()] * (1 + len(parts)), 4, tokens=tokens,
    )
    return call(middle, *parts)


def decode(row):
    code = jnp.broadcast_to(row, (128, row.shape[1])).T[:, 0:1]
    return code >> 1, (code & 1).astype(F32)


def pair_slices(pair, rows):
    for i in range(2):
        yield i, slice(i * rows, (i + 1) * rows), slice((2 * pair + i) * rows, (2 * pair + i + 1) * rows)


def keep_made(pair, rows, made, refs):
    done = 2 * pair * rows
    for old_ref, new_ref in zip(made, refs):
        new_ref[0:done, :] = old_ref[0:done, :]


def qkv_body(pair, tail_ref, xa_ref, xb_ref, w_ref, code_ref, was_ref, *rest):
    q_ref, k_ref, v_ref, pack_ref = rest[-4:]
    keep_made(pair, xa_ref.shape[0], rest[:-4], rest[-4:-1])
    width = q_ref.shape[1]
    block = same_head(width)
    state, sums = was_ref[0:HEAD, :], was_ref[HEAD:PACK, :]
    for i, _, at in pair_slices(pair, xa_ref.shape[0]):
        x = (xa_ref, xb_ref)[i][...]
        q_ref[at, :] = feature(nn(x, w_ref[0])).astype(BF)
        segment, valid = decode(code_ref[2 * pair + i])
        k = (feature(nn(x, w_ref[1])) * valid).astype(BF)
        v = nn(x, w_ref[2]).astype(BF)
        k_ref[at, :] = k
        v_ref[at, :] = v
        kept = pick(segment == tail_ref[0], k)
        state = state + fold_heads(pick(block, tn(kept, v)), width)
        sums = sums + jnp.sum(kept.astype(F32), axis=0, keepdims=True)
    pack_ref[0:HEAD, :] = state
    pack_ref[HEAD:PACK, :] = sums


def project_qkv(pair, tail, xa, xb, w, code, was, made, tokens=()):
    width, whole = w.shape[2], code.shape[0] * code.shape[2]
    call = kernel(
        functools.partial(qkv_body, pair), "project_qkv",
        (shape(whole, width, BF),) * 3 + (shape(PACK, width, F32),),
        [smem()] + [vmem()] * (5 + len(made)), 8,
        aliases={6 + i: i for i in range(len(made))}, tokens=tokens,
    )
    return call(tail, xa, xb, w, code, was, *made)


def swap_heads(x):
    return jnp.concatenate(
        [pltpu.roll(x[:, i : i + 2 * HEAD], HEAD, 1) for i in range(0, x.shape[1], 2 * HEAD)], axis=1
    )


def forward_body(
    last_ref, spot_ref, q_ref, k_ref, v_ref, code_ref, num_ref, den_ref, st_ref, ks_ref
):
    rows, width = q_ref.shape
    size = code_ref.shape[2]
    block = same_head(width)
    ones_block = block.astype(BF)
    lanes = lane_head(size, width)
    even = (lanes % 2) == 0
    lower = causal(size)
    st_ref[...] = jnp.zeros_like(st_ref)
    ks_ref[...] = jnp.zeros_like(ks_ref)

    def step(c, carry):
        spot = spot_ref[c]
        at = pl.ds(pl.multiple_of(spot * size, size), size)
        q, k, v = q_ref[at, :], k_ref[at, :], v_ref[at, :]
        seg = decode(code_ref[spot])[0]
        keep = (lower & (seg == code_ref[spot] >> 1)).astype(BF)
        before, after = last_ref[c], last_ref[c + 1]
        carried = (seg == before).astype(F32)
        sums = [jnp.zeros((size, width), F32)] * 2
        for h in range(width // HEAD):
            mine = lanes == h
            score = nt(pick(mine, q), k).astype(BF) * keep
            both = jnp.where(mine, v, (lanes == (h ^ 1)).astype(BF))
            sums[h % 2] = sums[h % 2] + nn(score, both)
        num = jnp.where(even, sums[0], sums[1])
        den = swap_heads(jnp.where(even, sums[1], sums[0]))
        num_ref[at, :] = num + carried * nn(q, st_ref[...].astype(BF))
        den_ref[at, :] = den + carried * nn((q.astype(F32) * ks_ref[0:1, :]).astype(BF), ones_block)
        kept = pick(seg == after, k)
        cont = (before == after).astype(F32)
        st_ref[...] = cont * st_ref[...] + pick(block, tn(kept, v))
        ks_ref[...] = cont * ks_ref[...] + jnp.sum(kept.astype(F32), axis=0, keepdims=True)
        return carry

    lax.fori_loop(0, rows // size, step, 0)


def attend(last, spot, q, k, v, code):
    rows, width = q.shape
    call = kernel(
        forward_body, "attend", (shape(rows, width, F32),) * 2, [smem()] * 2 + [vmem()] * 4, 8,
        scratch=[pltpu.VMEM((width, width), F32), pltpu.VMEM((8, width), F32)],
    )
    return call(last, spot, q, k, v, code)


def project_body(
    pair, first_ref, num_ref, den_ref, q_ref, pack_ref, code_ref, w_ref,
    heads_ref, rinv_ref, a_ref, b_ref
):
    width = q_ref.shape[1]
    block = same_head(width)
    state = spread_heads(pack_ref[0:HEAD, :], width, block).astype(BF)
    sums = pack_ref[HEAD : HEAD + 1, :]
    for i, own, at in pair_slices(pair, a_ref.shape[0]):
        q = q_ref[at, :]
        segment, valid = decode(code_ref[2 * pair + i])
        opening = (segment == first_ref[0]).astype(F32)
        num = num_ref[at, :] + opening * nn(q, state)
        den = den_ref[at, :] + opening * nn((q.astype(F32) * sums).astype(BF), block.astype(BF))
        rinv = valid / (den + 1e-06 + 1.0 - valid)
        heads = (num * rinv).astype(BF)
        heads_ref[own, :] = heads
        rinv_ref[own, :] = rinv.astype(BF)
        (a_ref, b_ref)[i][...] = nn(heads, w_ref[...]).astype(BF)


def project(pair, rows, last, num, den, q, pack, code, w, tokens):
    width = q.shape[1]
    call = kernel(
        functools.partial(project_body, pair), "project",
        (shape(2 * rows, width, BF),) * 2 + (shape(rows, D, BF),) * 2,
        [smem()] + [vmem()] * 6, 8, tokens=tokens,
    )
    return call(last, num, den, q, pack, code, w)


def mlp_body(
    xa_ref, xb_ref, ga_ref, gb_ref, up_ref, down_ref, act_ref, hid_ref, na_ref, nb_ref, ba_ref, bb_ref
):
    root = 0.7978845608028654
    tile = min(512, up_ref.shape[1])
    for i, own, _ in pair_slices(0, xa_ref.shape[0]):
        x, g = (xa_ref, xb_ref)[i][...], (ga_ref, gb_ref)[i][...]
        for j in range(0, up_ref.shape[1], tile):
            cols = slice(j, j + tile)
            h = nn(x, up_ref[:, cols])
            grad = nt(g, down_ref[cols, :])
            square = h * h
            t = jnp.tanh(root * h * (1.0 + 0.044715 * square))
            plus = 0.5 * (1.0 + t)
            slope = plus + 0.5 * h * (1.0 - t * t) * (root + (3.0 * 0.044715 * root) * square)
            act_ref[own, cols] = (h * plus).astype(BF)
            hid_ref[own, cols] = (grad * slope).astype(BF)
        (na_ref, nb_ref)[i][...] = nt(hid_ref[own, :], up_ref[...]).astype(BF)
        (ba_ref, bb_ref)[i][...] = nn(act_ref[own, :], down_ref[...]).astype(BF)


def mlp(xa, xb, ga, gb, up, down):
    rows, hidden = xa.shape[0], up.shape[1]
    call = kernel(
        mlp_body, "mlp", (shape(2 * rows, hidden, BF),) * 2 + (shape(rows, D, BF),) * 4,
        [vmem()] * 6, 9,
    )
    return call(xa, xb, ga, gb, up, down)


def heads_back_body(
    pair, first_ref, ga_ref, gb_ref, w_ref, heads_ref, rinv_ref, q_ref, code_ref, was_ref, *rest
):
    ng_ref, dg_ref, pack_ref = rest[-3:]
    keep_made(pair, ga_ref.shape[0], rest[:-3], rest[-3:-1])
    width = q_ref.shape[1]
    block = same_head(width)
    ones_block = block.astype(BF)
    state, sums = was_ref[0:HEAD, :], was_ref[HEAD:PACK, :]
    for i, own, at in pair_slices(pair, ga_ref.shape[0]):
        hg = nt((ga_ref, gb_ref)[i][...], w_ref[...])
        rinv = rinv_ref[own, :].astype(F32)
        ng = (hg * rinv).astype(BF)
        prod = hg * heads_ref[own, :].astype(F32)
        high = prod.astype(BF)
        low = (prod - high.astype(F32)).astype(BF)
        dg = -(nn(high, ones_block) + nn(low, ones_block)) * rinv
        ng_ref[at, :] = ng
        dg_ref[at, :] = dg
        opened = pick(decode(code_ref[2 * pair + i])[0] == first_ref[0], q_ref[at, :])
        state = state + fold_heads(pick(block, tn(opened, ng)), width)
        sums = sums + jnp.sum(opened.astype(F32) * dg, axis=0, keepdims=True)
    pack_ref[0:HEAD, :] = state
    pack_ref[HEAD:PACK, :] = sums


def heads_back(pair, last, ga, gb, w, heads, rinv, q, code, was, made, tokens=()):
    whole, width = q.shape
    call = kernel(
        functools.partial(heads_back_body, pair), "heads_back",
        (shape(whole, width, BF), shape(whole, width, F32), shape(PACK, width, F32)),
        [smem()] + [vmem()] * (8 + len(made)), 5,
        aliases={9 + i: i for i in range(len(made))}, tokens=tokens,
    )
    return call(last, ga, gb, w, heads, rinv, q, code, was, *made)


def backward_body(
    last_ref, spot_ref, q_ref, k_ref, v_ref, ng_ref, dg_ref, code_ref, pack_ref,
    dq_ref, dk_ref, dv_ref, all_ref, sums_ref, st_ref, ks_ref
):
    rows, width = q_ref.shape
    size = code_ref.shape[2]
    count = rows // size
    block = same_head(width)
    lanes = lane_head(size, width)
    half = (lax.broadcasted_iota(jnp.int32, (size, width), 1) % HEAD) < HEAD // 2
    lower = causal(size)
    st_ref[...] = spread_heads(pack_ref[0:HEAD, :], width, block)
    ks_ref[...] = jnp.broadcast_to(pack_ref[HEAD : HEAD + 1, :], ks_ref.shape)
    k_ref, v_ref = k_ref.here(), v_ref.here()

    def collect(c, carry):
        at = pl.ds(pl.multiple_of(spot_ref[c] * size, size), size)
        all_ref[c] = st_ref[...].astype(BF)
        sums_ref[c] = ks_ref[...]
        before, after = last_ref[c], last_ref[c + 1]
        kept = pick(decode(code_ref[spot_ref[c]])[0] == after, k_ref[at, :])
        cont = (before == after).astype(F32)
        st_ref[...] = cont * st_ref[...] + pick(block, tn(kept, v_ref[at, :]))
        ks_ref[...] = cont * ks_ref[...] + jnp.sum(kept.astype(F32), axis=0, keepdims=True)
        return carry

    lax.fori_loop(0, count, collect, 0)
    q_ref, ng_ref, dg_ref = q_ref.here(), ng_ref.here(), dg_ref.here()
    st_ref[...] = jnp.zeros_like(st_ref)
    ks_ref[...] = jnp.zeros_like(ks_ref)

    def step(i, carry):
        c = count - 1 - i
        spot = spot_ref[c]
        at = pl.ds(pl.multiple_of(spot * size, size), size)
        q, k, v, ng, dg = q_ref[at, :], k_ref[at, :], v_ref[at, :], ng_ref[at, :], dg_ref[at, :]
        seg = decode(code_ref[spot])[0]
        keep = (lower & (seg == code_ref[spot] >> 1)).astype(BF)
        before, after = last_ref[c], last_ref[c + 1]
        opened = seg == before
        carried = opened.astype(F32)
        tail = (seg == after).astype(F32)
        grad_state = st_ref[...].astype(BF)
        moved = swap_heads(dg)
        high = moved.astype(BF)
        low = (moved - high.astype(F32)).astype(BF)
        terms = jnp.where(half, high, low) * jnp.asarray(2.0 / HEAD, BF)
        one = jnp.ones((), BF)
        dq = carried * (nt(ng, all_ref[c]) + dg * sums_ref[c][0:1, :])
        dk = tail * (nt(v, grad_state) + ks_ref[0:1, :])
        dv = tail * nn(k, grad_state)
        for h in range(width // HEAD):
            mine = lanes == h
            qh, kh, nh = pick(mine, q), pick(mine, k), pick(mine, ng)
            score = nt(qh, k).astype(BF) * keep
            left = jnp.where(mine, ng, pick(lanes == (h ^ 1), terms))
            back = nt(left, jnp.where(mine, v, one)).astype(BF) * keep
            dq = dq + nn(back, kh)
            dk = dk + tn(back, qh)
            dv = dv + tn(score, nh)
        dq_ref[at, :] = (dq * jnp.minimum(q.astype(F32), 1.0)).astype(BF)
        dk_ref[at, :] = dk.astype(BF)
        dv_ref[at, :] = dv.astype(BF)
        cont = (before == after).astype(F32)
        st_ref[...] = cont * st_ref[...] + pick(block, tn(pick(opened, q), ng))
        ks_ref[...] = cont * ks_ref[...] + jnp.sum(carried * q.astype(F32) * dg, axis=0, keepdims=True)
        return carry

    lax.fori_loop(0, count, step, 0)


def attend_back(last, spot, q, k, v, ng, dg, code, pack, tokens):
    rows, width = q.shape
    count = code.shape[0]
    call = kernel(
        backward_body, "attend_back",
        (shape(rows, width, BF),) * 3,
        [smem()] * 2 + [vmem()] * 7, 12, far=(3, 4, 2, 5, 6),
        scratch=[
            pltpu.VMEM((count, width, width), BF),
            pltpu.VMEM((count, 8, width), F32),
            pltpu.VMEM((width, width), F32),
            pltpu.VMEM((8, width), F32),
        ],
        tokens=tokens,
    )
    return call(last, spot, q, k, v, ng, dg, code, pack)


def mix_body(tail_ref, dq_ref, dk_ref, dv_ref, k_ref, v_ref, code_ref, pack_ref, w_ref, mixed_ref, *part_refs):
    width = k_ref.shape[1]
    rows = part_refs[0].shape[0]
    block = same_head(width)
    state = spread_heads(pack_ref[0:HEAD, :], width, block).astype(BF)
    sums = pack_ref[HEAD : HEAD + 1, :]
    for i, part_ref in enumerate(part_refs):
        at = slice(i * rows, (i + 1) * rows)
        tail = (decode(code_ref[i])[0] == tail_ref[0]).astype(F32)
        k = k_ref[at, :]
        dk = dk_ref[at, :].astype(F32) + tail * (nt(v_ref[at, :], state) + sums)
        dv = dv_ref[at, :].astype(F32) + tail * nn(k, state)
        dq = dq_ref[at, :]
        dk = (dk * jnp.minimum(k.astype(F32), 1.0)).astype(BF)
        dv = dv.astype(BF)
        mixed_ref[at, 0:width] = dq
        mixed_ref[at, width : 2 * width] = dk
        mixed_ref[at, 2 * width : 3 * width] = dv
        part_ref[...] = (nt(dq, w_ref[0]) + nt(dk, w_ref[1]) + nt(dv, w_ref[2])).astype(BF)


def mix(rows, tail, dq, dk, dv, k, v, code, pack, w):
    whole, width = k.shape
    call = kernel(
        mix_body, "mix", (shape(whole, 3 * width, BF),) + (shape(rows, D, BF),) * (whole // rows),
        [smem()] + [vmem()] * 8, 8, far=(4, 1, 2, 5, 3, 8),
    )
    return call(tail, dq, dk, dv, k, v, code, pack, w)


def feature(values):
    return jnp.where(values > 0, values + 1.0, jnp.exp(jnp.minimum(values, 0.0)))


def bits_of(count):
    return [1 << b for b in range(count.bit_length() - 1)]


def swap(value, axis, bit):
    return lax.ppermute(value, axis, [(i, i ^ bit) for i in range(lax.axis_size(axis))])


def after(value, *tokens):
    return lax.optimization_barrier((value, *tokens))[0] if tokens else value


def gather_begin(value):
    slots = {0: value}
    for bit in reversed(bits_of(lax.axis_size("feat"))[1:]):
        for s in sorted(slots):
            slots[s | bit] = swap(slots[s], "feat", bit)
    slots[1] = swap(value, "feat", 1)
    return slots


def gather_end(slots, *tokens):
    for s in range(2, lax.axis_size("feat"), 2):
        slots[s + 1] = swap(after(slots[s], *tokens), "feat", 1)
    return [slots[s] for s in range(len(slots))]


def scatter_begin(parts):
    sums = {}
    for s in range(len(parts) - 2, -1, -2):
        got = swap(parts[s + 1], "feat", 1)
        sums[s] = (parts[s].astype(F32) + got.astype(F32)).astype(BF) if s else [parts[0], got]
    return sums


def scatter_end(sums, *tokens):
    sums = {s: part if s == 0 else [after(part, *tokens)] for s, part in sums.items()}
    for bit in bits_of(lax.axis_size("feat"))[1:]:
        for s in sorted(sums, reverse=True):
            if s & bit:
                pieces = sums.pop(s)
                value = pieces[0]
                if len(pieces) > 1:
                    value = functools.reduce(jnp.add, [p.astype(F32) for p in pieces]).astype(BF)
                sums[s ^ bit].append(swap(value, "feat", bit))
    return sums[0]


def sum_everywhere(value):
    for axis in ("feat", "rows"):
        for bit in bits_of(lax.axis_size(axis)):
            value = value + swap(value, axis, bit)
    return value


class RowSum:
    def __init__(self, value, order, *tokens):
        self.order, self.step = order, 0
        self.value = after(value, *tokens)
        self.launch()

    def launch(self):
        count = len(self.order)
        halving = self.step < count
        bit = self.order[self.step] if halving else self.order[2 * count - 1 - self.step]
        self.upper = (lax.axis_index("rows") & bit) != 0
        self.sent = self.kept = self.value
        if halving:
            half = self.value.shape[0] // 2
            low, high = self.value[:half], self.value[half:]
            self.sent = jnp.where(self.upper, low, high)
            self.kept = jnp.where(self.upper, high, low)
        self.got = swap(self.sent, "rows", bit)

    def next(self, *tokens):
        got = after(self.got, *tokens)
        if self.step < len(self.order):
            self.value = (self.kept.astype(F32) + got.astype(F32)).astype(BF)
        else:
            first = jnp.where(self.upper, got, self.kept)
            self.value = jnp.concatenate([first, jnp.where(self.upper, self.kept, got)], axis=0)
        self.step += 1
        if self.step < 2 * len(self.order):
            self.launch()
            return self.sent
        return self.value

    def finish(self, *tokens):
        while self.step < 2 * len(self.order):
            self.next(*tokens)
        return self.value


def shifted(pack, hop, groups, reverse):
    if reverse:
        pairs = [(i, i - hop) for i in range(hop, groups)]
    else:
        pairs = [(i, i + hop) for i in range(groups - hop)]
    return lax.ppermute(pack, "rows", pairs)


def reached(crops_at, here, groups, reach, reverse):
    mine = crops_at[here + 1] if reverse else crops_at[here]
    flags = []
    for hop in range(1, reach + 1):
        other = here + hop if reverse else here - hop
        inside = (other < groups) if reverse else (other >= 0)
        at = jnp.clip(other, 0, groups - 1)
        theirs = crops_at[at] if reverse else crops_at[at + 1]
        flags.append((inside & (theirs == mine)).astype(F32))
    return jnp.stack(flags)


def gather_carry(pack, flags, groups, reverse):
    total = jnp.zeros(pack.shape, F32)
    for i in range(flags.shape[0]):
        got = shifted(pack, i + 1, groups, reverse).astype(F32)
        total = total + jnp.where(flags[i] > 0, got, 0.0)
    return total


def on_device(
    pixels,
    qkv_weight,
    out_weight,
    up_weight,
    down_weight,
    norm1_gain,
    norm1_bias,
    norm2_gain,
    norm2_bias,
    crop_lengths,
    crop_offsets,
    pixel_mask,
    out_grad,
):
    local_rows = pixels.shape[0]
    group_rows = pixel_mask.shape[0]
    width = qkv_weight.shape[2]
    crop_count = crop_offsets.shape[0]
    groups = lax.axis_size("rows")
    members = lax.axis_size("feat")
    pairs = members // 2
    here = lax.axis_index("rows")
    member = lax.axis_index("feat")
    reach = min(groups - 1, -(-(CROP_MAX - 1) // group_rows))
    group_start = here * group_rows
    slot_ids = jnp.arange(members, dtype=jnp.int32) ^ member
    in_group = (slot_ids[:, None] * local_rows + jnp.arange(local_rows, dtype=jnp.int32)[None, :]).reshape(-1)
    places = group_start + in_group
    started = crop_offsets[None, :] <= places[:, None]
    crop_ends = crop_offsets + crop_lengths
    segment = jnp.sum(started.astype(jnp.int32), axis=1) - 1
    inside = jnp.sum((started & (places[:, None] < crop_ends[None, :])).astype(jnp.int32), axis=1)
    mask = jnp.concatenate(
        [
            lax.dynamic_slice_in_dim(pixel_mask, (member ^ s) * local_rows, local_rows)
            for s in range(members)
        ]
    )
    pixel_valid = (mask * inside).astype(F32)
    edges = jnp.arange(groups + 1, dtype=jnp.int32) * group_rows - 1
    crops_at = jnp.sum((crop_offsets[None, :] <= edges[:, None]).astype(jnp.int32), axis=1) - 1
    chunk_edges = group_start - 1 + jnp.arange(members + 1, dtype=jnp.int32) * local_rows
    last = jnp.sum((crop_offsets[None, :] <= chunk_edges[:, None]).astype(jnp.int32), axis=1) - 1
    tail = last[-1:]
    spot = slot_ids
    code = (segment * 2 + mask * inside).reshape(members, 1, local_rows)
    validc = pixel_valid[:, None]
    gain1, bias1, gain2, bias2 = (
        a[None, :] for a in (norm1_gain, norm1_bias, norm2_gain, norm2_bias)
    )
    no_pack = jnp.zeros((PACK, width), F32)
    before = reached(crops_at, here, groups, reach, False)
    behind = reached(crops_at, here, groups, reach, True)

    normed_slots = gather_begin(norm_one(pixels, gain1, bias1))
    grad_slots = gather_begin(after(out_grad, normed_slots[members // 2]))
    *made, pack = project_qkv(0, tail, normed_slots[0], normed_slots[1], qkv_weight, code, no_pack, (), [before, behind, spot])
    normed_slots = gather_end(normed_slots, pack)
    for p in range(1, pairs):
        *made, pack = project_qkv(
            p, tail, normed_slots[2 * p], normed_slots[2 * p + 1], qkv_weight, code, pack, made
        )
    q, k, v = made
    carry = gather_carry(pack.astype(BF), before, groups, False)
    num, den = attend(last, spot, q, k, v, code)
    grad_slots = gather_end(grad_slots, num)
    sent = {
        p: project(
            p, local_rows, last, num, den, q, carry, code, out_weight, [grad_slots[members // 2]]
        )
        for p in reversed(range(pairs))
    }
    parts = scatter_end(scatter_begin([sent[s // 2][2 + s % 2] for s in range(members)]))
    middle, normed_two, attended_square = norm_two(pixels, gain2, bias2, parts)
    two_slots = gather_begin(normed_two)
    hidden = [mlp(two_slots[0], two_slots[1], grad_slots[0], grad_slots[1], up_weight, down_weight)]
    two_slots = gather_end(two_slots, hidden[0][0])
    for p in range(1, pairs):
        hidden.append(mlp(*two_slots[2 * p : 2 * p + 2], *grad_slots[2 * p : 2 * p + 2], up_weight, down_weight))
    two_sums = scatter_begin([hidden[s // 2][2 + s % 2] for s in range(members)])
    two_parts = scatter_end(two_sums)
    branch_sums = scatter_begin([hidden[s // 2][4 + s % 2] for s in range(members)])
    acts, hids, twos = after(
        ([h[0] for h in hidden], [h[1] for h in hidden], two_slots), two_sums[members - 2]
    )
    hids = after(hids, two_sums[0][1], branch_sums[0][1], branch_sums[members - 2])
    down_grad = tn(jnp.concatenate(acts, axis=0), jnp.concatenate(grad_slots, axis=0)).astype(BF)
    up_grad = tn(jnp.concatenate(twos, axis=0), jnp.concatenate(hids, axis=0)).astype(BF)
    bits = bits_of(groups)
    turned = bits[1:] + bits[:1]
    both = jnp.concatenate([down_grad, up_grad.reshape(-1, D)], axis=0)
    both = lax.psum_scatter(after(both, two_parts[-1]), "rows", scatter_dimension=0, tiled=True)
    middle_low, gain2_grad, bias2_grad = norm_two_back(
        out_grad, middle, gain2, two_parts,
        [down_grad, up_grad, branch_sums[0][1], branch_sums[members - 2]],
    )
    middle_slots = gather_begin(middle_low)
    *made, grad_pack = heads_back(
        0, last, middle_slots[0], middle_slots[1], out_weight, sent[0][0], sent[0][1], q, code, no_pack, ()
    )
    branch_parts = scatter_end(branch_sums, middle_slots[members // 2], grad_pack)
    middle_slots = gather_end(middle_slots, grad_pack)
    for p in range(1, pairs):
        *made, grad_pack = heads_back(
            p, last, middle_slots[2 * p], middle_slots[2 * p + 1], out_weight,
            sent[p][0], sent[p][1], q, code, grad_pack, made
        )
    ng, dg = made
    grad_carry = gather_carry(grad_pack.astype(BF), behind, groups, True)
    heads_all = jnp.concatenate([sent[p][0] for p in range(pairs)], axis=0)
    out_weight_grad = tn(heads_all, jnp.concatenate(middle_slots, axis=0))
    out_sum = RowSum(out_weight_grad.astype(BF), turned)
    dq, dk, dv = attend_back(last, spot, q, k, v, ng, dg, code, carry, [out_sum.sent])
    out_sum.next(dq)
    mixed_grad, *mixed_parts = mix(local_rows, tail, dq, dk, dv, k, v, code, grad_carry, qkv_weight)
    normed_sums = scatter_begin(mixed_parts)
    normed_parts = scatter_end(normed_sums)
    qkv_grad = tn(mixed_grad, jnp.concatenate(normed_slots, axis=0)).astype(BF)
    both = lax.all_gather(after(both, dq), "rows", axis=0, tiled=True)
    down_grad = both[: down_grad.shape[0]].astype(F32)
    up_grad = both[down_grad.shape[0] :].reshape(up_grad.shape).astype(F32)
    out_sum.next(mixed_grad)
    cut = 3 * width // 2
    low_sum = RowSum(qkv_grad[:cut], bits)
    high_sum = RowSum(qkv_grad[cut:], turned)
    normed_sent = normed_sums[members - 2]
    tokens = [low_sum.next(normed_sent), high_sum.next(normed_sent)]
    output, result_square, branch_square = finish(middle, branch_parts, tokens)
    pixels_grad, gain1_grad, bias1_grad = norm_one_back(pixels, middle_low, gain1, normed_parts)
    tokens = [out_sum.next(*tokens)]
    tokens = [low_sum.next(*tokens), high_sum.next(*tokens)]
    out_weight_grad = out_sum.finish(*tokens).astype(F32)
    qkv_grad = jnp.concatenate([low_sum.finish(), high_sum.finish()], axis=0)
    qkv_grad = jnp.swapaxes(qkv_grad.reshape(3, width, D), 1, 2).astype(F32)

    crop_onehot = (
        segment[:local_rows, None] == jnp.arange(crop_count, dtype=jnp.int32)[None, :]
    ).astype(F32)
    squares = (
        jnp.concatenate(
            [result_square, attended_square, branch_square, jnp.ones((local_rows, 1), F32)], axis=1
        )
        * validc[:local_rows]
    )
    crop_sums = lax.dot_general(
        squares, crop_onehot, (((0,), (0,)), ((), ())), precision=precise, preferred_element_type=F32
    )
    sums = jnp.concatenate(
        [gain1_grad[0], bias1_grad[0], gain2_grad[0], bias2_grad[0], crop_sums.reshape(-1)]
    )
    sums = sum_everywhere(sums)
    gain1_grad, bias1_grad, gain2_grad, bias2_grad = sums[: 4 * D].reshape(4, D)
    crop_sums = sums[4 * D :].reshape(4, crop_count)
    crop_rms = jnp.sqrt(crop_sums[:3] / (D * jnp.maximum(crop_sums[3], 1.0))[None, :])
    return (
        output,
        pixels_grad,
        qkv_grad,
        out_weight_grad,
        up_grad,
        down_grad,
        gain1_grad,
        bias1_grad,
        gain2_grad,
        bias2_grad,
        crop_rms,
    )


def solution(mesh):
    split = P(("rows", "feat"), None)
    qkv, rows_feat, cols_feat = P(None, None, "feat"), P("feat", None), P(None, "feat")
    in_specs = (
        (split, qkv, rows_feat, cols_feat, rows_feat) + (P(),) * 6 + (P("rows"), split)
    )
    out_specs = (split, split, qkv, rows_feat, cols_feat, rows_feat) + (P(),) * 5
    return jax.shard_map(
        on_device, mesh=mesh, in_specs=in_specs, out_specs=out_specs, check_vma=False
    )
```

```python
import functools

import jax
import jax.numpy as jnp
from jax import lax
from jax.experimental import pallas as pl
from jax.experimental.pallas import tpu as pltpu
from jax.sharding import PartitionSpec as P

D = 1024
HEAD = 64
CROP_MAX = 3072
PACK = HEAD + 16

BF = jnp.bfloat16
F32 = jnp.float32
precise = lax.Precision.HIGHEST


def nn(a, b):
    return lax.dot_general(a, b, (((1,), (0,)), ((), ())), preferred_element_type=F32)


def nt(a, b):
    return lax.dot_general(a, b, (((1,), (1,)), ((), ())), preferred_element_type=F32)


def tn(a, b):
    return lax.dot_general(a, b, (((0,), (0,)), ((), ())), preferred_element_type=F32)


def same_head(width):
    row = lax.broadcasted_iota(jnp.int32, (width, width), 0) // HEAD
    col = lax.broadcasted_iota(jnp.int32, (width, width), 1) // HEAD
    return row == col


def lane_head(rows, width):
    return lax.broadcasted_iota(jnp.int32, (rows, width), 1) // HEAD


def causal(rows):
    row = lax.broadcasted_iota(jnp.int32, (rows, rows), 0)
    col = lax.broadcasted_iota(jnp.int32, (rows, rows), 1)
    return row >= col


def fold_heads(full, width):
    out = full[0:HEAD]
    for h in range(1, width // HEAD):
        out = out + full[h * HEAD : (h + 1) * HEAD]
    return out


def spread_heads(part, width, block):
    tall = jnp.concatenate([part] * (width // HEAD), axis=0)
    return jnp.where(block, tall, jnp.zeros_like(tall))


def pick(mask, value):
    return jnp.where(mask, value, jnp.zeros_like(value))


def vmem():
    return pl.BlockSpec(memory_space=pltpu.VMEM)


def smem():
    return pl.BlockSpec(memory_space=pltpu.SMEM)


def shape(rows, cols, kind):
    return jax.ShapeDtypeStruct((rows, cols), kind)


ROW_TILE = 192


def tiles(rows):
    return [slice(i, i + ROW_TILE) for i in range(0, rows, ROW_TILE)]


class Incoming:
    def __init__(self, buffer, copy):
        self.buffer, self.copy, self.shape = buffer, copy, buffer.shape
        copy.start()

    def here(self):
        if self.copy is not None:
            self.copy.wait()
            self.copy = None
        return self.buffer

    def __getitem__(self, index):
        return self.here()[index]


def kernel(body, name, out_shape, in_specs, megabytes, scratch=(), aliases=None, tokens=(), far=()):
    outs = vmem() if not isinstance(out_shape, tuple) else (vmem(),) * len(out_shape)
    made = 1 if not isinstance(out_shape, tuple) else len(out_shape)
    count = len(in_specs)
    specs = [pl.BlockSpec(memory_space=pl.ANY) if i in far else spec for i, spec in enumerate(in_specs)]
    skip = pl.BlockSpec(memory_space=pl.ANY)

    def call(*args):
        buffers = [pltpu.VMEM(args[i].shape, args[i].dtype) for i in far]

        def run(*refs):
            given = list(refs[:count])
            rest = refs[count + len(tokens) :]
            results, own, copied = rest[:made], rest[made : made + len(scratch)], rest[made + len(scratch) :]
            arriving = []
            for n, i in enumerate(far):
                given[i] = Incoming(copied[n], pltpu.make_async_copy(given[i], copied[n], copied[-1].at[n]))
                arriving.append(given[i])
            body(*given, *results, *own)
            for value in arriving:
                value.here()

        sems = [pltpu.SemaphoreType.DMA((len(far),))] if far else []
        return pl.pallas_call(
            run,
            out_shape=out_shape,
            in_specs=specs + [skip] * len(tokens),
            out_specs=outs,
            scratch_shapes=list(scratch) + buffers + sems,
            input_output_aliases=aliases or {},
            compiler_params=pltpu.CompilerParams(vmem_limit_bytes=(60 if far else megabytes) << 20),
            name=name,
        )(*args, *tokens)

    return call


def normal(values):
    centre = jnp.mean(values, axis=-1, keepdims=True)
    moved = values - centre
    scale = lax.rsqrt(jnp.mean(moved * moved, axis=-1, keepdims=True) + 1e-05)
    return moved * scale, scale


def normal_back(grad, gain, xhat, scale):
    g = grad * gain
    return scale * (
        g - jnp.mean(g, axis=-1, keepdims=True) - xhat * jnp.mean(g * xhat, axis=-1, keepdims=True)
    )


def total(refs):
    value = refs[0][...].astype(F32)
    for ref in refs[1:]:
        value = value + ref[...].astype(F32)
    return value


def norm_body(x_ref, gain_ref, bias_ref, out_ref):
    for at in tiles(x_ref.shape[0]):
        xhat, _ = normal(x_ref[at, :].astype(F32))
        out_ref[at, :] = (xhat * gain_ref[...] + bias_ref[...]).astype(BF)


def norm_one(x, gain, bias):
    call = kernel(norm_body, "norm_one", shape(x.shape[0], D, BF), [vmem()] * 3, 4)
    return call(x, gain, bias)


def total(refs, at):
    value = refs[0][at, :].astype(F32)
    for ref in refs[1:]:
        value = value + ref[at, :].astype(F32)
    return value


def middle_body(*refs):
    x_ref, gain_ref, bias_ref = refs[:3]
    parts = refs[3:-3]
    middle_ref, out_ref, square_ref = refs[-3:]
    for at in tiles(x_ref.shape[0]):
        attended = total(parts, at)
        middle = x_ref[at, :].astype(F32) + attended
        middle_ref[at, :] = middle.astype(BF)
        xhat, _ = normal(middle)
        out_ref[at, :] = (xhat * gain_ref[...] + bias_ref[...]).astype(BF)
        square_ref[at, :] = jnp.sum(attended * attended, axis=-1, keepdims=True)


def norm_two(x, gain, bias, parts):
    rows = x.shape[0]
    call = kernel(
        middle_body, "norm_two", (shape(rows, D, BF), shape(rows, D, BF), shape(rows, 1, F32)),
        [vmem()] * (3 + len(parts)), 4,
    )
    return call(x, gain, bias, *parts)


def middle_back_body(*refs):
    grad_ref, middle_ref, gain_ref = refs[:3]
    parts = refs[3:-3]
    low_ref, gain_grad_ref, bias_grad_ref = refs[-3:]
    gain_grad = bias_grad = jnp.zeros(gain_ref.shape, F32)
    for at in tiles(grad_ref.shape[0]):
        grad = total(parts, at)
        xhat, scale = normal(middle_ref[at, :].astype(F32))
        gain_grad = gain_grad + jnp.sum(grad * xhat, axis=0, keepdims=True)
        bias_grad = bias_grad + jnp.sum(grad, axis=0, keepdims=True)
        out = grad_ref[at, :].astype(F32) + normal_back(grad, gain_ref[...], xhat, scale)
        low_ref[at, :] = out.astype(BF)
    gain_grad_ref[...] = gain_grad
    bias_grad_ref[...] = bias_grad


def norm_two_back(grad, middle, gain, parts, tokens):
    rows = grad.shape[0]
    call = kernel(
        middle_back_body, "norm_two_back",
        (shape(rows, D, BF), shape(1, D, F32), shape(1, D, F32)),
        [vmem()] * (3 + len(parts)), 9, tokens=tokens, far=(0, 1) + tuple(range(3, 3 + len(parts))),
    )
    return call(grad, middle, gain, *parts)


def pixels_back_body(*refs):
    x_ref, wide_ref, gain_ref = refs[:3]
    parts = refs[3:-3]
    out_ref, gain_grad_ref, bias_grad_ref = refs[-3:]
    gain_grad = bias_grad = jnp.zeros(gain_ref.shape, F32)
    for at in tiles(x_ref.shape[0]):
        grad = total(parts, at)
        xhat, scale = normal(x_ref[at, :].astype(F32))
        gain_grad = gain_grad + jnp.sum(grad * xhat, axis=0, keepdims=True)
        bias_grad = bias_grad + jnp.sum(grad, axis=0, keepdims=True)
        out_ref[at, :] = (wide_ref[at, :].astype(F32) + normal_back(grad, gain_ref[...], xhat, scale)).astype(BF)
    gain_grad_ref[...] = gain_grad
    bias_grad_ref[...] = bias_grad


def norm_one_back(x, wide, gain, parts):
    rows = x.shape[0]
    call = kernel(
        pixels_back_body, "norm_one_back", (shape(rows, D, BF), shape(1, D, F32), shape(1, D, F32)),
        [vmem()] * (3 + len(parts)), 9,
    )
    return call(x, wide, gain, *parts)


def result_body(*refs):
    middle_ref = refs[0]
    parts = refs[1:-3]
    out_ref, result_square_ref, branch_square_ref = refs[-3:]
    for at in tiles(middle_ref.shape[0]):
        branch = total(parts, at)
        result = middle_ref[at, :].astype(F32) + branch
        out_ref[at, :] = result.astype(BF)
        result_square_ref[at, :] = jnp.sum(result * result, axis=-1, keepdims=True)
        branch_square_ref[at, :] = jnp.sum(branch * branch, axis=-1, keepdims=True)


def finish(middle, parts, tokens):
    rows = middle.shape[0]
    call = kernel(
        result_body, "finish", (shape(rows, D, BF), shape(rows, 1, F32), shape(rows, 1, F32)),
        [vmem()] * (1 + len(parts)), 4, tokens=tokens,
    )
    return call(middle, *parts)


def decode(row):
    code = jnp.broadcast_to(row, (128, row.shape[1])).T[:, 0:1]
    return code >> 1, (code & 1).astype(F32)


def pair_slices(pair, rows):
    for i in range(2):
        yield i, slice(i * rows, (i + 1) * rows), slice((2 * pair + i) * rows, (2 * pair + i + 1) * rows)


def keep_made(pair, rows, made, refs):
    done = 2 * pair * rows
    for old_ref, new_ref in zip(made, refs):
        new_ref[0:done, :] = old_ref[0:done, :]


def qkv_body(pair, tail_ref, xa_ref, xb_ref, w_ref, code_ref, was_ref, *rest):
    q_ref, k_ref, v_ref, pack_ref = rest[-4:]
    keep_made(pair, xa_ref.shape[0], rest[:-4], rest[-4:-1])
    width = q_ref.shape[1]
    block = same_head(width)
    state, sums = was_ref[0:HEAD, :], was_ref[HEAD:PACK, :]
    for i, _, at in pair_slices(pair, xa_ref.shape[0]):
        x = (xa_ref, xb_ref)[i][...]
        q_ref[at, :] = feature(nn(x, w_ref[0])).astype(BF)
        segment, valid = decode(code_ref[2 * pair + i])
        k = (feature(nn(x, w_ref[1])) * valid).astype(BF)
        v = nn(x, w_ref[2]).astype(BF)
        k_ref[at, :] = k
        v_ref[at, :] = v
        kept = pick(segment == tail_ref[0], k)
        state = state + fold_heads(pick(block, tn(kept, v)), width)
        sums = sums + jnp.sum(kept.astype(F32), axis=0, keepdims=True)
    pack_ref[0:HEAD, :] = state
    pack_ref[HEAD:PACK, :] = sums


def project_qkv(pair, tail, xa, xb, w, code, was, made, tokens=()):
    width, whole = w.shape[2], code.shape[0] * code.shape[2]
    call = kernel(
        functools.partial(qkv_body, pair), "project_qkv",
        (shape(whole, width, BF),) * 3 + (shape(PACK, width, F32),),
        [smem()] + [vmem()] * (5 + len(made)), 8,
        aliases={6 + i: i for i in range(len(made))}, tokens=tokens,
    )
    return call(tail, xa, xb, w, code, was, *made)


def swap_heads(x):
    return jnp.concatenate(
        [pltpu.roll(x[:, i : i + 2 * HEAD], HEAD, 1) for i in range(0, x.shape[1], 2 * HEAD)], axis=1
    )


def forward_body(
    last_ref, spot_ref, q_ref, k_ref, v_ref, code_ref, num_ref, den_ref, st_ref, ks_ref
):
    rows, width = q_ref.shape
    size = code_ref.shape[2]
    block = same_head(width)
    ones_block = block.astype(BF)
    lanes = lane_head(size, width)
    even = (lanes % 2) == 0
    lower = causal(size)
    st_ref[...] = jnp.zeros_like(st_ref)
    ks_ref[...] = jnp.zeros_like(ks_ref)

    def step(c, carry):
        spot = spot_ref[c]
        at = pl.ds(pl.multiple_of(spot * size, size), size)
        q, k, v = q_ref[at, :], k_ref[at, :], v_ref[at, :]
        seg = decode(code_ref[spot])[0]
        keep = (lower & (seg == code_ref[spot] >> 1)).astype(BF)
        before, after = last_ref[c], last_ref[c + 1]
        carried = (seg == before).astype(F32)
        sums = [jnp.zeros((size, width), F32)] * 2
        for h in range(width // HEAD):
            mine = lanes == h
            score = nt(pick(mine, q), k).astype(BF) * keep
            both = jnp.where(mine, v, (lanes == (h ^ 1)).astype(BF))
            sums[h % 2] = sums[h % 2] + nn(score, both)
        num = jnp.where(even, sums[0], sums[1])
        den = swap_heads(jnp.where(even, sums[1], sums[0]))
        num_ref[at, :] = num + carried * nn(q, st_ref[...].astype(BF))
        den_ref[at, :] = den + carried * nn((q.astype(F32) * ks_ref[0:1, :]).astype(BF), ones_block)
        kept = pick(seg == after, k)
        cont = (before == after).astype(F32)
        st_ref[...] = cont * st_ref[...] + pick(block, tn(kept, v))
        ks_ref[...] = cont * ks_ref[...] + jnp.sum(kept.astype(F32), axis=0, keepdims=True)
        return carry

    lax.fori_loop(0, rows // size, step, 0)


def attend(last, spot, q, k, v, code):
    rows, width = q.shape
    call = kernel(
        forward_body, "attend", (shape(rows, width, F32),) * 2, [smem()] * 2 + [vmem()] * 4, 8,
        scratch=[pltpu.VMEM((width, width), F32), pltpu.VMEM((8, width), F32)],
    )
    return call(last, spot, q, k, v, code)


def project_body(
    pair, first_ref, num_ref, den_ref, q_ref, pack_ref, code_ref, w_ref,
    heads_ref, rinv_ref, a_ref, b_ref
):
    width = q_ref.shape[1]
    block = same_head(width)
    state = spread_heads(pack_ref[0:HEAD, :], width, block).astype(BF)
    sums = pack_ref[HEAD : HEAD + 1, :]
    for i, own, at in pair_slices(pair, a_ref.shape[0]):
        q = q_ref[at, :]
        segment, valid = decode(code_ref[2 * pair + i])
        opening = (segment == first_ref[0]).astype(F32)
        num = num_ref[at, :] + opening * nn(q, state)
        den = den_ref[at, :] + opening * nn((q.astype(F32) * sums).astype(BF), block.astype(BF))
        rinv = valid / (den + 1e-06 + 1.0 - valid)
        heads = (num * rinv).astype(BF)
        heads_ref[own, :] = heads
        rinv_ref[own, :] = rinv.astype(BF)
        (a_ref, b_ref)[i][...] = nn(heads, w_ref[...]).astype(BF)


def project(pair, rows, last, num, den, q, pack, code, w, tokens):
    width = q.shape[1]
    call = kernel(
        functools.partial(project_body, pair), "project",
        (shape(2 * rows, width, BF),) * 2 + (shape(rows, D, BF),) * 2,
        [smem()] + [vmem()] * 6, 8, tokens=tokens,
    )
    return call(last, num, den, q, pack, code, w)


def mlp_body(
    xa_ref, xb_ref, ga_ref, gb_ref, up_ref, down_ref, act_ref, hid_ref, na_ref, nb_ref, ba_ref, bb_ref
):
    root = 0.7978845608028654
    tile = min(512, up_ref.shape[1])
    for i, own, _ in pair_slices(0, xa_ref.shape[0]):
        x, g = (xa_ref, xb_ref)[i][...], (ga_ref, gb_ref)[i][...]
        for j in range(0, up_ref.shape[1], tile):
            cols = slice(j, j + tile)
            h = nn(x, up_ref[:, cols])
            grad = nt(g, down_ref[cols, :])
            square = h * h
            t = jnp.tanh(root * h * (1.0 + 0.044715 * square))
            plus = 0.5 * (1.0 + t)
            slope = plus + 0.5 * h * (1.0 - t * t) * (root + (3.0 * 0.044715 * root) * square)
            act_ref[own, cols] = (h * plus).astype(BF)
            hid_ref[own, cols] = (grad * slope).astype(BF)
        (na_ref, nb_ref)[i][...] = nt(hid_ref[own, :], up_ref[...]).astype(BF)
        (ba_ref, bb_ref)[i][...] = nn(act_ref[own, :], down_ref[...]).astype(BF)


def mlp(xa, xb, ga, gb, up, down):
    rows, hidden = xa.shape[0], up.shape[1]
    call = kernel(
        mlp_body, "mlp", (shape(2 * rows, hidden, BF),) * 2 + (shape(rows, D, BF),) * 4,
        [vmem()] * 6, 9,
    )
    return call(xa, xb, ga, gb, up, down)


def heads_back_body(
    pair, first_ref, ga_ref, gb_ref, w_ref, heads_ref, rinv_ref, q_ref, code_ref, was_ref, *rest
):
    ng_ref, dg_ref, pack_ref = rest[-3:]
    keep_made(pair, ga_ref.shape[0], rest[:-3], rest[-3:-1])
    width = q_ref.shape[1]
    block = same_head(width)
    ones_block = block.astype(BF)
    state, sums = was_ref[0:HEAD, :], was_ref[HEAD:PACK, :]
    for i, own, at in pair_slices(pair, ga_ref.shape[0]):
        hg = nt((ga_ref, gb_ref)[i][...], w_ref[...])
        rinv = rinv_ref[own, :].astype(F32)
        ng = (hg * rinv).astype(BF)
        prod = hg * heads_ref[own, :].astype(F32)
        high = prod.astype(BF)
        low = (prod - high.astype(F32)).astype(BF)
        dg = -(nn(high, ones_block) + nn(low, ones_block)) * rinv
        ng_ref[at, :] = ng
        dg_ref[at, :] = dg
        opened = pick(decode(code_ref[2 * pair + i])[0] == first_ref[0], q_ref[at, :])
        state = state + fold_heads(pick(block, tn(opened, ng)), width)
        sums = sums + jnp.sum(opened.astype(F32) * dg, axis=0, keepdims=True)
    pack_ref[0:HEAD, :] = state
    pack_ref[HEAD:PACK, :] = sums


def heads_back(pair, last, ga, gb, w, heads, rinv, q, code, was, made, tokens=()):
    whole, width = q.shape
    call = kernel(
        functools.partial(heads_back_body, pair), "heads_back",
        (shape(whole, width, BF), shape(whole, width, F32), shape(PACK, width, F32)),
        [smem()] + [vmem()] * (8 + len(made)), 5,
        aliases={9 + i: i for i in range(len(made))}, tokens=tokens,
    )
    return call(last, ga, gb, w, heads, rinv, q, code, was, *made)


def backward_body(
    last_ref, spot_ref, q_ref, k_ref, v_ref, ng_ref, dg_ref, code_ref, pack_ref,
    dq_ref, dk_ref, dv_ref, all_ref, sums_ref, st_ref, ks_ref
):
    rows, width = q_ref.shape
    size = code_ref.shape[2]
    count = rows // size
    block = same_head(width)
    lanes = lane_head(size, width)
    half = (lax.broadcasted_iota(jnp.int32, (size, width), 1) % HEAD) < HEAD // 2
    lower = causal(size)
    st_ref[...] = spread_heads(pack_ref[0:HEAD, :], width, block)
    ks_ref[...] = jnp.broadcast_to(pack_ref[HEAD : HEAD + 1, :], ks_ref.shape)
    k_ref, v_ref = k_ref.here(), v_ref.here()

    def collect(c, carry):
        at = pl.ds(pl.multiple_of(spot_ref[c] * size, size), size)
        all_ref[c] = st_ref[...].astype(BF)
        sums_ref[c] = ks_ref[...]
        before, after = last_ref[c], last_ref[c + 1]
        kept = pick(decode(code_ref[spot_ref[c]])[0] == after, k_ref[at, :])
        cont = (before == after).astype(F32)
        st_ref[...] = cont * st_ref[...] + pick(block, tn(kept, v_ref[at, :]))
        ks_ref[...] = cont * ks_ref[...] + jnp.sum(kept.astype(F32), axis=0, keepdims=True)
        return carry

    lax.fori_loop(0, count, collect, 0)
    q_ref, ng_ref, dg_ref = q_ref.here(), ng_ref.here(), dg_ref.here()
    st_ref[...] = jnp.zeros_like(st_ref)
    ks_ref[...] = jnp.zeros_like(ks_ref)

    def step(i, carry):
        c = count - 1 - i
        spot = spot_ref[c]
        at = pl.ds(pl.multiple_of(spot * size, size), size)
        q, k, v, ng, dg = q_ref[at, :], k_ref[at, :], v_ref[at, :], ng_ref[at, :], dg_ref[at, :]
        seg = decode(code_ref[spot])[0]
        keep = (lower & (seg == code_ref[spot] >> 1)).astype(BF)
        before, after = last_ref[c], last_ref[c + 1]
        opened = seg == before
        carried = opened.astype(F32)
        tail = (seg == after).astype(F32)
        grad_state = st_ref[...].astype(BF)
        moved = swap_heads(dg)
        high = moved.astype(BF)
        low = (moved - high.astype(F32)).astype(BF)
        terms = jnp.where(half, high, low) * jnp.asarray(2.0 / HEAD, BF)
        one = jnp.ones((), BF)
        dq = carried * (nt(ng, all_ref[c]) + dg * sums_ref[c][0:1, :])
        dk = tail * (nt(v, grad_state) + ks_ref[0:1, :])
        dv = tail * nn(k, grad_state)
        for h in range(width // HEAD):
            mine = lanes == h
            qh, kh, nh = pick(mine, q), pick(mine, k), pick(mine, ng)
            score = nt(qh, k).astype(BF) * keep
            left = jnp.where(mine, ng, pick(lanes == (h ^ 1), terms))
            back = nt(left, jnp.where(mine, v, one)).astype(BF) * keep
            dq = dq + nn(back, kh)
            dk = dk + tn(back, qh)
            dv = dv + tn(score, nh)
        dq_ref[at, :] = (dq * jnp.minimum(q.astype(F32), 1.0)).astype(BF)
        dk_ref[at, :] = dk.astype(BF)
        dv_ref[at, :] = dv.astype(BF)
        cont = (before == after).astype(F32)
        st_ref[...] = cont * st_ref[...] + pick(block, tn(pick(opened, q), ng))
        ks_ref[...] = cont * ks_ref[...] + jnp.sum(carried * q.astype(F32) * dg, axis=0, keepdims=True)
        return carry

    lax.fori_loop(0, count, step, 0)


def attend_back(last, spot, q, k, v, ng, dg, code, pack, tokens):
    rows, width = q.shape
    count = code.shape[0]
    call = kernel(
        backward_body, "attend_back",
        (shape(rows, width, BF),) * 3,
        [smem()] * 2 + [vmem()] * 7, 12, far=(3, 4, 2, 5, 6),
        scratch=[
            pltpu.VMEM((count, width, width), BF),
            pltpu.VMEM((count, 8, width), F32),
            pltpu.VMEM((width, width), F32),
            pltpu.VMEM((8, width), F32),
        ],
        tokens=tokens,
    )
    return call(last, spot, q, k, v, ng, dg, code, pack)


def mix_body(tail_ref, dq_ref, dk_ref, dv_ref, k_ref, v_ref, code_ref, pack_ref, w_ref, mixed_ref, *part_refs):
    width = k_ref.shape[1]
    rows = part_refs[0].shape[0]
    block = same_head(width)
    state = spread_heads(pack_ref[0:HEAD, :], width, block).astype(BF)
    sums = pack_ref[HEAD : HEAD + 1, :]
    for i, part_ref in enumerate(part_refs):
        at = slice(i * rows, (i + 1) * rows)
        tail = (decode(code_ref[i])[0] == tail_ref[0]).astype(F32)
        k = k_ref[at, :]
        dk = dk_ref[at, :].astype(F32) + tail * (nt(v_ref[at, :], state) + sums)
        dv = dv_ref[at, :].astype(F32) + tail * nn(k, state)
        dq = dq_ref[at, :]
        dk = (dk * jnp.minimum(k.astype(F32), 1.0)).astype(BF)
        dv = dv.astype(BF)
        mixed_ref[at, 0:width] = dq
        mixed_ref[at, width : 2 * width] = dk
        mixed_ref[at, 2 * width : 3 * width] = dv
        part_ref[...] = (nt(dq, w_ref[0]) + nt(dk, w_ref[1]) + nt(dv, w_ref[2])).astype(BF)


def mix(rows, tail, dq, dk, dv, k, v, code, pack, w):
    whole, width = k.shape
    call = kernel(
        mix_body, "mix", (shape(whole, 3 * width, BF),) + (shape(rows, D, BF),) * (whole // rows),
        [smem()] + [vmem()] * 8, 8, far=(4, 1, 2, 5, 3, 8),
    )
    return call(tail, dq, dk, dv, k, v, code, pack, w)


def feature(values):
    return jnp.where(values > 0, values + 1.0, jnp.exp(jnp.minimum(values, 0.0)))


def bits_of(count):
    return [1 << b for b in range(count.bit_length() - 1)]


def swap(value, axis, bit):
    return lax.ppermute(value, axis, [(i, i ^ bit) for i in range(lax.axis_size(axis))])


def after(value, *tokens):
    return lax.optimization_barrier((value, *tokens))[0] if tokens else value


def gather_begin(value):
    slots = {0: value}
    for bit in reversed(bits_of(lax.axis_size("feat"))[1:]):
        for s in sorted(slots):
            slots[s | bit] = swap(slots[s], "feat", bit)
    slots[1] = swap(value, "feat", 1)
    return slots


def gather_end(slots, *tokens):
    for s in range(2, lax.axis_size("feat"), 2):
        slots[s + 1] = swap(after(slots[s], *tokens), "feat", 1)
    return [slots[s] for s in range(len(slots))]


def scatter_begin(parts):
    sums = {}
    for s in range(len(parts) - 2, -1, -2):
        got = swap(parts[s + 1], "feat", 1)
        sums[s] = (parts[s].astype(F32) + got.astype(F32)).astype(BF) if s else [parts[0], got]
    return sums


def scatter_end(sums, *tokens):
    sums = {s: part if s == 0 else [after(part, *tokens)] for s, part in sums.items()}
    for bit in bits_of(lax.axis_size("feat"))[1:]:
        for s in sorted(sums, reverse=True):
            if s & bit:
                pieces = sums.pop(s)
                value = pieces[0]
                if len(pieces) > 1:
                    value = functools.reduce(jnp.add, [p.astype(F32) for p in pieces]).astype(BF)
                sums[s ^ bit].append(swap(value, "feat", bit))
    return sums[0]


def sum_everywhere(value):
    for axis in ("feat", "rows"):
        for bit in bits_of(lax.axis_size(axis)):
            value = value + swap(value, axis, bit)
    return value


class RowSum:
    def __init__(self, value, order, *tokens):
        self.order, self.step = order, 0
        self.value = after(value, *tokens)
        self.launch()

    def launch(self):
        count = len(self.order)
        halving = self.step < count
        bit = self.order[self.step] if halving else self.order[2 * count - 1 - self.step]
        self.upper = (lax.axis_index("rows") & bit) != 0
        self.sent = self.kept = self.value
        if halving:
            half = self.value.shape[0] // 2
            low, high = self.value[:half], self.value[half:]
            self.sent = jnp.where(self.upper, low, high)
            self.kept = jnp.where(self.upper, high, low)
        self.got = swap(self.sent, "rows", bit)

    def next(self, *tokens):
        got = after(self.got, *tokens)
        if self.step < len(self.order):
            self.value = (self.kept.astype(F32) + got.astype(F32)).astype(BF)
        else:
            first = jnp.where(self.upper, got, self.kept)
            self.value = jnp.concatenate([first, jnp.where(self.upper, self.kept, got)], axis=0)
        self.step += 1
        if self.step < 2 * len(self.order):
            self.launch()
            return self.sent
        return self.value

    def finish(self, *tokens):
        while self.step < 2 * len(self.order):
            self.next(*tokens)
        return self.value


def shifted(pack, hop, groups, reverse):
    if reverse:
        pairs = [(i, i - hop) for i in range(hop, groups)]
    else:
        pairs = [(i, i + hop) for i in range(groups - hop)]
    return lax.ppermute(pack, "rows", pairs)


def reached(crops_at, here, groups, reach, reverse):
    mine = crops_at[here + 1] if reverse else crops_at[here]
    flags = []
    for hop in range(1, reach + 1):
        other = here + hop if reverse else here - hop
        inside = (other < groups) if reverse else (other >= 0)
        at = jnp.clip(other, 0, groups - 1)
        theirs = crops_at[at] if reverse else crops_at[at + 1]
        flags.append((inside & (theirs == mine)).astype(F32))
    return jnp.stack(flags)


def gather_carry(pack, flags, groups, reverse):
    total = jnp.zeros(pack.shape, F32)
    for i in range(flags.shape[0]):
        got = shifted(pack, i + 1, groups, reverse).astype(F32)
        total = total + jnp.where(flags[i] > 0, got, 0.0)
    return total


def on_device(
    pixels,
    qkv_weight,
    out_weight,
    up_weight,
    down_weight,
    norm1_gain,
    norm1_bias,
    norm2_gain,
    norm2_bias,
    crop_lengths,
    crop_offsets,
    pixel_mask,
    out_grad,
):
    local_rows = pixels.shape[0]
    group_rows = pixel_mask.shape[0]
    width = qkv_weight.shape[2]
    crop_count = crop_offsets.shape[0]
    groups = lax.axis_size("rows")
    members = lax.axis_size("feat")
    pairs = members // 2
    here = lax.axis_index("rows")
    member = lax.axis_index("feat")
    reach = min(groups - 1, -(-(CROP_MAX - 1) // group_rows))
    group_start = here * group_rows
    slot_ids = jnp.arange(members, dtype=jnp.int32) ^ member
    in_group = (slot_ids[:, None] * local_rows + jnp.arange(local_rows, dtype=jnp.int32)[None, :]).reshape(-1)
    places = group_start + in_group
    started = crop_offsets[None, :] <= places[:, None]
    crop_ends = crop_offsets + crop_lengths
    segment = jnp.sum(started.astype(jnp.int32), axis=1) - 1
    inside = jnp.sum((started & (places[:, None] < crop_ends[None, :])).astype(jnp.int32), axis=1)
    mask = jnp.concatenate(
        [
            lax.dynamic_slice_in_dim(pixel_mask, (member ^ s) * local_rows, local_rows)
            for s in range(members)
        ]
    )
    pixel_valid = (mask * inside).astype(F32)
    edges = jnp.arange(groups + 1, dtype=jnp.int32) * group_rows - 1
    crops_at = jnp.sum((crop_offsets[None, :] <= edges[:, None]).astype(jnp.int32), axis=1) - 1
    chunk_edges = group_start - 1 + jnp.arange(members + 1, dtype=jnp.int32) * local_rows
    last = jnp.sum((crop_offsets[None, :] <= chunk_edges[:, None]).astype(jnp.int32), axis=1) - 1
    tail = last[-1:]
    spot = slot_ids
    code = (segment * 2 + mask * inside).reshape(members, 1, local_rows)
    validc = pixel_valid[:, None]
    gain1, bias1, gain2, bias2 = (
        a[None, :] for a in (norm1_gain, norm1_bias, norm2_gain, norm2_bias)
    )
    no_pack = jnp.zeros((PACK, width), F32)
    before = reached(crops_at, here, groups, reach, False)
    behind = reached(crops_at, here, groups, reach, True)

    normed_slots = gather_begin(norm_one(pixels, gain1, bias1))
    grad_slots = gather_begin(after(out_grad, normed_slots[members // 2]))
    *made, pack = project_qkv(0, tail, normed_slots[0], normed_slots[1], qkv_weight, code, no_pack, (), [before, behind, spot])
    normed_slots = gather_end(normed_slots, pack)
    for p in range(1, pairs):
        *made, pack = project_qkv(
            p, tail, normed_slots[2 * p], normed_slots[2 * p + 1], qkv_weight, code, pack, made
        )
    q, k, v = made
    carry = gather_carry(pack.astype(BF), before, groups, False)
    num, den = attend(last, spot, q, k, v, code)
    grad_slots = gather_end(grad_slots, num)
    sent = {
        p: project(
            p, local_rows, last, num, den, q, carry, code, out_weight, [grad_slots[members // 2]]
        )
        for p in reversed(range(pairs))
    }
    parts = scatter_end(scatter_begin([sent[s // 2][2 + s % 2] for s in range(members)]))
    middle, normed_two, attended_square = norm_two(pixels, gain2, bias2, parts)
    two_slots = gather_begin(normed_two)
    hidden = [mlp(two_slots[0], two_slots[1], grad_slots[0], grad_slots[1], up_weight, down_weight)]
    two_slots = gather_end(two_slots, hidden[0][0])
    for p in range(1, pairs):
        hidden.append(mlp(*two_slots[2 * p : 2 * p + 2], *grad_slots[2 * p : 2 * p + 2], up_weight, down_weight))
    two_sums = scatter_begin([hidden[s // 2][2 + s % 2] for s in range(members)])
    two_parts = scatter_end(two_sums)
    branch_sums = scatter_begin([hidden[s // 2][4 + s % 2] for s in range(members)])
    acts, hids, twos = after(
        ([h[0] for h in hidden], [h[1] for h in hidden], two_slots), two_sums[members - 2]
    )
    hids = after(hids, two_sums[0][1], branch_sums[0][1], branch_sums[members - 2])
    down_grad = tn(jnp.concatenate(acts, axis=0), jnp.concatenate(grad_slots, axis=0)).astype(BF)
    up_grad = tn(jnp.concatenate(twos, axis=0), jnp.concatenate(hids, axis=0)).astype(BF)
    bits = bits_of(groups)
    turned = bits[1:] + bits[:1]
    both = jnp.concatenate([down_grad, up_grad.reshape(-1, D)], axis=0)
    both = lax.psum_scatter(after(both, two_parts[-1]), "rows", scatter_dimension=0, tiled=True)
    middle_low, gain2_grad, bias2_grad = norm_two_back(
        out_grad, middle, gain2, two_parts,
        [down_grad, up_grad, branch_sums[0][1], branch_sums[members - 2]],
    )
    middle_slots = gather_begin(middle_low)
    *made, grad_pack = heads_back(
        0, last, middle_slots[0], middle_slots[1], out_weight, sent[0][0], sent[0][1], q, code, no_pack, ()
    )
    branch_parts = scatter_end(branch_sums, middle_slots[members // 2], grad_pack)
    middle_slots = gather_end(middle_slots, grad_pack)
    for p in range(1, pairs):
        *made, grad_pack = heads_back(
            p, last, middle_slots[2 * p], middle_slots[2 * p + 1], out_weight,
            sent[p][0], sent[p][1], q, code, grad_pack, made
        )
    ng, dg = made
    grad_carry = gather_carry(grad_pack.astype(BF), behind, groups, True)
    heads_all = jnp.concatenate([sent[p][0] for p in range(pairs)], axis=0)
    out_weight_grad = tn(heads_all, jnp.concatenate(middle_slots, axis=0))
    out_sum = RowSum(out_weight_grad.astype(BF), turned)
    dq, dk, dv = attend_back(last, spot, q, k, v, ng, dg, code, carry, [out_sum.sent])
    out_sum.next(dq)
    mixed_grad, *mixed_parts = mix(local_rows, tail, dq, dk, dv, k, v, code, grad_carry, qkv_weight)
    normed_sums = scatter_begin(mixed_parts)
    normed_parts = scatter_end(normed_sums)
    qkv_grad = tn(mixed_grad, jnp.concatenate(normed_slots, axis=0)).astype(BF)
    both = lax.all_gather(after(both, dq), "rows", axis=0, tiled=True)
    down_grad = both[: down_grad.shape[0]].astype(F32)
    up_grad = both[down_grad.shape[0] :].reshape(up_grad.shape).astype(F32)
    out_sum.next(mixed_grad)
    cut = 3 * width // 2
    low_sum = RowSum(qkv_grad[:cut], bits)
    high_sum = RowSum(qkv_grad[cut:], turned)
    normed_sent = normed_sums[members - 2]
    tokens = [low_sum.next(normed_sent), high_sum.next(normed_sent)]
    output, result_square, branch_square = finish(middle, branch_parts, tokens)
    pixels_grad, gain1_grad, bias1_grad = norm_one_back(pixels, middle_low, gain1, normed_parts)
    tokens = [out_sum.next(*tokens)]
    tokens = [low_sum.next(*tokens, pixels_grad), high_sum.next(*tokens, pixels_grad)]
    out_weight_grad = out_sum.finish(*tokens).astype(F32)
    qkv_grad = jnp.concatenate([low_sum.finish(), high_sum.finish()], axis=0)
    qkv_grad = jnp.swapaxes(qkv_grad.reshape(3, width, D), 1, 2).astype(F32)

    crop_onehot = (
        segment[:local_rows, None] == jnp.arange(crop_count, dtype=jnp.int32)[None, :]
    ).astype(F32)
    squares = (
        jnp.concatenate(
            [result_square, attended_square, branch_square, jnp.ones((local_rows, 1), F32)], axis=1
        )
        * validc[:local_rows]
    )
    crop_sums = lax.dot_general(
        squares, crop_onehot, (((0,), (0,)), ((), ())), precision=precise, preferred_element_type=F32
    )
    sums = jnp.concatenate(
        [gain1_grad[0], bias1_grad[0], gain2_grad[0], bias2_grad[0], crop_sums.reshape(-1)]
    )
    sums = sum_everywhere(sums)
    gain1_grad, bias1_grad, gain2_grad, bias2_grad = sums[: 4 * D].reshape(4, D)
    crop_sums = sums[4 * D :].reshape(4, crop_count)
    crop_rms = jnp.sqrt(crop_sums[:3] / (D * jnp.maximum(crop_sums[3], 1.0))[None, :])
    return (
        output,
        pixels_grad,
        qkv_grad,
        out_weight_grad,
        up_grad,
        down_grad,
        gain1_grad,
        bias1_grad,
        gain2_grad,
        bias2_grad,
        crop_rms,
    )


def solution(mesh):
    split = P(("rows", "feat"), None)
    qkv, rows_feat, cols_feat = P(None, None, "feat"), P("feat", None), P(None, "feat")
    in_specs = (
        (split, qkv, rows_feat, cols_feat, rows_feat) + (P(),) * 6 + (P("rows"), split)
    )
    out_specs = (split, split, qkv, rows_feat, cols_feat, rows_feat) + (P(),) * 5
    return jax.shard_map(
        on_device, mesh=mesh, in_specs=in_specs, out_specs=out_specs, check_vma=False
    )
```
